128 devices in a mesh: space: 16 (over z, y_hi, core), tm: 8 (over y_lo, x).
Axes of the slice: x: 4, y: 4 (y_hi: 2, y_lo: 2; y = y_hi * 2 + y_lo), z: 4, core: 2. Of those that a mesh axis runs over, the one named last changes fastest.
Arguments:
- gauge_links: float32 [4, 2, 3, 3, 32, 64, 256], P(None, None, None, None, 'tm', 'space'), may hold values from -1 to 1, as said below
Outputs:
- flowed_links: float32 [4, 2, 3, 3, 32, 64, 256], P(None, None, None, None, 'tm', 'space')
- flow_force: float32 [4, 2, 3, 3, 32, 64, 256], P(None, None, None, None, 'tm', 'space')
- holonomy: float32 [2, 3, 3, 8, 64, 256], P(None, None, None, 'tm', 'space')
The draws below stay inside these ranges and needn't reach their ends.
Inputs may be any that keep to these rules, and one draw needn't show every extreme that they name: `gauge_links`: every link is a special unitary 3 x 3 matrix.
All inputs are finite; a program needn't handle non-finite values.
Results may differ from the reference program's by a relative error of at most 0.00002.
Values sent between devices are 32-bit elements; how exact they have to be, the bound alone decides.
No kernel may reach another device: no remote copies, remote signals or barrier semaphores. Data moves between devices by JAX's collectives and lax.ppermute only.
A program may use at most 64 MiB of HBM per device.

```python
import jax
import jax.numpy as jnp

NX = 16
NY = 16
CT = 4
NZ = 64
NT = 32
N_TM = 8


def complex_mul(left_re, left_im, right_re, right_im):
    return (left_re * right_re - left_im * right_im, left_re * right_im + left_im * right_re)


def normalize_row(row_vec):
    row_norm = jnp.sqrt(jnp.sum(row_vec * row_vec, axis=(0, 1)))
    return row_vec / row_norm[None, None]


def draw_gauge_links(key, part):
    raw_rows = jax.random.normal(key, (2, 3, 3, 4, NT, NZ, NY * NX), jnp.float32)
    diag_boost = 0.8
    unit_matrix = jnp.eye(3, dtype=jnp.float32).reshape(1, 3, 3, 1, 1, 1, 1)
    part_mask = jnp.array([1.0, 0.0], jnp.float32).reshape(2, 1, 1, 1, 1, 1, 1)
    raw_rows = raw_rows + diag_boost * unit_matrix * part_mask
    first_row = normalize_row(raw_rows[:, 0])
    second_row = raw_rows[:, 1]
    inner_re = jnp.sum(first_row[0] * second_row[0] + first_row[1] * second_row[1], axis=0)
    inner_im = jnp.sum(first_row[0] * second_row[1] - first_row[1] * second_row[0], axis=0)
    proj_re, proj_im = complex_mul(inner_re[None], inner_im[None], first_row[0], first_row[1])
    second_row = normalize_row(jnp.stack([second_row[0] - proj_re, second_row[1] - proj_im]))
    third_re = []
    third_im = []
    for column_id in range(3):
        next_id = (column_id + 1) % 3
        after_id = (column_id + 2) % 3
        one_re, one_im = complex_mul(first_row[0][next_id], first_row[1][next_id], second_row[0][after_id], second_row[1][after_id])
        two_re, two_im = complex_mul(first_row[0][after_id], first_row[1][after_id], second_row[0][next_id], second_row[1][next_id])
        third_re.append(one_re - two_re)
        third_im.append(-(one_im - two_im))
    third_row = jnp.stack([jnp.stack(third_re), jnp.stack(third_im)])
    matrix = jnp.stack([first_row, second_row, third_row], axis=1)
    return jnp.moveaxis(matrix, 3, 0).astype(jnp.float32)


def setup_inputs(seed: int = 0) -> dict:
    key_of = jax.random.split(jax.random.key(seed), 2)
    return {
        "gauge_links": draw_gauge_links(jax.random.fold_in(key_of[1], 71), 0),
    }


flow_step = 0.5


def matmul_su(former, latter):
    real_part = 0.0
    imag_part = 0.0
    for inner_index in range(3):
        left_re = former[0][:, inner_index][:, None]
        left_im = former[1][:, inner_index][:, None]
        right_re = latter[0][inner_index][None]
        right_im = latter[1][inner_index][None]
        real_part = real_part + left_re * right_re - left_im * right_im
        imag_part = imag_part + left_re * right_im + left_im * right_re
    return jnp.stack([real_part, imag_part])


def dagger(matrix):
    return jnp.stack([jnp.swapaxes(matrix[0], 0, 1), -jnp.swapaxes(matrix[1], 0, 1)])


def identity_as(matrix):
    shape = matrix.shape[1:]
    unit_matrix = jnp.eye(3, dtype=matrix.dtype).reshape((3, 3) + (1,) * (len(shape) - 2))
    return jnp.stack([jnp.broadcast_to(unit_matrix, shape), jnp.zeros(shape, matrix.dtype)])


def project(matrix):
    anti_part = 0.5 * (matrix - dagger(matrix))
    trace_part = (anti_part[:, 0, 0] + anti_part[:, 1, 1] + anti_part[:, 2, 2]) / 3.0
    unit_matrix = identity_as(matrix)[0]
    return anti_part - unit_matrix[None] * trace_part[:, None, None]


def flow_update(omega_field, link_field):
    force_field = -project(omega_field)
    exponent = (0.25 * flow_step) * force_field
    unit_matrix = identity_as(link_field)
    power_sum = unit_matrix
    for term_order in range(6, 0, -1):
        power_sum = unit_matrix + matmul_su(exponent, power_sum) / term_order
    return force_field, matmul_su(power_sum, link_field)


def unit_step(direct):
    return tuple(1 if axis_id == direct else 0 for axis_id in range(4))


def offset_sum(first_offset, second_offset, sign_factor):
    return tuple(first_offset[slot_index] + sign_factor * second_offset[slot_index] for slot_index in range(4))


def reference(gauge_links):
    lattice = gauge_links.reshape(4, 2, 3, 3, NT, NZ, NY, NX)
    anchor = (0, 0, 0, 0)

    def fetch_link(direct, offset):
        link_field = lattice[direct]
        for shift_by, axis_id in zip(offset, (6, 5, 4, 3)):
            if shift_by != 0:
                link_field = jnp.roll(link_field, -shift_by, axis_id)
        return link_field

    forces = []
    flowed = []
    for direct in range(4):
        staple_sum = None
        for across in range(4):
            if across == direct:
                continue
            step_across = unit_step(across)
            step_direct = unit_step(direct)
            back_step = offset_sum(anchor, step_across, -1)
            upper_part = matmul_su(matmul_su(fetch_link(across, anchor), fetch_link(direct, step_across)), dagger(fetch_link(across, step_direct)))
            lower_part = matmul_su(matmul_su(dagger(fetch_link(across, back_step)), fetch_link(direct, back_step)), fetch_link(across, offset_sum(step_direct, step_across, -1)))
            staple_piece = upper_part + lower_part
            staple_sum = staple_piece if staple_sum is None else staple_sum + staple_piece
        omega_field = matmul_su(lattice[direct], dagger(staple_sum))
        force_field, renewed = flow_update(omega_field, lattice[direct])
        forces.append(force_field)
        flowed.append(renewed)
    force_all = jnp.stack(forces).reshape(4, 2, 3, 3, NT, NZ, NY * NX)
    flowed_all = jnp.stack(flowed).reshape(4, 2, 3, 3, NT, NZ, NY * NX)
    time_links = flowed[3]
    slabs = []
    for slab_id in range(N_TM):
        product = time_links[:, :, :, slab_id * CT]
        for inner_index in range(1, CT):
            product = matmul_su(product, time_links[:, :, :, slab_id * CT + inner_index])
        slabs.append(product)
    loops = []
    for slab_id in range(N_TM):
        product = slabs[slab_id]
        for term_order in range(1, N_TM):
            product = matmul_su(product, slabs[(slab_id + term_order) % N_TM])
        loops.append(product)
    holonomy = jnp.stack(loops, axis=3).reshape(2, 3, 3, N_TM, NZ, NY * NX)
    return flowed_all, force_all, holonomy
```

```python
import jax
import jax.numpy as jnp
from jax import lax
from jax.experimental import pallas as pl
from jax.experimental.pallas import tpu as pltpu
from jax.sharding import PartitionSpec as P

F32 = jnp.float32
VMEM = pltpu.VMEM
PAIRS = ((0, 1), (0, 2), (1, 2))


def entry(terms):
    re = im = None
    for (ar, ai), ca, (br, bi), cb in terms:
        p = ar * br
        q = ai * bi
        re = p if re is None else re + p
        re = re + q if ca != cb else re - q
        u = ar * bi
        v = ai * br
        if im is None:
            im = (v - u) if cb and not ca else (u - v) if ca and not cb else (u + v)
        else:
            im = im - u if cb else im + u
            im = im - v if ca else im + v
    return re, im


def entry_im(terms):
    im = None
    for (ar, ai), ca, (br, bi), cb in terms:
        u = ar * bi
        v = ai * br
        if im is None:
            im = (v - u) if cb and not ca else (u - v) if ca and not cb else (u + v)
        else:
            im = im - u if cb else im + u
            im = im - v if ca else im + v
    return im


def terms(a, ha, b, hb, i, j):
    out = []
    for k in range(3):
        x = a[k][i] if ha else a[i][k]
        y = b[j][k] if hb else b[k][j]
        out.append((x, ha, y, hb))
    return out


def product(a, b, ha=False, hb=False):
    return [[entry(terms(a, ha, b, hb, i, j)) for j in range(3)] for i in range(3)]


def twice_ta(a, b):
    out = []
    for i, j in PAIRS:
        r1, i1 = entry(terms(a, False, b, False, i, j))
        r2, i2 = entry(terms(a, False, b, False, j, i))
        out += [r1 - r2, i1 + i2]
    d = [entry_im(terms(a, False, b, False, k, k)) for k in range(3)]
    tr = (d[0] + d[1] + d[2]) * (2.0 / 3.0)
    return out + [d[0] + d[0] - tr, d[1] + d[1] - tr]


def transport(u, c):
    r01, i01, r02, i02, r12, i12, d0, d1 = c
    d2 = -(d0 + d1)
    off = {(0, 1): (r01, i01), (0, 2): (r02, i02), (1, 2): (r12, i12)}
    diag = (d0, d1, d2)
    t = []
    for i in range(3):
        row = []
        for j in range(3):
            ur, ui = u[i][j]
            re = -(ui * diag[j])
            im = ur * diag[j]
            for k in range(3):
                if k == j:
                    continue
                ar, ai = u[i][k]
                if k < j:
                    cr, ci = off[k, j]
                    re = re + ar * cr - ai * ci
                    im = im + ar * ci + ai * cr
                else:
                    cr, ci = off[j, k]
                    re = re - ar * cr - ai * ci
                    im = im + ar * ci - ai * cr
            row.append((re, im))
        t.append(row)
    out = []
    for i, j in PAIRS:
        out += list(entry(terms(t, False, u, True, i, j)))
    for k in range(2):
        out.append(entry_im(terms(t, False, u, True, k, k)))
    return out


def taylor(f):
    r01, i01, r02, i02, r12, i12, h0, h1 = f
    h2 = -(h0 + h1)
    n01 = r01 * r01 + i01 * i01
    n02 = r02 * r02 + i02 * i02
    n12 = r12 * r12 + i12 * i12
    y0 = -(h0 * h0 + n01 + n02)
    y1 = -(h1 * h1 + n01 + n12)
    y2 = -(h2 * h2 + n02 + n12)
    s = 0.5 * (y0 + y1 + y2)
    y01 = (h2 * i01 - (r02 * r12 + i02 * i12), -(h2 * r01) - (i02 * r12 - r02 * i12))
    y02 = (h1 * i02 + (r01 * r12 - i01 * i12), -(h1 * r02) + (r01 * i12 + i01 * r12))
    y12 = (h0 * i12 - (r01 * r02 + i01 * i02), -(h0 * r12) - (r01 * i02 - i01 * r02))
    zr = r01 * r12 - i01 * i12
    zi = r01 * i12 + i01 * r12
    trip = zi * r02 - zr * i02
    e = -(h0 * h1 * h2 + (trip + trip) - h0 * n12 - h1 * n02 - h2 * n01)
    q0r = 1.0 - e * e * (1.0 / 720.0)
    q0i = e * (1.0 / 6.0 + s * (1.0 / 120.0))
    q1r = 1.0 + s * (1.0 / 6.0 + s * (1.0 / 120.0))
    q1i = e * (1.0 / 24.0 + s * (1.0 / 360.0))
    q2r = 0.5 + s * (1.0 / 24.0 + s * (1.0 / 720.0))
    q2i = e * (1.0 / 120.0)
    out = [[None] * 3 for _ in range(3)]
    offs = (((r01, i01), y01), ((r02, i02), y02), ((r12, i12), y12))
    for (i, j), ((xr, xi), (yr, yi)) in zip(PAIRS, offs):
        p1, p2, p3, p4 = q1r * xr, q1i * xi, q1r * xi, q1i * xr
        s1, s2, s3, s4 = q2r * yr, q2i * yi, q2r * yi, q2i * yr
        out[i][j] = ((p1 - p2) + (s1 - s2), (p3 + p4) + (s3 + s4))
        out[j][i] = ((s1 + s2) - (p1 + p2), (p3 - p4) + (s4 - s3))
    for k, (h, y) in enumerate(((h0, y0), (h1, y1), (h2, y2))):
        out[k][k] = (q0r - q1i * h + q2r * y, q0i + q1r * h + q2i * y)
    return out


def masks():
    lane = lax.broadcasted_iota(jnp.int32, (8, 128), 1)
    z = lax.broadcasted_iota(jnp.int32, (8, 128), 0) & 3
    return {"x": lane & 15, "y": lane >> 4, "z": z}


def shift_x(v, m, up):
    if up:
        return jnp.where(m["x"] == 15, pltpu.roll(v, 15, 1), pltpu.roll(v, 127, 1))
    return jnp.where(m["x"] == 0, pltpu.roll(v, 113, 1), pltpu.roll(v, 1, 1))


def shift_y(v, m, up):
    r = pltpu.roll(v, 112 if up else 16, 1)
    return jnp.where(m["y"] == (7 if up else 0), pltpu.roll(r, 4, 0), r)


def mat(fetch):
    return [[(fetch(0, i, j), fetch(1, i, j)) for j in range(3)] for i in range(3)]


def on_mat(m, f):
    return [[(f(a), f(b)) for a, b in row] for row in m]


def plane(u_mu, u_nu, mu_up, nu_up):
    d = product(u_mu, u_nu, ha=True)
    g = product(mu_up, nu_up, hb=True)
    return twice_ta(g, d), twice_ta(d, g)


def unpack_rows(ref, base, row):
    m = [[(ref[base * 12 + i * 3 + j], ref[base * 12 + 6 + i * 3 + j]) for j in range(3)] for i in range(2)]
    third = []
    for k in range(3):
        a, b = (k + 1) % 3, (k + 2) % 3
        r1, i1 = entry([(m[0][a], False, m[1][b], False)])
        r2, i2 = entry([(m[0][b], False, m[1][a], False)])
        third.append((r1 - r2, i2 - i1))
    return m + [third]


def tiles(ref, shape):
    return ref.reshape(*shape, 8, 128)


def load_kernel(u_hbm, u_ref, st_ref, sz_ref, sem):
    copies = []
    for h in range(2):
        c = pltpu.make_async_copy(u_hbm.at[:, :, :, :, :, :, pl.ds(128 * h, 128)], u_ref.at[:, :, :, :, :, h], sem.at[h])
        c.start()
        copies.append(c)
    for c in copies:
        c.wait()
    u = tiles(u_ref, (4, 2, 3, 3, 4))
    rows = u_ref.reshape(4, 2, 3, 3, 32, 128)
    for n, (dt, dz) in enumerate(((0, 0), (1, 1), (2, 3))):
        for p in range(2):
            for i in range(2):
                for j in range(3):
                    k = n * 12 + p * 6 + i * 3 + j
                    st_ref[k] = u[dt, p, i, j, 0]
                    sz_ref[k] = rows[dz, p, i, j, pl.ds(0, 8, stride=4), :]


def accumulate(ref, mu, t, vals, sign=1):
    for k in range(8):
        if sign > 0:
            ref[mu, k, t] += vals[k]
        else:
            ref[mu, k, t] -= vals[k]


def inner_kernel(u_ref, c_ref, r_ref):
    u = tiles(u_ref, (4, 2, 3, 3, 4))
    m = masks()
    c_ref[...] = jnp.zeros_like(c_ref)
    r_ref[...] = jnp.zeros_like(r_ref)

    def link(d, t):
        return mat(lambda p, i, j: u[d, p, i, j, t])

    def xy(t, carry):
        ux, uy = link(0, t), link(1, t)
        a, b = plane(ux, uy, on_mat(ux, lambda v: shift_y(v, m, True)), on_mat(uy, lambda v: shift_x(v, m, True)))
        accumulate(c_ref, 1, t, a)
        accumulate(c_ref, 0, t, b, -1)
        accumulate(r_ref, 0, t, [shift_y(v, m, False) for v in a])
        accumulate(r_ref, 1, t, [shift_x(v, m, False) for v in b], -1)
        return carry

    lax.fori_loop(0, 4, xy, 0)

    def timelike(t, carry):
        for mu, shift in ((0, shift_x), (1, shift_y)):
            side_time(c_ref, r_ref, mu, shift, m, t, link(mu, t), link(3, t), link(mu, t + 1))
        return carry

    lax.fori_loop(0, 3, timelike, 0)


def side_time(c_ref, r_ref, mu, shift, m, t, u_mu, u_t, mu_up):
    a, b = plane(u_mu, u_t, mu_up, on_mat(u_t, lambda v: shift(v, m, True)))
    accumulate(c_ref, 3, t, a)
    accumulate(c_ref, mu, t, b, -1)
    accumulate(r_ref, mu, t + 1, a)
    accumulate(r_ref, 3, t, [shift(v, m, False) for v in b], -1)


def outer_kernel(u_ref, ht_ref, hz_ref, c_in, r_in, c_ref, r_ref, fz_ref, ft_ref, up_ref, hx_ref, fx_ref):
    u = tiles(u_ref, (4, 2, 3, 3, 4))
    m = masks()
    above = [unpack_rows(ht_ref, n, None) for n in range(3)]
    for p in range(2):
        for i in range(3):
            for j in range(3):
                for t in range(4):
                    up_ref[2, p, i, j, t] = u[2, p, i, j, t]
                for d in range(3):
                    up_ref[d, p, i, j, 4] = above[d][i][j][p]
    for n in range(3):
        g = unpack_rows(hz_ref, n, None)
        for p in range(2):
            for i in range(3):
                for j in range(3):
                    hx_ref[n, p, i, j, pl.ds(3, 8, stride=4), :] = g[i][j][p]

    def link(d, t):
        return mat(lambda p, i, j: u[d, p, i, j, t])

    def rows(t):
        return pl.ds(pl.multiple_of(t * 8, 8), 8)

    def up_z(mtx, n, t):
        def one(p, i, j):
            return jnp.where(m["z"] == 3, hx_ref[n, p, i, j, rows(t), :], pltpu.roll(mtx[i][j][p], 7, 0))

        return mat(one)

    def down_z(v):
        return jnp.where(m["z"] == 0, 0.0, pltpu.roll(v, 1, 0))

    def body(t, carry):
        uz = link(2, t)
        ut = link(3, t)
        a, b = plane(uz, ut, mat(lambda p, i, j: up_ref[2, p, i, j, t + 1]), up_z(ut, 2, t))
        accumulate(c_ref, 3, t, a)
        accumulate(c_ref, 2, t, b, -1)
        accumulate(r_ref, 2, t + 1, a)
        for k in range(8):
            fx_ref[2, k, rows(t), :] = -b[k]
        accumulate(r_ref, 3, t, [down_z(v) for v in b], -1)
        for mu, shift in ((0, shift_x), (1, shift_y)):
            um = link(mu, t)
            a, b = plane(um, uz, up_z(um, mu, t), on_mat(uz, lambda v: shift(v, m, True)))
            accumulate(c_ref, 2, t, a)
            accumulate(c_ref, mu, t, b, -1)
            for k in range(8):
                fx_ref[mu, k, rows(t), :] = a[k]
            accumulate(r_ref, mu, t, [down_z(v) for v in a])
            accumulate(r_ref, 2, t, [shift(v, m, False) for v in b], -1)
        return carry

    lax.fori_loop(0, 4, body, 0)
    for mu, shift in ((0, shift_x), (1, shift_y)):
        side_time(c_ref, r_ref, mu, shift, m, 3, link(mu, 3), link(3, 3), mat(lambda p, i, j: up_ref[mu, p, i, j, 4]))
    for mu in range(3):
        for k in range(8):
            fz_ref[mu * 8 + k] = fx_ref[mu, k, pl.ds(3, 8, stride=4), :]
            ft_ref[mu * 8 + k] = r_ref[mu, k, 4]


def transport_kernel(u_ref, c_ref, r_ref, f_ref):
    u = tiles(u_ref, (4, 2, 3, 3, 4))

    def body(n, carry):
        mu, t = n // 4, n % 4
        w = transport(mat(lambda p, i, j: u[mu, p, i, j, t]), [c_ref[mu, k, t] for k in range(8)])
        for k in range(8):
            f_ref[mu, k, t] = w[k] + r_ref[mu, k, t]
        return carry

    lax.fori_loop(0, 16, body, 0)


def finish(f, u, z_out, new_out):
    z = [-0.5 * v for v in f]
    zero = jnp.zeros_like(z[0])
    for n, (i, j) in enumerate(PAIRS):
        z_out(0, i, j, z[2 * n])
        z_out(1, i, j, z[2 * n + 1])
        z_out(0, j, i, -z[2 * n])
        z_out(1, j, i, z[2 * n + 1])
    for k, d in enumerate((z[6], z[7], -(z[6] + z[7]))):
        z_out(0, k, k, zero)
        z_out(1, k, k, d)
    new = product(taylor([0.125 * v for v in z]), u)
    for i in range(3):
        for j in range(3):
            for p in range(2):
                new_out(p, i, j, new[i][j][p])
    return new


def writer(ref, *head, t):
    def put(p, i, j, v):
        ref[(*head, p, i, j, t)] = v

    return put


def spread(fz_ref, ez_ref, which):
    for n in which:
        for k in range(8):
            ez_ref[n, k] = jnp.zeros((32, 128), F32)
            ez_ref[n, k, pl.ds(0, 8, stride=4), :] = fz_ref[n * 8 + k]


def time_kernel(u_ref, f_ref, fz_ref, ft_ref, zt_ref, nt_ref, s_ref, b_ref, ez_ref):
    u = tiles(u_ref, (4, 2, 3, 3, 4))
    zt, nt = tiles(zt_ref, (2, 3, 3, 4)), tiles(nt_ref, (2, 3, 3, 4))
    spread(fz_ref, ez_ref, (2,))

    def body(t, carry):
        f = [f_ref[3, k, t] + ez_ref[2, k, pl.ds(pl.multiple_of(t * 8, 8), 8), :] for k in range(8)]
        finish(f, mat(lambda p, i, j: u[3, p, i, j, t]), writer(zt, t=t), writer(nt, t=t))
        return carry

    lax.fori_loop(0, 4, body, 0)
    slab = mat(lambda p, i, j: nt[p, i, j, 0])
    for t in range(1, 4):
        slab = product(slab, mat(lambda p, i, j: nt[p, i, j, t]))
    for i in range(3):
        for j in range(3):
            for p in range(2):
                s_ref[p, i, j] = slab[i][j][p]
                b_ref[p * 9 + i * 3 + j] = slab[i][j][p]
    for k in range(24):
        b_ref[18 + k] = ft_ref[k]


def out_copies(src, dst, sem, d, first, count):
    copies = []
    for h in range(2):
        t = pl.ds(first, count)
        copies.append(pltpu.make_async_copy(src.at[:, :, :, :, h], dst.at[d, :, :, :, t, :, pl.ds(128 * h, 128)], sem.at[h]))
    return copies


def space_kernel(u_ref, f_ref, fz_ref, zt_ref, nt_ref, new_hbm, z_hbm, zs_ref, ns_ref, ez_ref, sem):
    u = tiles(u_ref, (4, 2, 3, 3, 4))
    copies = out_copies(zt_ref, z_hbm, sem.at[6], 3, 0, 4) + out_copies(nt_ref, new_hbm, sem.at[7], 3, 0, 4)
    for c in copies:
        c.start()
    spread(fz_ref, ez_ref, (0, 1))
    for mu in range(3):
        zs, ns = tiles(zs_ref.at[mu], (2, 3, 3, 3)), tiles(ns_ref.at[mu], (2, 3, 3, 3))

        def body(n, carry):
            t = n + 1
            f = [f_ref[mu, k, t] for k in range(8)]
            if mu < 2:
                rows = pl.ds(pl.multiple_of(t * 8, 8), 8)
                f = [v + ez_ref[mu, k, rows, :] for k, v in enumerate(f)]
            finish(f, mat(lambda p, i, j: u[mu, p, i, j, t]), writer(zs, t=n), writer(ns, t=n))
            return carry

        lax.fori_loop(0, 3, body, 0)
        more = out_copies(zs_ref.at[mu], z_hbm, sem.at[2 * mu], mu, 1, 3)
        more += out_copies(ns_ref.at[mu], new_hbm, sem.at[2 * mu + 1], mu, 1, 3)
        for c in more:
            c.start()
        copies += more
    for c in copies:
        c.wait()


def first_kernel(u_ref, f_ref, fz_ref, b_ref, new_in, z_in, new_hbm, z_hbm, zs_ref, ns_ref, ez_ref, sem):
    u = tiles(u_ref, (4, 2, 3, 3, 4))
    spread(fz_ref, ez_ref, (0, 1))
    copies = []
    for mu in range(3):
        zs, ns = tiles(zs_ref.at[mu], (2, 3, 3, 1)), tiles(ns_ref.at[mu], (2, 3, 3, 1))
        f = [f_ref[mu, k, 0] + b_ref[18 + mu * 8 + k] for k in range(8)]
        if mu < 2:
            f = [v + ez_ref[mu, k, pl.ds(0, 8), :] for k, v in enumerate(f)]
        finish(f, mat(lambda p, i, j: u[mu, p, i, j, 0]), writer(zs, t=0), writer(ns, t=0))
        more = out_copies(zs_ref.at[mu], z_hbm, sem.at[2 * mu], mu, 0, 1)
        more += out_copies(ns_ref.at[mu], new_hbm, sem.at[2 * mu + 1], mu, 0, 1)
        for c in more:
            c.start()
        copies += more
    for c in copies:
        c.wait()


def get18(ref):
    return mat(lambda p, i, j: ref[p, i, j])


def put18(ref, m):
    for i in range(3):
        for j in range(3):
            for p in range(2):
                ref[p, i, j] = m[i][j][p]


def join_kernel(s_ref, s1_ref, s2_ref, b_ref, a_ref, l_ref):
    before = mat(lambda p, i, j: b_ref[p * 9 + i * 3 + j])
    a = product(product(get18(s_ref), get18(s1_ref)), get18(s2_ref))
    put18(a_ref, a)
    put18(l_ref, product(before, a))


def holonomy_kernel(a_ref, l_ref, b_ref, out_hbm, o_ref, sem):
    before = mat(lambda p, i, j: b_ref[p * 9 + i * 3 + j])
    loop = product(product(get18(a_ref), get18(l_ref)), before)
    put18(tiles(o_ref, (2, 3, 3)), loop)
    copies = []
    for h in range(2):
        copies.append(pltpu.make_async_copy(o_ref.at[:, :, :, h], out_hbm.at[:, :, :, 0, :, pl.ds(128 * h, 128)], sem.at[h]))
    for c in copies:
        c.start()
    for c in copies:
        c.wait()


def call(kernel, name, outs, args, scratch=(), aliases=None, us=1.0):
    def spec(kind):
        return pl.BlockSpec(memory_space=VMEM if kind == "v" else pl.ANY)

    shapes = [VMEM(s, F32) if kind == "v" else jax.ShapeDtypeStruct(s, F32) for kind, s in outs]
    values = [pltpu.with_memory_space_constraint(x, VMEM) if kind == "v" else x for kind, x in args]
    return pl.pallas_call(
        kernel,
        out_shape=shapes,
        in_specs=[spec(k) for k, _ in args],
        out_specs=[spec(k) for k, _ in outs],
        scratch_shapes=list(scratch),
        input_output_aliases=aliases or {},
        compiler_params=pltpu.CompilerParams(vmem_limit_bytes=24 << 20),
        cost_estimate=pl.CostEstimate(flops=int(us * 1e6), bytes_accessed=int(us * 3e6), transcendentals=0),
        name=name,
    )(*values)


def from_ahead(x, axis, k):
    n = lax.axis_size(axis)
    return lax.ppermute(x, axis, [(i, (i - k) % n) for i in range(n)])


def shards(gauge_links):
    dma = pltpu.SemaphoreType.DMA
    whole = (4, 2, 3, 3, 4, 2, 4, 128)
    full = gauge_links.shape
    u, st, sz = call(load_kernel, "load", [("v", whole), ("v", (36, 8, 128)), ("v", (36, 8, 128))], [("h", gauge_links)], [dma((2,))])
    ht = from_ahead(st, "tm", 1)
    hz = from_ahead(sz, "space", 1)
    u = ("v", u)
    c, r = call(inner_kernel, "inner", [("v", (4, 8, 4, 8, 128)), ("v", (4, 8, 5, 8, 128))], [u], us=2.0)
    c, r, fz, ft = call(
        outer_kernel,
        "outer",
        [("v", (4, 8, 4, 8, 128)), ("v", (4, 8, 5, 8, 128)), ("v", (24, 8, 128)), ("v", (24, 8, 128))],
        [u, ("v", ht), ("v", hz), ("v", c), ("v", r)],
        [VMEM((3, 2, 3, 3, 5, 8, 128), F32), VMEM((3, 2, 3, 3, 32, 128), F32), VMEM((3, 8, 32, 128), F32)],
        {3: 0, 4: 1},
    )
    fz = from_ahead(fz, "space", -1)
    (f,) = call(transport_kernel, "transport", [("v", (4, 8, 4, 8, 128))], [u, ("v", c), ("v", r)], us=2.0)
    f, fz = ("v", f), ("v", fz)
    ez = VMEM((3, 8, 32, 128), F32)
    zt, nt, s, b = call(
        time_kernel,
        "time",
        [("v", (2, 3, 3, 4, 2, 4, 128))] * 2 + [("v", (2, 3, 3, 8, 128)), ("v", (42, 8, 128))],
        [u, f, fz, ("v", ft)],
        [ez],
    )
    s1 = from_ahead(s, "tm", 1)
    b = from_ahead(b, "tm", -1)
    s2 = from_ahead(s, "tm", 2)
    new, force = call(
        space_kernel,
        "space",
        [("h", full), ("h", full)],
        [u, f, fz, ("v", zt), ("v", nt)],
        [VMEM((3, 2, 3, 3, 3, 2, 4, 128), F32)] * 2 + [ez, dma((8, 2))],
        us=3.0,
    )
    a, l = call(join_kernel, "join", [("v", (2, 3, 3, 8, 128))] * 2, [("v", s), ("v", s1), ("v", s2), ("v", b)])
    l = from_ahead(l, "tm", 4)
    new, force = call(
        first_kernel,
        "first",
        [("h", full), ("h", full)],
        [u, f, fz, ("v", b), ("h", new), ("h", force)],
        [VMEM((3, 2, 3, 3, 1, 2, 4, 128), F32)] * 2 + [ez, dma((6, 2))],
        {4: 0, 5: 1},
        us=3.0,
    )
    (hol,) = call(
        holonomy_kernel,
        "holonomy",
        [("h", (2, 3, 3, 1, 4, 256))],
        [("v", a), ("v", l), ("v", b)],
        [VMEM((2, 3, 3, 2, 4, 128), F32), dma((2,))],
    )
    return new, force, hol


def solution(mesh):
    in_specs = (P(None, None, None, None, "tm", "space", None),)
    out_specs = (
        P(None, None, None, None, "tm", "space", None),
        P(None, None, None, None, "tm", "space", None),
        P(None, None, None, "tm", "space", None),
    )
    return jax.shard_map(shards, mesh=mesh, in_specs=in_specs, out_specs=out_specs, check_vma=False)
```

```python
import jax
import jax.numpy as jnp
from jax import lax
from jax.experimental import pallas as pl
from jax.experimental.pallas import tpu as pltpu
from jax.sharding import PartitionSpec as P


F32 = jnp.float32
VMEM = pltpu.VMEM
PAIRS = ((0, 1), (0, 2), (1, 2))
ROW = 4


def entry(terms):
    re = im = None
    for (ar, ai), ca, (br, bi), cb in terms:
        p = ar * br
        q = ai * bi
        re = p if re is None else re + p
        re = re + q if ca != cb else re - q
        u = ar * bi
        v = ai * br
        if im is None:
            im = (v - u) if cb and not ca else (u - v) if ca and not cb else (u + v)
        else:
            im = im - u if cb else im + u
            im = im - v if ca else im + v
    return re, im


def entry_im(terms):
    im = None
    for (ar, ai), ca, (br, bi), cb in terms:
        u = ar * bi
        v = ai * br
        if im is None:
            im = (v - u) if cb and not ca else (u - v) if ca and not cb else (u + v)
        else:
            im = im - u if cb else im + u
            im = im - v if ca else im + v
    return im


def terms(a, ha, b, hb, i, j):
    out = []
    for k in range(3):
        x = a[k][i] if ha else a[i][k]
        y = b[j][k] if hb else b[k][j]
        out.append((x, ha, y, hb))
    return out


def product(a, b, ha=False, hb=False):
    return [[entry(terms(a, ha, b, hb, i, j)) for j in range(3)] for i in range(3)]


def twice_ta(a, b):
    out = []
    for i, j in PAIRS:
        r1, i1 = entry(terms(a, False, b, False, i, j))
        r2, i2 = entry(terms(a, False, b, False, j, i))
        out += [r1 - r2, i1 + i2]
    d = [entry_im(terms(a, False, b, False, k, k)) for k in range(3)]
    tr = (d[0] + d[1] + d[2]) * (2.0 / 3.0)
    return out + [d[0] + d[0] - tr, d[1] + d[1] - tr]


def transport(u, c):
    r01, i01, r02, i02, r12, i12, d0, d1 = c
    d2 = -(d0 + d1)
    off = {(0, 1): (r01, i01), (0, 2): (r02, i02), (1, 2): (r12, i12)}
    diag = (d0, d1, d2)
    t = []
    for i in range(3):
        row = []
        for j in range(3):
            ur, ui = u[i][j]
            re = -(ui * diag[j])
            im = ur * diag[j]
            for k in range(3):
                if k == j:
                    continue
                ar, ai = u[i][k]
                if k < j:
                    cr, ci = off[k, j]
                    re = re + ar * cr - ai * ci
                    im = im + ar * ci + ai * cr
                else:
                    cr, ci = off[j, k]
                    re = re - ar * cr - ai * ci
                    im = im + ar * ci - ai * cr
            row.append((re, im))
        t.append(row)
    out = []
    for i, j in PAIRS:
        out += list(entry(terms(t, False, u, True, i, j)))
    for k in range(2):
        out.append(entry_im(terms(t, False, u, True, k, k)))
    return out


def taylor(f):
    r01, i01, r02, i02, r12, i12, h0, h1 = f
    h2 = -(h0 + h1)
    n01 = r01 * r01 + i01 * i01
    n02 = r02 * r02 + i02 * i02
    n12 = r12 * r12 + i12 * i12
    y0 = -(h0 * h0 + n01 + n02)
    y1 = -(h1 * h1 + n01 + n12)
    y2 = -(h2 * h2 + n02 + n12)
    s = 0.5 * (y0 + y1 + y2)
    y01 = (h2 * i01 - (r02 * r12 + i02 * i12), -(h2 * r01) - (i02 * r12 - r02 * i12))
    y02 = (h1 * i02 + (r01 * r12 - i01 * i12), -(h1 * r02) + (r01 * i12 + i01 * r12))
    y12 = (h0 * i12 - (r01 * r02 + i01 * i02), -(h0 * r12) - (r01 * i02 - i01 * r02))
    zr = r01 * r12 - i01 * i12
    zi = r01 * i12 + i01 * r12
    trip = zi * r02 - zr * i02
    e = -(h0 * h1 * h2 + (trip + trip) - h0 * n12 - h1 * n02 - h2 * n01)
    q0r = 1.0 - e * e * (1.0 / 720.0)
    q0i = e * (1.0 / 6.0 + s * (1.0 / 120.0))
    q1r = 1.0 + s * (1.0 / 6.0 + s * (1.0 / 120.0))
    q1i = e * (1.0 / 24.0 + s * (1.0 / 360.0))
    q2r = 0.5 + s * (1.0 / 24.0 + s * (1.0 / 720.0))
    q2i = e * (1.0 / 120.0)
    out = [[None] * 3 for _ in range(3)]
    offs = (((r01, i01), y01), ((r02, i02), y02), ((r12, i12), y12))
    for (i, j), ((xr, xi), (yr, yi)) in zip(PAIRS, offs):
        p1, p2, p3, p4 = q1r * xr, q1i * xi, q1r * xi, q1i * xr
        s1, s2, s3, s4 = q2r * yr, q2i * yi, q2r * yi, q2i * yr
        out[i][j] = ((p1 - p2) + (s1 - s2), (p3 + p4) + (s3 + s4))
        out[j][i] = ((s1 + s2) - (p1 + p2), (p3 - p4) + (s4 - s3))
    for k, (h, y) in enumerate(((h0, y0), (h1, y1), (h2, y2))):
        out[k][k] = (q0r - q1i * h + q2r * y, q0i + q1r * h + q2i * y)
    return out


def masks():
    lane = lax.broadcasted_iota(jnp.int32, (8, 128), 1)
    z = lax.broadcasted_iota(jnp.int32, (8, 128), 0) & 3
    return {"x": lane & 15, "y": lane >> 4, "z": z}


def shift_x(v, m, up):
    if up:
        return jnp.where(m["x"] == 15, pltpu.roll(v, 15, 1), pltpu.roll(v, 127, 1))
    return jnp.where(m["x"] == 0, pltpu.roll(v, 113, 1), pltpu.roll(v, 1, 1))


def shift_y(v, m, up):
    r = pltpu.roll(v, 112 if up else 16, 1)
    return jnp.where(m["y"] == (7 if up else 0), pltpu.roll(r, 4, 0), r)


def mat(fetch):
    return [[(fetch(0, i, j), fetch(1, i, j)) for j in range(3)] for i in range(3)]


def on_mat(m, f):
    return [[(f(a), f(b)) for a, b in row] for row in m]


def plane(u_mu, u_nu, mu_up, nu_up):
    d = product(u_mu, u_nu, ha=True)
    g = product(mu_up, nu_up, hb=True)
    return twice_ta(g, d), twice_ta(d, g)


def unpack_rows(ref, base):
    m = [[(ref[base * 12 + i * 3 + j], ref[base * 12 + 6 + i * 3 + j]) for j in range(3)] for i in range(2)]
    third = []
    for k in range(3):
        a, b = (k + 1) % 3, (k + 2) % 3
        r1, i1 = entry([(m[0][a], False, m[1][b], False)])
        r2, i2 = entry([(m[0][b], False, m[1][a], False)])
        third.append((r1 - r2, i2 - i1))
    return m + [third]


def tiles(ref, shape):
    return ref.reshape(*shape, 8, 128)


def load_kernel(u_hbm, u_ref, st_ref, szt_ref, szxy_ref, sem):
    copies = {}
    for d in (3, 0, 1, 2):
        for h in range(2):
            src = u_hbm.at[d, :, :, :, :, :, pl.ds(128 * h, 128)]
            copies[d, h] = pltpu.make_async_copy(src, u_ref.at[d, :, :, :, :, h], sem.at[d, h])
            copies[d, h].start()
    u = tiles(u_ref, (4, 2, 3, 3, 4))
    rows = u_ref.reshape(4, 2, 3, 3, 32, 128)
    for d in (3, 0, 1, 2):
        for h in range(2):
            copies[d, h].wait()
        for p in range(2):
            for i in range(2):
                for j in range(3):
                    k = p * 6 + i * 3 + j
                    if d < 3:
                        st_ref[d * 12 + k] = u[d, p, i, j, 0]
                    if d < 2:
                        szxy_ref[d * 12 + k] = rows[d, p, i, j, pl.ds(0, 8, stride=4), :]
                    if d == 3:
                        szt_ref[k] = rows[d, p, i, j, pl.ds(0, 8, stride=4), :]


def accumulate(ref, mu, t, vals, sign=1):
    for k in range(8):
        if sign > 0:
            ref[mu, k, t] += vals[k]
        else:
            ref[mu, k, t] -= vals[k]


def inside(vals, m):
    return [jnp.where(m["z"] == 3, 0.0, v) for v in vals]


def next_z(v):
    return pltpu.roll(v, 7, 0)


def down_z(v, m):
    return jnp.where(m["z"] == 0, 0.0, pltpu.roll(v, 1, 0))


def links(u):
    return lambda d, t: mat(lambda p, i, j: u[d, p, i, j, t])


def side_z(c_ref, r_ref, mu, shift, m, t, u_mu, u_z):
    a, b = plane(u_mu, u_z, on_mat(u_mu, next_z), on_mat(u_z, lambda v: shift(v, m, True)))
    b = inside(b, m)
    accumulate(c_ref, 2, t, inside(a, m))
    accumulate(c_ref, mu, t, b, -1)
    accumulate(r_ref, mu, t, [down_z(v, m) for v in a])
    accumulate(r_ref, 2, t, [shift(v, m, False) for v in b], -1)


def zt_inside(c_ref, r_ref, m, t, u_z, u_t, z_up):
    a, b = plane(u_z, u_t, z_up, on_mat(u_t, next_z))
    a = inside(a, m)
    accumulate(c_ref, 3, t, a)
    accumulate(c_ref, 2, t, inside(b, m), -1)
    accumulate(r_ref, 2, t + 1, a)
    accumulate(r_ref, 3, t, [down_z(v, m) for v in b], -1)


def inner_kernel(u_ref, c_ref, r_ref):
    link = links(tiles(u_ref, (4, 2, 3, 3, 4)))
    m = masks()
    c_ref[...] = jnp.zeros_like(c_ref)
    r_ref[...] = jnp.zeros_like(r_ref)

    def spatial(t, carry):
        ux, uy, uz = link(0, t), link(1, t), link(2, t)
        a, b = plane(ux, uy, on_mat(ux, lambda v: shift_y(v, m, True)), on_mat(uy, lambda v: shift_x(v, m, True)))
        accumulate(c_ref, 1, t, a)
        accumulate(c_ref, 0, t, b, -1)
        accumulate(r_ref, 0, t, [shift_y(v, m, False) for v in a])
        accumulate(r_ref, 1, t, [shift_x(v, m, False) for v in b], -1)
        side_z(c_ref, r_ref, 0, shift_x, m, t, ux, uz)
        side_z(c_ref, r_ref, 1, shift_y, m, t, uy, uz)
        return carry

    lax.fori_loop(0, 4, spatial, 0)

    def timelike(t, carry):
        for mu, shift in ((0, shift_x), (1, shift_y)):
            side_time(c_ref, r_ref, mu, shift, m, t, link(mu, t), link(3, t), link(mu, t + 1))
        zt_inside(c_ref, r_ref, m, t, link(2, t), link(3, t), link(2, t + 1))
        return carry

    lax.fori_loop(0, 3, timelike, 0)


def side_time(c_ref, r_ref, mu, shift, m, t, u_mu, u_t, mu_up):
    a, b = plane(u_mu, u_t, mu_up, on_mat(u_t, lambda v: shift(v, m, True)))
    accumulate(c_ref, 3, t, a)
    accumulate(c_ref, mu, t, b, -1)
    accumulate(r_ref, mu, t + 1, a)
    accumulate(r_ref, 3, t, [shift(v, m, False) for v in b], -1)


LAST = pl.ds(3, 8, stride=4)


def edge_kernel(u_ref, ht_ref, hzt_ref, after_ref, fzt_ref, ab_ref, uz4_ref, pk_ref):
    rows = u_ref.reshape(4, 2, 3, 3, 32, 128)
    above = unpack_rows(ht_ref, 2)
    for p in range(2):
        for i in range(3):
            for j in range(3):
                uz4_ref[p, i, j] = above[i][j][p]
                pk_ref[p, i, j, pl.ds(0, 6), :] = rows[2, p, i, j, pl.ds(11, 6, stride=4), :]
                pk_ref[p, i, j, pl.ds(6, 2), :] = uz4_ref[p, i, j, pl.ds(3, 2, stride=4), :]
    uz = mat(lambda p, i, j: rows[2, p, i, j, LAST, :])
    ut = mat(lambda p, i, j: rows[3, p, i, j, LAST, :])
    a, b = plane(uz, ut, mat(lambda p, i, j: pk_ref[p, i, j]), unpack_rows(hzt_ref, 0))
    for k in range(8):
        fzt_ref[k] = -b[k]
        ab_ref[k] = a[k]
        ab_ref[8 + k] = b[k]


def expand(x_ref, n, tile, offset):
    x_ref[n] = jnp.zeros((32, 128), F32)
    x_ref[n, pl.ds(offset, 8, stride=4), :] = tile


def at(t):
    return pl.ds(t * 8 if isinstance(t, int) else pl.multiple_of(t * 8, 8), 8)


def middle_kernel(u_ref, ht_ref, uz4_ref, ab_ref, c_in, r_in, c_ref, r_ref, f_ref, ft_ref, x_ref):
    link = links(tiles(u_ref, (4, 2, 3, 3, 4)))
    m = masks()
    for k in range(16):
        expand(x_ref, k, ab_ref[k], 3)
    for k in range(8):
        for t in range(4):
            a = x_ref[k, at(t), :]
            c_ref[3, k, t] += a
            c_ref[2, k, t] -= x_ref[8 + k, at(t), :]
            r_ref[2, k, t + 1] += a
    for mu, shift in ((0, shift_x), (1, shift_y)):
        side_time(c_ref, r_ref, mu, shift, m, 3, link(mu, 3), link(3, 3), unpack_rows(ht_ref, mu))
    zt_inside(c_ref, r_ref, m, 3, link(2, 3), link(3, 3), get18(uz4_ref))
    for mu in range(3):
        for k in range(8):
            ft_ref[mu * 8 + k] = r_ref[mu, k, 4]

    def body(t, carry):
        w = transport(link(3, t), [c_ref[3, k, t] for k in range(8)])
        for k in range(8):
            f_ref[k, t] = w[k] + r_ref[3, k, t]
        return carry

    lax.fori_loop(0, 4, body, 0)


def packed_shift_y(v, m, up):
    r = pltpu.roll(v, 112 if up else 16, 1)
    other = jnp.where(m["odd"], pltpu.roll(r, 1, 0), pltpu.roll(r, 7, 0))
    return jnp.where(m["y"] == (7 if up else 0), other, r)


def late_edge_kernel(u_ref, hzxy_ref, after_ref, fz_ref, p_ref):
    rows = u_ref.reshape(4, 2, 3, 3, 32, 128)
    m = masks()
    m["odd"] = (lax.broadcasted_iota(jnp.int32, (8, 128), 0) & 1) == 1
    uz = mat(lambda p, i, j: rows[2, p, i, j, LAST, :])
    for mu, shift in ((0, shift_x), (1, packed_shift_y)):
        um = mat(lambda p, i, j: rows[mu, p, i, j, LAST, :])
        a, b = plane(um, uz, unpack_rows(hzxy_ref, mu), on_mat(uz, lambda v: shift(v, m, True)))
        for k in range(8):
            fz_ref[mu * 8 + k] = a[k]
            p_ref[mu * 8 + k] = b[k]
            back = shift(b[k], m, False)
            p_ref[16 + k] = a[k] if mu == 0 else p_ref[16 + k] + a[k]
            p_ref[24 + k] = back if mu == 0 else p_ref[24 + k] + back


def space_sum_kernel(u_ref, c_ref, r_ref, p_ref, after_ref, f_ref, x_ref):
    link = links(tiles(u_ref, (4, 2, 3, 3, 4)))
    for k in range(32):
        expand(x_ref, k, p_ref[k], 3)

    def body(t, carry):
        for mu in range(3):
            x = [x_ref[(16 if mu == 2 else mu * 8) + k, at(t), :] for k in range(8)]
            c = [c_ref[mu, k, t] for k in range(8)]
            w = transport(link(mu, t), [a + b if mu == 2 else a - b for a, b in zip(c, x)])
            for k in range(8):
                v = w[k] + r_ref[mu, k, t]
                f_ref[mu, k, t] = v - x_ref[24 + k, at(t), :] if mu == 2 else v
        return carry

    lax.fori_loop(0, 4, body, 0)


def finish(f, u, z_out, new_out):
    z = [-0.5 * v for v in f]
    zero = jnp.zeros_like(z[0])
    for n, (i, j) in enumerate(PAIRS):
        z_out(0, i, j, z[2 * n])
        z_out(1, i, j, z[2 * n + 1])
        z_out(0, j, i, -z[2 * n])
        z_out(1, j, i, z[2 * n + 1])
    for k, d in enumerate((z[6], z[7], -(z[6] + z[7]))):
        z_out(0, k, k, zero)
        z_out(1, k, k, d)
    new = product(taylor([0.125 * v for v in z]), u)
    for i in range(3):
        for j in range(3):
            for p in range(2):
                new_out(p, i, j, new[i][j][p])
    return new


def writer(ref, *head, t):
    def put(p, i, j, v):
        ref[(*head, p, i, j, t)] = v

    return put


def time_kernel(u_ref, f_ref, fz_ref, after_ref, zt_ref, nt_ref, s_ref, x_ref):
    link = links(tiles(u_ref, (4, 2, 3, 3, 4)))
    zt, nt = tiles(zt_ref, (2, 3, 3, 4)), tiles(nt_ref, (2, 3, 3, 4))
    for k in range(8):
        expand(x_ref, k, fz_ref[k], 0)

    def body(t, carry):
        f = [f_ref[k, t] + x_ref[k, at(t), :] for k in range(8)]
        finish(f, link(3, t), writer(zt, t=t), writer(nt, t=t))
        return carry

    lax.fori_loop(0, 4, body, 0)
    slab = mat(lambda p, i, j: nt[p, i, j, 0])
    for t in range(1, 4):
        slab = product(slab, mat(lambda p, i, j: nt[p, i, j, t]))
    put18(s_ref, slab)


def out_copies(src, dst, sem, d):
    return [pltpu.make_async_copy(src.at[:, :, :, :, h], dst.at[d, :, :, :, :, :, pl.ds(128 * h, 128)], sem.at[h]) for h in range(2)]


def space_kernel(u_ref, f_ref, fz_ref, ft_ref, zt_ref, nt_ref, new_hbm, z_hbm, zs_ref, ns_ref, x_ref, sem):
    link = links(tiles(u_ref, (4, 2, 3, 3, 4)))
    copies = out_copies(zt_ref, z_hbm, sem.at[6], 3) + out_copies(nt_ref, new_hbm, sem.at[7], 3)
    for c in copies:
        c.start()
    for k in range(16):
        expand(x_ref, k, fz_ref[k], 0)
    for k in range(24):
        f_ref[k // 8, k % 8, 0] += ft_ref[k]
    for mu in range(3):
        zs, ns = tiles(zs_ref.at[mu], (2, 3, 3, 4)), tiles(ns_ref.at[mu], (2, 3, 3, 4))

        def body(t, carry):
            f = [f_ref[mu, k, t] for k in range(8)]
            if mu < 2:
                f = [v + x_ref[mu * 8 + k, at(t), :] for k, v in enumerate(f)]
            finish(f, link(mu, t), writer(zs, t=t), writer(ns, t=t))
            return carry

        lax.fori_loop(0, 4, body, 0)
        more = out_copies(zs_ref.at[mu], z_hbm, sem.at[2 * mu], mu) + out_copies(ns_ref.at[mu], new_hbm, sem.at[2 * mu + 1], mu)
        for c in more:
            c.start()
        copies += more
    for c in copies:
        c.wait()


def get18(ref):
    return mat(lambda p, i, j: ref[p, i, j])


def put18(ref, m):
    for i in range(3):
        for j in range(3):
            for p in range(2):
                ref[p, i, j] = m[i][j][p]


def chain(mats):
    out = mats[0]
    for x in mats[1:]:
        out = product(out, x)
    return out


def join_kernel(s0_ref, s1_ref, s2_ref, s3_ref, head_ref, tail_ref, row_ref):
    x = lax.rem(lax.axis_index("tm"), ROW)
    cyc = [s0_ref, s1_ref, s2_ref, s3_ref]
    for n in range(ROW):

        @pl.when(x == n)
        def _():
            head = chain([get18(r) for r in cyc[: ROW - n]])
            put18(head_ref, head)
            if n == 0:
                put18(row_ref, head)
                one, zero = jnp.ones((8, 128), F32), jnp.zeros((8, 128), F32)
                put18(tail_ref, [[(one if i == j else zero, zero) for j in range(3)] for i in range(3)])
            else:
                tail = chain([get18(r) for r in cyc[ROW - n :]])
                put18(tail_ref, tail)
                put18(row_ref, product(tail, head))


def holonomy_kernel(head_ref, row_ref, tail_ref, out_hbm, o_ref, sem):
    loop = product(product(get18(head_ref), get18(row_ref)), get18(tail_ref))
    put18(tiles(o_ref, (2, 3, 3)), loop)
    copies = []
    for h in range(2):
        copies.append(pltpu.make_async_copy(o_ref.at[:, :, :, h], out_hbm.at[:, :, :, 0, :, pl.ds(128 * h, 128)], sem.at[h]))
    for c in copies:
        c.start()
    for c in copies:
        c.wait()


def call(kernel, outs, args, scratch=(), aliases=None, us=1.0):
    def spec(kind):
        return pl.BlockSpec(memory_space=VMEM if kind == "v" else pltpu.HBM)

    shapes = [VMEM(s, F32) if kind == "v" else jax.ShapeDtypeStruct(s, F32) for kind, s in outs]
    values = [pltpu.with_memory_space_constraint(x, VMEM if kind == "v" else pltpu.HBM) for kind, x in args]
    return pl.pallas_call(
        kernel,
        out_shape=shapes,
        in_specs=[spec(k) for k, _ in args],
        out_specs=[spec(k) for k, _ in outs],
        scratch_shapes=list(scratch),
        input_output_aliases=aliases or {},
        compiler_params=pltpu.CompilerParams(vmem_limit_bytes=24 << 20),
        cost_estimate=pl.CostEstimate(flops=int(us * 1e6), bytes_accessed=int(us * 3e6), transcendentals=0),
    )(*values)


def from_ahead(x, axis, k):
    n = lax.axis_size(axis)
    return lax.ppermute(x, axis, [(i, (i - k) % n) for i in range(n)])


def in_row(x, k):
    n = lax.axis_size("tm")
    return lax.ppermute(x, "tm", [(i, i // ROW * ROW + (i - k) % ROW) for i in range(n)])


def program(gauge_links):
    dma = pltpu.SemaphoreType.DMA
    whole = (4, 2, 3, 3, 4, 2, 4, 128)
    mat18 = ("v", (2, 3, 3, 8, 128))
    full = ("h", gauge_links.shape)

    def packed(n):
        return ("v", (n, 8, 128))

    u, st, szt, szxy = call(load_kernel, [("v", whole), packed(36), packed(12), packed(24)], [("h", gauge_links)], [dma((4, 2))])
    u = ("v", u)
    hzt = ("v", from_ahead(szt, "space", 1))
    ht = ("v", from_ahead(st, "tm", 1))
    hzxy = ("v", from_ahead(szxy, "space", 1))
    acc = [("v", (4, 8, 4, 8, 128)), ("v", (4, 8, 5, 8, 128))]
    c, r = call(inner_kernel, acc, [u], us=4.0)
    fzt, ab, uz4 = call(edge_kernel, [packed(8), packed(16), mat18], [u, ht, hzt, ("v", c)], [VMEM((2, 3, 3, 8, 128), F32)], us=0.3)
    fzt = ("v", from_ahead(fzt, "space", -1))
    c, r, f3, ft = call(
        middle_kernel,
        [*acc, ("v", (8, 4, 8, 128)), packed(24)],
        [u, ht, ("v", uz4), ("v", ab), ("v", c), ("v", r)],
        [VMEM((16, 32, 128), F32)],
        {4: 0, 5: 1},
    )
    ft = ("v", from_ahead(ft, "tm", -1))
    fz, p = call(late_edge_kernel, [packed(16), packed(32)], [u, hzxy, ("v", f3)], us=0.5)
    fz = ("v", from_ahead(fz, "space", -1))
    slices = ("v", (2, 3, 3, 4, 2, 4, 128))
    zt, nt, s = call(time_kernel, [slices, slices, mat18], [u, ("v", f3), fzt, ("v", p)], [VMEM((8, 32, 128), F32)], us=0.4)
    s1, s3, s2 = in_row(s, 1), in_row(s, 3), in_row(s, 2)
    (f,) = call(space_sum_kernel, [("v", (3, 8, 4, 8, 128))], [u, ("v", c), ("v", r), ("v", p), ("v", s)], [VMEM((32, 32, 128), F32)], us=1.0)
    head, tail, row = call(join_kernel, [mat18] * 3, [("v", s), ("v", s1), ("v", s2), ("v", s3)], us=0.1)
    row = from_ahead(row, "tm", ROW)
    stage = VMEM((3, 2, 3, 3, 4, 2, 4, 128), F32)
    new, force = call(
        space_kernel,
        [full, full],
        [u, ("v", f), fz, ft, ("v", zt), ("v", nt)],
        [stage, stage, VMEM((16, 32, 128), F32), dma((8, 2))],
        us=3.0,
    )
    (hol,) = call(
        holonomy_kernel,
        [("h", (2, 3, 3, 1, *gauge_links.shape[5:]))],
        [("v", head), ("v", row), ("v", tail)],
        [VMEM((2, 3, 3, 2, 4, 128), F32), dma((2,))],
    )
    return new, force, hol


def solution(mesh):
    in_specs = (P(None, None, None, None, "tm", "space", None),)
    out_specs = (
        P(None, None, None, None, "tm", "space", None),
        P(None, None, None, None, "tm", "space", None),
        P(None, None, None, "tm", "space", None),
    )
    return jax.shard_map(program, mesh=mesh, in_specs=in_specs, out_specs=out_specs, check_vma=False)
```

```python
import jax
import jax.numpy as jnp
from jax import lax
from jax.experimental import pallas as pl
from jax.experimental.pallas import tpu as pltpu
from jax.sharding import PartitionSpec as P


F32 = jnp.float32
VMEM = pltpu.VMEM
PAIRS = ((0, 1), (0, 2), (1, 2))
ROW = 4


def entry(terms):
    re = im = None
    for (ar, ai), ca, (br, bi), cb in terms:
        p = ar * br
        q = ai * bi
        re = p if re is None else re + p
        re = re + q if ca != cb else re - q
        u = ar * bi
        v = ai * br
        if im is None:
            im = (v - u) if cb and not ca else (u - v) if ca and not cb else (u + v)
        else:
            im = im - u if cb else im + u
            im = im - v if ca else im + v
    return re, im


def entry_im(terms):
    im = None
    for (ar, ai), ca, (br, bi), cb in terms:
        u = ar * bi
        v = ai * br
        if im is None:
            im = (v - u) if cb and not ca else (u - v) if ca and not cb else (u + v)
        else:
            im = im - u if cb else im + u
            im = im - v if ca else im + v
    return im


def terms(a, ha, b, hb, i, j):
    out = []
    for k in range(3):
        x = a[k][i] if ha else a[i][k]
        y = b[j][k] if hb else b[k][j]
        out.append((x, ha, y, hb))
    return out


def product(a, b, ha=False, hb=False):
    return [[entry(terms(a, ha, b, hb, i, j)) for j in range(3)] for i in range(3)]


def twice_ta(a, b):
    out = []
    for i, j in PAIRS:
        r1, i1 = entry(terms(a, False, b, False, i, j))
        r2, i2 = entry(terms(a, False, b, False, j, i))
        out += [r1 - r2, i1 + i2]
    d = [entry_im(terms(a, False, b, False, k, k)) for k in range(3)]
    tr = (d[0] + d[1] + d[2]) * (2.0 / 3.0)
    return out + [d[0] + d[0] - tr, d[1] + d[1] - tr]


def transport(u, c):
    r01, i01, r02, i02, r12, i12, d0, d1 = c
    d2 = -(d0 + d1)
    off = {(0, 1): (r01, i01), (0, 2): (r02, i02), (1, 2): (r12, i12)}
    diag = (d0, d1, d2)
    t = []
    for i in range(3):
        row = []
        for j in range(3):
            ur, ui = u[i][j]
            re = -(ui * diag[j])
            im = ur * diag[j]
            for k in range(3):
                if k == j:
                    continue
                ar, ai = u[i][k]
                if k < j:
                    cr, ci = off[k, j]
                    re = re + ar * cr - ai * ci
                    im = im + ar * ci + ai * cr
                else:
                    cr, ci = off[j, k]
                    re = re - ar * cr - ai * ci
                    im = im + ar * ci - ai * cr
            row.append((re, im))
        t.append(row)
    out = []
    for i, j in PAIRS:
        out += list(entry(terms(t, False, u, True, i, j)))
    for k in range(2):
        out.append(entry_im(terms(t, False, u, True, k, k)))
    return out


def taylor(f):
    r01, i01, r02, i02, r12, i12, h0, h1 = f
    h2 = -(h0 + h1)
    n01 = r01 * r01 + i01 * i01
    n02 = r02 * r02 + i02 * i02
    n12 = r12 * r12 + i12 * i12
    y0 = -(h0 * h0 + n01 + n02)
    y1 = -(h1 * h1 + n01 + n12)
    y2 = -(h2 * h2 + n02 + n12)
    s = 0.5 * (y0 + y1 + y2)
    y01 = (h2 * i01 - (r02 * r12 + i02 * i12), -(h2 * r01) - (i02 * r12 - r02 * i12))
    y02 = (h1 * i02 + (r01 * r12 - i01 * i12), -(h1 * r02) + (r01 * i12 + i01 * r12))
    y12 = (h0 * i12 - (r01 * r02 + i01 * i02), -(h0 * r12) - (r01 * i02 - i01 * r02))
    zr = r01 * r12 - i01 * i12
    zi = r01 * i12 + i01 * r12
    trip = zi * r02 - zr * i02
    e = -(h0 * h1 * h2 + (trip + trip) - h0 * n12 - h1 * n02 - h2 * n01)
    q0r = 1.0 - e * e * (1.0 / 720.0)
    q0i = e * (1.0 / 6.0 + s * (1.0 / 120.0))
    q1r = 1.0 + s * (1.0 / 6.0 + s * (1.0 / 120.0))
    q1i = e * (1.0 / 24.0 + s * (1.0 / 360.0))
    q2r = 0.5 + s * (1.0 / 24.0 + s * (1.0 / 720.0))
    q2i = e * (1.0 / 120.0)
    out = [[None] * 3 for _ in range(3)]
    offs = (((r01, i01), y01), ((r02, i02), y02), ((r12, i12), y12))
    for (i, j), ((xr, xi), (yr, yi)) in zip(PAIRS, offs):
        p1, p2, p3, p4 = q1r * xr, q1i * xi, q1r * xi, q1i * xr
        s1, s2, s3, s4 = q2r * yr, q2i * yi, q2r * yi, q2i * yr
        out[i][j] = ((p1 - p2) + (s1 - s2), (p3 + p4) + (s3 + s4))
        out[j][i] = ((s1 + s2) - (p1 + p2), (p3 - p4) + (s4 - s3))
    for k, (h, y) in enumerate(((h0, y0), (h1, y1), (h2, y2))):
        out[k][k] = (q0r - q1i * h + q2r * y, q0i + q1r * h + q2i * y)
    return out


def masks():
    lane = lax.broadcasted_iota(jnp.int32, (8, 128), 1)
    z = lax.broadcasted_iota(jnp.int32, (8, 128), 0) & 3
    return {"x": lane & 15, "y": lane >> 4, "z": z}


def shift_x(v, m, up):
    if up:
        return jnp.where(m["x"] == 15, pltpu.roll(v, 15, 1), pltpu.roll(v, 127, 1))
    return jnp.where(m["x"] == 0, pltpu.roll(v, 113, 1), pltpu.roll(v, 1, 1))


def shift_y(v, m, up):
    r = pltpu.roll(v, 112 if up else 16, 1)
    return jnp.where(m["y"] == (7 if up else 0), pltpu.roll(r, 4, 0), r)


def mat(fetch):
    return [[(fetch(0, i, j), fetch(1, i, j)) for j in range(3)] for i in range(3)]


def on_mat(m, f):
    return [[(f(a), f(b)) for a, b in row] for row in m]


def plane(u_mu, u_nu, mu_up, nu_up):
    d = product(u_mu, u_nu, ha=True)
    g = product(mu_up, nu_up, hb=True)
    return twice_ta(g, d), twice_ta(d, g)


def unpack_rows(ref, base):
    m = [[(ref[base * 12 + i * 3 + j], ref[base * 12 + 6 + i * 3 + j]) for j in range(3)] for i in range(2)]
    third = []
    for k in range(3):
        a, b = (k + 1) % 3, (k + 2) % 3
        r1, i1 = entry([(m[0][a], False, m[1][b], False)])
        r2, i2 = entry([(m[0][b], False, m[1][a], False)])
        third.append((r1 - r2, i2 - i1))
    return m + [third]


def tiles(ref, shape):
    return ref.reshape(*shape, 8, 128)


def load_kernel(u_hbm, u_ref, st_ref, szt_ref, szxy_ref, sem):
    copies = {}
    for d in (3, 0, 1, 2):
        for h in range(2):
            src = u_hbm.at[d, :, :, :, :, :, pl.ds(128 * h, 128)]
            copies[d, h] = pltpu.make_async_copy(src, u_ref.at[d, :, :, :, :, h], sem.at[d, h])
            copies[d, h].start()
    u = tiles(u_ref, (4, 2, 3, 3, 4))
    rows = u_ref.reshape(4, 2, 3, 3, 32, 128)
    for d in (3, 0, 1, 2):
        for h in range(2):
            copies[d, h].wait()
        for p in range(2):
            for i in range(2):
                for j in range(3):
                    k = p * 6 + i * 3 + j
                    if d < 3:
                        st_ref[d * 12 + k] = u[d, p, i, j, 0]
                    if d < 2:
                        szxy_ref[d * 12 + k] = rows[d, p, i, j, pl.ds(0, 8, stride=4), :]
                    if d == 3:
                        szt_ref[k] = rows[d, p, i, j, pl.ds(0, 8, stride=4), :]


def accumulate(ref, mu, t, vals, sign=1):
    for k in range(8):
        if sign > 0:
            ref[mu, k, t] += vals[k]
        else:
            ref[mu, k, t] -= vals[k]


def inside(vals, m):
    return [jnp.where(m["z"] == 3, 0.0, v) for v in vals]


def next_z(v):
    return pltpu.roll(v, 7, 0)


def down_z(v, m):
    return jnp.where(m["z"] == 0, 0.0, pltpu.roll(v, 1, 0))


def links(u):
    return lambda d, t: mat(lambda p, i, j: u[d, p, i, j, t])


def side_z(c_ref, r_ref, mu, shift, m, t, u_mu, u_z):
    a, b = plane(u_mu, u_z, on_mat(u_mu, next_z), on_mat(u_z, lambda v: shift(v, m, True)))
    b = inside(b, m)
    accumulate(c_ref, 2, t, inside(a, m))
    accumulate(c_ref, mu, t, b, -1)
    accumulate(r_ref, mu, t, [down_z(v, m) for v in a])
    accumulate(r_ref, 2, t, [shift(v, m, False) for v in b], -1)


def zt_inside(c_ref, r_ref, m, t, u_z, u_t, z_up):
    a, b = plane(u_z, u_t, z_up, on_mat(u_t, next_z))
    a = inside(a, m)
    accumulate(c_ref, 3, t, a)
    accumulate(c_ref, 2, t, inside(b, m), -1)
    accumulate(r_ref, 2, t + 1, a)
    accumulate(r_ref, 3, t, [down_z(v, m) for v in b], -1)


def flat_kernel(u_ref, c_ref, r_ref):
    link = links(tiles(u_ref, (4, 2, 3, 3, 4)))
    m = masks()
    c_ref[...] = jnp.zeros_like(c_ref)
    r_ref[...] = jnp.zeros_like(r_ref)

    def body(t, carry):
        ux, uy = link(0, t), link(1, t)
        a, b = plane(ux, uy, on_mat(ux, lambda v: shift_y(v, m, True)), on_mat(uy, lambda v: shift_x(v, m, True)))
        accumulate(c_ref, 1, t, a)
        accumulate(c_ref, 0, t, b, -1)
        accumulate(r_ref, 0, t, [shift_y(v, m, False) for v in a])
        accumulate(r_ref, 1, t, [shift_x(v, m, False) for v in b], -1)
        return carry

    lax.fori_loop(0, 4, body, 0)


def inner_kernel(u_ref, c_in, r_in, after_ref, c_ref, r_ref):
    link = links(tiles(u_ref, (4, 2, 3, 3, 4)))
    m = masks()

    def spatial(t, carry):
        uz = link(2, t)
        side_z(c_ref, r_ref, 0, shift_x, m, t, link(0, t), uz)
        side_z(c_ref, r_ref, 1, shift_y, m, t, link(1, t), uz)
        return carry

    lax.fori_loop(0, 4, spatial, 0)

    def timelike(t, carry):
        for mu, shift in ((0, shift_x), (1, shift_y)):
            side_time(c_ref, r_ref, mu, shift, m, t, link(mu, t), link(3, t), link(mu, t + 1))
        zt_inside(c_ref, r_ref, m, t, link(2, t), link(3, t), link(2, t + 1))
        return carry

    lax.fori_loop(0, 3, timelike, 0)


def side_time(c_ref, r_ref, mu, shift, m, t, u_mu, u_t, mu_up):
    a, b = plane(u_mu, u_t, mu_up, on_mat(u_t, lambda v: shift(v, m, True)))
    accumulate(c_ref, 3, t, a)
    accumulate(c_ref, mu, t, b, -1)
    accumulate(r_ref, mu, t + 1, a)
    accumulate(r_ref, 3, t, [shift(v, m, False) for v in b], -1)


LAST = pl.ds(3, 8, stride=4)


def edge_kernel(u_ref, ht_ref, hzt_ref, after_ref, fzt_ref, ab_ref, uz4_ref, pk_ref):
    rows = u_ref.reshape(4, 2, 3, 3, 32, 128)
    above = unpack_rows(ht_ref, 2)
    for p in range(2):
        for i in range(3):
            for j in range(3):
                uz4_ref[p, i, j] = above[i][j][p]
                pk_ref[p, i, j, pl.ds(0, 6), :] = rows[2, p, i, j, pl.ds(11, 6, stride=4), :]
                pk_ref[p, i, j, pl.ds(6, 2), :] = uz4_ref[p, i, j, pl.ds(3, 2, stride=4), :]
    uz = mat(lambda p, i, j: rows[2, p, i, j, LAST, :])
    ut = mat(lambda p, i, j: rows[3, p, i, j, LAST, :])
    a, b = plane(uz, ut, mat(lambda p, i, j: pk_ref[p, i, j]), unpack_rows(hzt_ref, 0))
    for k in range(8):
        fzt_ref[k] = -b[k]
        ab_ref[k] = a[k]
        ab_ref[8 + k] = b[k]


def expand(x_ref, n, tile, offset):
    x_ref[n] = jnp.zeros((32, 128), F32)
    x_ref[n, pl.ds(offset, 8, stride=4), :] = tile


def at(t):
    return pl.ds(t * 8 if isinstance(t, int) else pl.multiple_of(t * 8, 8), 8)


def middle_kernel(u_ref, ht_ref, uz4_ref, ab_ref, c_in, r_in, c_ref, r_ref, f_ref, ft_ref, x_ref):
    link = links(tiles(u_ref, (4, 2, 3, 3, 4)))
    m = masks()
    for k in range(16):
        expand(x_ref, k, ab_ref[k], 3)
    for k in range(8):
        for t in range(4):
            a = x_ref[k, at(t), :]
            c_ref[3, k, t] += a
            c_ref[2, k, t] -= x_ref[8 + k, at(t), :]
            r_ref[2, k, t + 1] += a
    for mu, shift in ((0, shift_x), (1, shift_y)):
        side_time(c_ref, r_ref, mu, shift, m, 3, link(mu, 3), link(3, 3), unpack_rows(ht_ref, mu))
    zt_inside(c_ref, r_ref, m, 3, link(2, 3), link(3, 3), get18(uz4_ref))
    for mu in range(3):
        for k in range(8):
            ft_ref[mu * 8 + k] = r_ref[mu, k, 4]

    def body(t, carry):
        w = transport(link(3, t), [c_ref[3, k, t] for k in range(8)])
        for k in range(8):
            f_ref[k, t] = w[k] + r_ref[3, k, t]
        return carry

    lax.fori_loop(0, 4, body, 0)


def packed_shift_y(v, m, up):
    r = pltpu.roll(v, 112 if up else 16, 1)
    other = jnp.where(m["odd"], pltpu.roll(r, 1, 0), pltpu.roll(r, 7, 0))
    return jnp.where(m["y"] == (7 if up else 0), other, r)


def late_edge_kernel(u_ref, hzxy_ref, after_ref, fz_ref, p_ref):
    rows = u_ref.reshape(4, 2, 3, 3, 32, 128)
    m = masks()
    m["odd"] = (lax.broadcasted_iota(jnp.int32, (8, 128), 0) & 1) == 1
    uz = mat(lambda p, i, j: rows[2, p, i, j, LAST, :])
    for mu, shift in ((0, shift_x), (1, packed_shift_y)):
        um = mat(lambda p, i, j: rows[mu, p, i, j, LAST, :])
        a, b = plane(um, uz, unpack_rows(hzxy_ref, mu), on_mat(uz, lambda v: shift(v, m, True)))
        for k in range(8):
            fz_ref[mu * 8 + k] = a[k]
            p_ref[mu * 8 + k] = b[k]
            back = shift(b[k], m, False)
            p_ref[16 + k] = a[k] if mu == 0 else p_ref[16 + k] + a[k]
            p_ref[24 + k] = back if mu == 0 else p_ref[24 + k] + back


def space_sum_kernel(u_ref, c_ref, r_ref, p_ref, after_ref, f_ref, x_ref):
    link = links(tiles(u_ref, (4, 2, 3, 3, 4)))
    for k in range(32):
        expand(x_ref, k, p_ref[k], 3)

    def body(t, carry):
        for mu in range(3):
            x = [x_ref[(16 if mu == 2 else mu * 8) + k, at(t), :] for k in range(8)]
            c = [c_ref[mu, k, t] for k in range(8)]
            w = transport(link(mu, t), [a + b if mu == 2 else a - b for a, b in zip(c, x)])
            for k in range(8):
                v = w[k] + r_ref[mu, k, t]
                f_ref[mu, k, t] = v - x_ref[24 + k, at(t), :] if mu == 2 else v
        return carry

    lax.fori_loop(0, 4, body, 0)


def finish(f, u, z_out, new_out):
    z = [-0.5 * v for v in f]
    zero = jnp.zeros_like(z[0])
    for n, (i, j) in enumerate(PAIRS):
        z_out(0, i, j, z[2 * n])
        z_out(1, i, j, z[2 * n + 1])
        z_out(0, j, i, -z[2 * n])
        z_out(1, j, i, z[2 * n + 1])
    for k, d in enumerate((z[6], z[7], -(z[6] + z[7]))):
        z_out(0, k, k, zero)
        z_out(1, k, k, d)
    new = product(taylor([0.125 * v for v in z]), u)
    for i in range(3):
        for j in range(3):
            for p in range(2):
                new_out(p, i, j, new[i][j][p])
    return new


def writer(ref, *head, t):
    def put(p, i, j, v):
        ref[(*head, p, i, j, t)] = v

    return put


def time_kernel(u_ref, f_ref, fz_ref, after_ref, zt_ref, nt_ref, s_ref, x_ref):
    link = links(tiles(u_ref, (4, 2, 3, 3, 4)))
    zt, nt = tiles(zt_ref, (2, 3, 3, 4)), tiles(nt_ref, (2, 3, 3, 4))
    for k in range(8):
        expand(x_ref, k, fz_ref[k], 0)

    def body(t, carry):
        f = [f_ref[k, t] + x_ref[k, at(t), :] for k in range(8)]
        finish(f, link(3, t), writer(zt, t=t), writer(nt, t=t))
        return carry

    lax.fori_loop(0, 4, body, 0)
    slab = mat(lambda p, i, j: nt[p, i, j, 0])
    for t in range(1, 4):
        slab = product(slab, mat(lambda p, i, j: nt[p, i, j, t]))
    put18(s_ref, slab)


def out_copies(src, dst, sem, d):
    return [pltpu.make_async_copy(src.at[:, :, :, :, h], dst.at[d, :, :, :, :, :, pl.ds(128 * h, 128)], sem.at[h]) for h in range(2)]


def space_kernel(u_ref, f_ref, fz_ref, ft_ref, zt_ref, nt_ref, new_hbm, z_hbm, zs_ref, ns_ref, x_ref, sem):
    link = links(tiles(u_ref, (4, 2, 3, 3, 4)))
    copies = out_copies(zt_ref, z_hbm, sem.at[6], 3) + out_copies(nt_ref, new_hbm, sem.at[7], 3)
    for c in copies:
        c.start()
    for k in range(16):
        expand(x_ref, k, fz_ref[k], 0)
    for k in range(24):
        f_ref[k // 8, k % 8, 0] += ft_ref[k]
    for mu in range(3):
        zs, ns = tiles(zs_ref.at[mu], (2, 3, 3, 4)), tiles(ns_ref.at[mu], (2, 3, 3, 4))

        def body(t, carry):
            f = [f_ref[mu, k, t] for k in range(8)]
            if mu < 2:
                f = [v + x_ref[mu * 8 + k, at(t), :] for k, v in enumerate(f)]
            finish(f, link(mu, t), writer(zs, t=t), writer(ns, t=t))
            return carry

        lax.fori_loop(0, 4, body, 0)
        more = out_copies(zs_ref.at[mu], z_hbm, sem.at[2 * mu], mu) + out_copies(ns_ref.at[mu], new_hbm, sem.at[2 * mu + 1], mu)
        for c in more:
            c.start()
        copies += more
    for c in copies:
        c.wait()


def get18(ref):
    return mat(lambda p, i, j: ref[p, i, j])


def put18(ref, m):
    for i in range(3):
        for j in range(3):
            for p in range(2):
                ref[p, i, j] = m[i][j][p]


def chain(mats):
    out = mats[0]
    for x in mats[1:]:
        out = product(out, x)
    return out


def join_kernel(s0_ref, s1_ref, s2_ref, s3_ref, head_ref, tail_ref, row_ref):
    x = lax.rem(lax.axis_index("tm"), ROW)
    cyc = [s0_ref, s1_ref, s2_ref, s3_ref]
    for n in range(ROW):

        @pl.when(x == n)
        def _():
            head = chain([get18(r) for r in cyc[: ROW - n]])
            put18(head_ref, head)
            if n == 0:
                put18(row_ref, head)
                one, zero = jnp.ones((8, 128), F32), jnp.zeros((8, 128), F32)
                put18(tail_ref, [[(one if i == j else zero, zero) for j in range(3)] for i in range(3)])
            else:
                tail = chain([get18(r) for r in cyc[ROW - n :]])
                put18(tail_ref, tail)
                put18(row_ref, product(tail, head))


def holonomy_kernel(head_ref, row_ref, tail_ref, out_hbm, o_ref, sem):
    loop = product(product(get18(head_ref), get18(row_ref)), get18(tail_ref))
    put18(tiles(o_ref, (2, 3, 3)), loop)
    copies = []
    for h in range(2):
        copies.append(pltpu.make_async_copy(o_ref.at[:, :, :, h], out_hbm.at[:, :, :, 0, :, pl.ds(128 * h, 128)], sem.at[h]))
    for c in copies:
        c.start()
    for c in copies:
        c.wait()


def call(kernel, outs, args, scratch=(), aliases=None, us=1.0):
    def spec(kind):
        return pl.BlockSpec(memory_space=VMEM if kind == "v" else pltpu.HBM)

    shapes = [VMEM(s, F32) if kind == "v" else jax.ShapeDtypeStruct(s, F32) for kind, s in outs]
    values = [pltpu.with_memory_space_constraint(x, VMEM if kind == "v" else pltpu.HBM) for kind, x in args]
    return pl.pallas_call(
        kernel,
        out_shape=shapes,
        in_specs=[spec(k) for k, _ in args],
        out_specs=[spec(k) for k, _ in outs],
        scratch_shapes=list(scratch),
        input_output_aliases=aliases or {},
        compiler_params=pltpu.CompilerParams(vmem_limit_bytes=24 << 20),
        cost_estimate=pl.CostEstimate(flops=int(us * 1e6), bytes_accessed=int(us * 3e6), transcendentals=0),
    )(*values)


def from_ahead(x, axis, k):
    n = lax.axis_size(axis)
    return lax.ppermute(x, axis, [(i, (i - k) % n) for i in range(n)])


def in_row(x, k):
    n = lax.axis_size("tm")
    return lax.ppermute(x, "tm", [(i, i // ROW * ROW + (i - k) % ROW) for i in range(n)])


def program(gauge_links):
    dma = pltpu.SemaphoreType.DMA
    whole = (4, 2, 3, 3, 4, 2, 4, 128)
    mat18 = ("v", (2, 3, 3, 8, 128))
    full = ("h", gauge_links.shape)

    def packed(n):
        return ("v", (n, 8, 128))

    u, st, szt, szxy = call(load_kernel, [("v", whole), packed(36), packed(12), packed(24)], [("h", gauge_links)], [dma((4, 2))])
    u = ("v", u)
    hzt = ("v", from_ahead(szt, "space", 1))
    ht = ("v", from_ahead(st, "tm", 1))
    hzxy = ("v", from_ahead(szxy, "space", 1))
    acc = [("v", (4, 8, 4, 8, 128)), ("v", (4, 8, 5, 8, 128))]
    c, r = call(flat_kernel, acc, [u], us=1.0)
    fzt, ab, uz4 = call(edge_kernel, [packed(8), packed(16), mat18], [u, ht, hzt, ("v", c)], [VMEM((2, 3, 3, 8, 128), F32)], us=0.3)
    fzt = ("v", from_ahead(fzt, "space", -1))
    c, r = call(inner_kernel, acc, [u, ("v", c), ("v", r), ("v", ab)], (), {1: 0, 2: 1}, us=3.0)
    c, r, f3, ft = call(
        middle_kernel,
        [*acc, ("v", (8, 4, 8, 128)), packed(24)],
        [u, ht, ("v", uz4), ("v", ab), ("v", c), ("v", r)],
        [VMEM((16, 32, 128), F32)],
        {4: 0, 5: 1},
    )
    ft = ("v", from_ahead(ft, "tm", -1))
    fz, p = call(late_edge_kernel, [packed(16), packed(32)], [u, hzxy, ("v", f3)], us=0.5)
    fz = ("v", from_ahead(fz, "space", -1))
    slices = ("v", (2, 3, 3, 4, 2, 4, 128))
    zt, nt, s = call(time_kernel, [slices, slices, mat18], [u, ("v", f3), fzt, ("v", p)], [VMEM((8, 32, 128), F32)], us=0.4)
    s1, s3, s2 = in_row(s, 1), in_row(s, 3), in_row(s, 2)
    (f,) = call(space_sum_kernel, [("v", (3, 8, 4, 8, 128))], [u, ("v", c), ("v", r), ("v", p), ("v", s)], [VMEM((32, 32, 128), F32)], us=1.0)
    head, tail, row = call(join_kernel, [mat18] * 3, [("v", s), ("v", s1), ("v", s2), ("v", s3)], us=0.1)
    row = from_ahead(row, "tm", ROW)
    stage = VMEM((3, 2, 3, 3, 4, 2, 4, 128), F32)
    new, force = call(
        space_kernel,
        [full, full],
        [u, ("v", f), fz, ft, ("v", zt), ("v", nt)],
        [stage, stage, VMEM((16, 32, 128), F32), dma((8, 2))],
        us=3.0,
    )
    (hol,) = call(
        holonomy_kernel,
        [("h", (2, 3, 3, 1, *gauge_links.shape[5:]))],
        [("v", head), ("v", row), ("v", tail)],
        [VMEM((2, 3, 3, 2, 4, 128), F32), dma((2,))],
    )
    return new, force, hol


def solution(mesh):
    in_specs = (P(None, None, None, None, "tm", "space", None),)
    out_specs = (
        P(None, None, None, None, "tm", "space", None),
        P(None, None, None, None, "tm", "space", None),
        P(None, None, None, "tm", "space", None),
    )
    return jax.shard_map(program, mesh=mesh, in_specs=in_specs, out_specs=out_specs, check_vma=False)
```

```python
import jax
import jax.numpy as jnp
from jax import lax
from jax.experimental import pallas as pl
from jax.experimental.pallas import tpu as pltpu
from jax.sharding import PartitionSpec as P


F32 = jnp.float32
VMEM = pltpu.VMEM
PAIRS = ((0, 1), (0, 2), (1, 2))
ROW = 4


def entry(terms):
    re = im = None
    for (ar, ai), ca, (br, bi), cb in terms:
        p = ar * br
        q = ai * bi
        re = p if re is None else re + p
        re = re + q if ca != cb else re - q
        u = ar * bi
        v = ai * br
        if im is None:
            im = (v - u) if cb and not ca else (u - v) if ca and not cb else (u + v)
        else:
            im = im - u if cb else im + u
            im = im - v if ca else im + v
    return re, im


def entry_im(terms):
    im = None
    for (ar, ai), ca, (br, bi), cb in terms:
        u = ar * bi
        v = ai * br
        if im is None:
            im = (v - u) if cb and not ca else (u - v) if ca and not cb else (u + v)
        else:
            im = im - u if cb else im + u
            im = im - v if ca else im + v
    return im


def terms(a, ha, b, hb, i, j):
    out = []
    for k in range(3):
        x = a[k][i] if ha else a[i][k]
        y = b[j][k] if hb else b[k][j]
        out.append((x, ha, y, hb))
    return out


def product(a, b, ha=False, hb=False):
    return [[entry(terms(a, ha, b, hb, i, j)) for j in range(3)] for i in range(3)]


def twice_ta(a, b):
    out = []
    for i, j in PAIRS:
        r1, i1 = entry(terms(a, False, b, False, i, j))
        r2, i2 = entry(terms(a, False, b, False, j, i))
        out += [r1 - r2, i1 + i2]
    d = [entry_im(terms(a, False, b, False, k, k)) for k in range(3)]
    tr = (d[0] + d[1] + d[2]) * (2.0 / 3.0)
    return out + [d[0] + d[0] - tr, d[1] + d[1] - tr]


def transport(u, c):
    r01, i01, r02, i02, r12, i12, d0, d1 = c
    d2 = -(d0 + d1)
    off = {(0, 1): (r01, i01), (0, 2): (r02, i02), (1, 2): (r12, i12)}
    diag = (d0, d1, d2)
    t = []
    for i in range(3):
        row = []
        for j in range(3):
            ur, ui = u[i][j]
            re = -(ui * diag[j])
            im = ur * diag[j]
            for k in range(3):
                if k == j:
                    continue
                ar, ai = u[i][k]
                if k < j:
                    cr, ci = off[k, j]
                    re = re + ar * cr - ai * ci
                    im = im + ar * ci + ai * cr
                else:
                    cr, ci = off[j, k]
                    re = re - ar * cr - ai * ci
                    im = im + ar * ci - ai * cr
            row.append((re, im))
        t.append(row)
    out = []
    for i, j in PAIRS:
        out += list(entry(terms(t, False, u, True, i, j)))
    for k in range(2):
        out.append(entry_im(terms(t, False, u, True, k, k)))
    return out


def taylor(f):
    r01, i01, r02, i02, r12, i12, h0, h1 = f
    h2 = -(h0 + h1)
    n01 = r01 * r01 + i01 * i01
    n02 = r02 * r02 + i02 * i02
    n12 = r12 * r12 + i12 * i12
    y0 = -(h0 * h0 + n01 + n02)
    y1 = -(h1 * h1 + n01 + n12)
    y2 = -(h2 * h2 + n02 + n12)
    s = 0.5 * (y0 + y1 + y2)
    y01 = (h2 * i01 - (r02 * r12 + i02 * i12), -(h2 * r01) - (i02 * r12 - r02 * i12))
    y02 = (h1 * i02 + (r01 * r12 - i01 * i12), -(h1 * r02) + (r01 * i12 + i01 * r12))
    y12 = (h0 * i12 - (r01 * r02 + i01 * i02), -(h0 * r12) - (r01 * i02 - i01 * r02))
    zr = r01 * r12 - i01 * i12
    zi = r01 * i12 + i01 * r12
    trip = zi * r02 - zr * i02
    e = -(h0 * h1 * h2 + (trip + trip) - h0 * n12 - h1 * n02 - h2 * n01)
    q0r = 1.0 - e * e * (1.0 / 720.0)
    q0i = e * (1.0 / 6.0 + s * (1.0 / 120.0))
    q1r = 1.0 + s * (1.0 / 6.0 + s * (1.0 / 120.0))
    q1i = e * (1.0 / 24.0 + s * (1.0 / 360.0))
    q2r = 0.5 + s * (1.0 / 24.0 + s * (1.0 / 720.0))
    q2i = e * (1.0 / 120.0)
    out = [[None] * 3 for _ in range(3)]
    offs = (((r01, i01), y01), ((r02, i02), y02), ((r12, i12), y12))
    for (i, j), ((xr, xi), (yr, yi)) in zip(PAIRS, offs):
        p1, p2, p3, p4 = q1r * xr, q1i * xi, q1r * xi, q1i * xr
        s1, s2, s3, s4 = q2r * yr, q2i * yi, q2r * yi, q2i * yr
        out[i][j] = ((p1 - p2) + (s1 - s2), (p3 + p4) + (s3 + s4))
        out[j][i] = ((s1 + s2) - (p1 + p2), (p3 - p4) + (s4 - s3))
    for k, (h, y) in enumerate(((h0, y0), (h1, y1), (h2, y2))):
        out[k][k] = (q0r - q1i * h + q2r * y, q0i + q1r * h + q2i * y)
    return out


def masks():
    lane = lax.broadcasted_iota(jnp.int32, (8, 128), 1)
    z = lax.broadcasted_iota(jnp.int32, (8, 128), 0) & 3
    return {"x": lane & 15, "y": lane >> 4, "z": z}


def shift_x(v, m, up):
    if up:
        return jnp.where(m["x"] == 15, pltpu.roll(v, 15, 1), pltpu.roll(v, 127, 1))
    return jnp.where(m["x"] == 0, pltpu.roll(v, 113, 1), pltpu.roll(v, 1, 1))


def shift_y(v, m, up):
    r = pltpu.roll(v, 112 if up else 16, 1)
    return jnp.where(m["y"] == (7 if up else 0), pltpu.roll(r, 4, 0), r)


def mat(fetch):
    return [[(fetch(0, i, j), fetch(1, i, j)) for j in range(3)] for i in range(3)]


def on_mat(m, f):
    return [[(f(a), f(b)) for a, b in row] for row in m]


def plane(u_mu, u_nu, mu_up, nu_up):
    d = product(u_mu, u_nu, ha=True)
    g = product(mu_up, nu_up, hb=True)
    return twice_ta(g, d), twice_ta(d, g)


def corner_loop(u_mu, u_nu, mu_up, nu_up, at_nu):
    d = product(u_mu, u_nu, ha=True)
    g = product(mu_up, nu_up, hb=True)
    return twice_ta(g, d) if at_nu else twice_ta(d, g)


def unpack_rows(ref, base):
    m = [[(ref[base * 12 + i * 3 + j], ref[base * 12 + 6 + i * 3 + j]) for j in range(3)] for i in range(2)]
    return m + [third_row(m)]


def third_row(m):
    third = []
    for k in range(3):
        a, b = (k + 1) % 3, (k + 2) % 3
        r1, i1 = entry([(m[0][a], False, m[1][b], False)])
        r2, i2 = entry([(m[0][b], False, m[1][a], False)])
        third.append((r1 - r2, i2 - i1))
    return third


def tiles(ref, shape):
    return ref.reshape(*shape, 8, 128)


FIRST = pl.ds(0, 8, stride=4)
LAST = pl.ds(3, 8, stride=4)


def load_kernel(u_hbm, u_ref, st_ref, low_ref, high_ref, corner_ref, sem):
    copies = {}
    for d in range(4):
        for h in range(2):
            src = u_hbm.at[d, :, :, :, :, :, pl.ds(128 * h, 128)]
            copies[d, h] = pltpu.make_async_copy(src, u_ref.at[d, :, :, :, :, h], sem.at[d, h])
            copies[d, h].start()
    u = tiles(u_ref, (4, 2, 3, 3, 4))
    rows = u_ref.reshape(4, 2, 3, 3, 32, 128)
    for d in range(4):
        for h in range(2):
            copies[d, h].wait()
        for p in range(2):
            for i in range(2):
                for j in range(3):
                    k = p * 6 + i * 3 + j
                    high_ref[d * 12 + k] = rows[d, p, i, j, LAST, :]
                    if d < 3:
                        st_ref[d * 12 + k] = u[d, p, i, j, 0]
                    if d != 2:
                        low_ref[min(d, 2) * 12 + k] = rows[d, p, i, j, FIRST, :]
                    if d == 2:
                        corner_ref[pl.ds(2 * k, 2), :] = rows[d, p, i, j, pl.ds(3, 2, stride=4), :]


def accumulate(ref, mu, t, vals, sign=1):
    for k in range(8):
        if sign > 0:
            ref[mu, k, t] += vals[k]
        else:
            ref[mu, k, t] -= vals[k]


def inside(vals, m):
    return [jnp.where(m["z"] == 3, 0.0, v) for v in vals]


def next_z(v):
    return pltpu.roll(v, 7, 0)


def down_z(v, m):
    return jnp.where(m["z"] == 0, 0.0, pltpu.roll(v, 1, 0))


def links(u):
    return lambda d, t: mat(lambda p, i, j: u[d, p, i, j, t])


def side_z(c_ref, r_ref, mu, shift, m, t, u_mu, u_z):
    a, b = plane(u_mu, u_z, on_mat(u_mu, next_z), on_mat(u_z, lambda v: shift(v, m, True)))
    b = inside(b, m)
    accumulate(c_ref, 2, t, inside(a, m))
    accumulate(c_ref, mu, t, b, -1)
    accumulate(r_ref, mu, t, [down_z(v, m) for v in a])
    accumulate(r_ref, 2, t, [shift(v, m, False) for v in b], -1)


def zt_inside(c_ref, r_ref, m, t, u_z, u_t, z_up):
    a, b = plane(u_z, u_t, z_up, on_mat(u_t, next_z))
    a = inside(a, m)
    accumulate(c_ref, 3, t, a)
    accumulate(c_ref, 2, t, inside(b, m), -1)
    accumulate(r_ref, 2, t + 1, a)
    accumulate(r_ref, 3, t, [down_z(v, m) for v in b], -1)


def steep_kernel(u_ref, c_ref, r_ref):
    link = links(tiles(u_ref, (4, 2, 3, 3, 4)))
    m = masks()
    c_ref[...] = jnp.zeros_like(c_ref)
    r_ref[...] = jnp.zeros_like(r_ref)

    def body(t, carry):
        for mu, shift in ((0, shift_x), (1, shift_y)):
            side_time(c_ref, r_ref, mu, shift, m, t, link(mu, t), link(3, t), link(mu, t + 1))
        zt_inside(c_ref, r_ref, m, t, link(2, t), link(3, t), link(2, t + 1))
        return carry

    lax.fori_loop(0, 3, body, 0)


def flat_kernel(u_ref, c_in, r_in, after_ref, c_ref, r_ref):
    link = links(tiles(u_ref, (4, 2, 3, 3, 4)))
    m = masks()

    def body(t, carry):
        ux, uy, uz = link(0, t), link(1, t), link(2, t)
        a, b = plane(ux, uy, on_mat(ux, lambda v: shift_y(v, m, True)), on_mat(uy, lambda v: shift_x(v, m, True)))
        accumulate(c_ref, 1, t, a)
        accumulate(c_ref, 0, t, b, -1)
        accumulate(r_ref, 0, t, [shift_y(v, m, False) for v in a])
        accumulate(r_ref, 1, t, [shift_x(v, m, False) for v in b], -1)
        side_z(c_ref, r_ref, 0, shift_x, m, t, ux, uz)
        side_z(c_ref, r_ref, 1, shift_y, m, t, uy, uz)
        return carry

    lax.fori_loop(0, 4, body, 0)


def side_time(c_ref, r_ref, mu, shift, m, t, u_mu, u_t, mu_up):
    a, b = plane(u_mu, u_t, mu_up, on_mat(u_t, lambda v: shift(v, m, True)))
    accumulate(c_ref, 3, t, a)
    accumulate(c_ref, mu, t, b, -1)
    accumulate(r_ref, mu, t + 1, a)
    accumulate(r_ref, 3, t, [shift(v, m, False) for v in b], -1)


def expand(x_ref, n, tile, offset):
    x_ref[n] = jnp.zeros((32, 128), F32)
    x_ref[n, pl.ds(offset, 8, stride=4), :] = tile


def at(t):
    return pl.ds(t * 8 if isinstance(t, int) else pl.multiple_of(t * 8, 8), 8)


def packed_shift_y(v, m, up):
    r = pltpu.roll(v, 112 if up else 16, 1)
    other = jnp.where(m["odd"], pltpu.roll(r, 1, 0), pltpu.roll(r, 7, 0))
    return jnp.where(m["y"] == (7 if up else 0), other, r)


def packed(rows, d, part):
    return mat(lambda p, i, j: rows[d, p, i, j, part, :])


def finish(f, u, z_out, new_out):
    z = [-0.5 * v for v in f]
    zero = jnp.zeros_like(z[0])
    for n, (i, j) in enumerate(PAIRS):
        z_out(0, i, j, z[2 * n])
        z_out(1, i, j, z[2 * n + 1])
        z_out(0, j, i, -z[2 * n])
        z_out(1, j, i, z[2 * n + 1])
    for k, d in enumerate((z[6], z[7], -(z[6] + z[7]))):
        z_out(0, k, k, zero)
        z_out(1, k, k, d)
    new = product(taylor([0.125 * v for v in z]), u)
    for i in range(3):
        for j in range(3):
            for p in range(2):
                new_out(p, i, j, new[i][j][p])
    return new


def writer(ref, *head, t):
    def put(p, i, j, v):
        ref[(*head, p, i, j, t)] = v

    return put


def time_kernel(u_ref, ht_ref, low_ref, high_ref, corner_ref, c_in, r_in, c_ref, r_ref, ft_ref, ab_ref, zt_ref, nt_ref, s_ref, x_ref, uz4_ref, pk_ref):
    link = links(tiles(u_ref, (4, 2, 3, 3, 4)))
    rows = u_ref.reshape(4, 2, 3, 3, 32, 128)
    zt, nt = tiles(zt_ref, (2, 3, 3, 4)), tiles(nt_ref, (2, 3, 3, 4))
    m = masks()
    above = unpack_rows(ht_ref, 2)
    for p in range(2):
        for i in range(3):
            for j in range(3):
                uz4_ref[p, i, j] = above[i][j][p]
                pk_ref[p, i, j, pl.ds(0, 6), :] = rows[2, p, i, j, pl.ds(11, 6, stride=4), :]
                pk_ref[p, i, j, pl.ds(6, 2), :] = uz4_ref[p, i, j, pl.ds(3, 2, stride=4), :]
    a, b = plane(packed(rows, 2, LAST), packed(rows, 3, LAST), get18(pk_ref), unpack_rows(low_ref, 2))
    for k in range(8):
        ab_ref[k] = a[k]
        ab_ref[8 + k] = b[k]
        expand(x_ref, k, a[k], 3)
    for k in range(12):
        pk_ref[k // 6, k // 3 % 2, k % 3, pl.ds(0, 6), :] = high_ref[24 + k, pl.ds(2, 6), :]
        pk_ref[k // 6, k // 3 % 2, k % 3, pl.ds(6, 2), :] = corner_ref[pl.ds(2 * k, 2), :]
    up = [[(pk_ref[0, i, j], pk_ref[1, i, j]) for j in range(3)] for i in range(2)]
    b = corner_loop(unpack_rows(high_ref, 2), unpack_rows(high_ref, 3), up + [third_row(up)], packed(rows, 3, FIRST), False)
    for k in range(8):
        expand(x_ref, 8 + k, b[k], 0)
    for mu, shift in ((0, shift_x), (1, shift_y)):
        side_time(c_ref, r_ref, mu, shift, m, 3, link(mu, 3), link(3, 3), unpack_rows(ht_ref, mu))
    zt_inside(c_ref, r_ref, m, 3, link(2, 3), link(3, 3), get18(uz4_ref))
    for mu in range(3):
        for k in range(8):
            v = r_ref[mu, k, 4]
            ft_ref[mu * 8 + k] = v + x_ref[k, at(3), :] if mu == 2 else v

    def body(t, carry):
        u = link(3, t)
        w = transport(u, [c_ref[3, k, t] + x_ref[k, at(t), :] for k in range(8)])
        f = [w[k] + (r_ref[3, k, t] - x_ref[8 + k, at(t), :]) for k in range(8)]
        finish(f, u, writer(zt, t=t), writer(nt, t=t))
        return carry

    lax.fori_loop(0, 4, body, 0)
    slab = mat(lambda p, i, j: nt[p, i, j, 0])
    for t in range(1, 4):
        slab = product(slab, mat(lambda p, i, j: nt[p, i, j, t]))
    put18(s_ref, slab)


def out_copies(src, dst, sem, d):
    return [pltpu.make_async_copy(src.at[:, :, :, :, h], dst.at[d, :, :, :, :, :, pl.ds(128 * h, 128)], sem.at[h]) for h in range(2)]


def space_kernel(u_ref, low_ref, high_ref, ab_ref, ft_ref, c_ref, r_ref, zt_ref, nt_ref, new_hbm, z_hbm, zs_ref, ns_ref, x_ref, sem):
    link = links(tiles(u_ref, (4, 2, 3, 3, 4)))
    rows = u_ref.reshape(4, 2, 3, 3, 32, 128)
    copies = out_copies(zt_ref, z_hbm, sem.at[6], 3) + out_copies(nt_ref, new_hbm, sem.at[7], 3)
    for c in copies:
        c.start()
    m = masks()
    line = lax.broadcasted_iota(jnp.int32, (8, 128), 0)
    m["odd"] = (line & 1) == 1
    uz = packed(rows, 2, LAST)
    uz_low = unpack_rows(high_ref, 2)
    cz = [-ab_ref[8 + k] for k in range(8)]
    rz = [jnp.where(line >= 2, pltpu.roll(ab_ref[k], 2, 0), 0.0) for k in range(8)]
    for mu, shift in ((0, shift_x), (1, packed_shift_y)):
        a, b = plane(packed(rows, mu, LAST), uz, unpack_rows(low_ref, mu), on_mat(uz, lambda v: shift(v, m, True)))
        for k in range(8):
            expand(x_ref, mu * 8 + k, -b[k], 3)
        cz = [v + a[k] for k, v in enumerate(cz)]
        rz = [v - shift(b[k], m, False) for k, v in enumerate(rz)]
        a = corner_loop(unpack_rows(high_ref, mu), uz_low, packed(rows, mu, FIRST), on_mat(uz_low, lambda v: shift(v, m, True)), True)
        for k in range(8):
            expand(x_ref, 32 + mu * 8 + k, a[k], 0)
    for k in range(8):
        expand(x_ref, 16 + k, cz[k], 3)
        expand(x_ref, 24 + k, rz[k], 3)
    for mu, first in ((0, 32), (1, 40), (2, 24)):
        for k in range(8):
            x_ref[first + k, at(0), :] += ft_ref[mu * 8 + k]
    for mu, first in ((0, 32), (1, 40), (2, 24)):
        zs, ns = tiles(zs_ref.at[mu], (2, 3, 3, 4)), tiles(ns_ref.at[mu], (2, 3, 3, 4))

        def body(t, carry):
            u = link(mu, t)
            w = transport(u, [c_ref[mu, k, t] + x_ref[mu * 8 + k, at(t), :] for k in range(8)])
            f = [w[k] + (r_ref[mu, k, t] + x_ref[first + k, at(t), :]) for k in range(8)]
            finish(f, u, writer(zs, t=t), writer(ns, t=t))
            return carry

        lax.fori_loop(0, 4, body, 0)
        more = out_copies(zs_ref.at[mu], z_hbm, sem.at[2 * mu], mu) + out_copies(ns_ref.at[mu], new_hbm, sem.at[2 * mu + 1], mu)
        for c in more:
            c.start()
        copies += more
    for c in copies:
        c.wait()


def get18(ref):
    return mat(lambda p, i, j: ref[p, i, j])


def put18(ref, m):
    for i in range(3):
        for j in range(3):
            for p in range(2):
                ref[p, i, j] = m[i][j][p]


def chain(mats):
    out = mats[0]
    for x in mats[1:]:
        out = product(out, x)
    return out


def join_kernel(s0_ref, s1_ref, s2_ref, s3_ref, head_ref, tail_ref, row_ref):
    x = lax.rem(lax.axis_index("tm"), ROW)
    cyc = [s0_ref, s1_ref, s2_ref, s3_ref]
    for n in range(ROW):

        @pl.when(x == n)
        def _():
            head = chain([get18(r) for r in cyc[: ROW - n]])
            put18(head_ref, head)
            if n == 0:
                put18(row_ref, head)
                one, zero = jnp.ones((8, 128), F32), jnp.zeros((8, 128), F32)
                put18(tail_ref, [[(one if i == j else zero, zero) for j in range(3)] for i in range(3)])
            else:
                tail = chain([get18(r) for r in cyc[ROW - n :]])
                put18(tail_ref, tail)
                put18(row_ref, product(tail, head))


def holonomy_kernel(head_ref, row_ref, tail_ref, out_hbm, o_ref, sem):
    loop = product(product(get18(head_ref), get18(row_ref)), get18(tail_ref))
    put18(tiles(o_ref, (2, 3, 3)), loop)
    copies = []
    for h in range(2):
        copies.append(pltpu.make_async_copy(o_ref.at[:, :, :, h], out_hbm.at[:, :, :, 0, :, pl.ds(128 * h, 128)], sem.at[h]))
    for c in copies:
        c.start()
    for c in copies:
        c.wait()


def call(kernel, outs, args, scratch=(), aliases=None, us=1.0):
    def spec(kind):
        return pl.BlockSpec(memory_space=VMEM if kind == "v" else pltpu.HBM)

    shapes = [VMEM(s, F32) if kind == "v" else jax.ShapeDtypeStruct(s, F32) for kind, s in outs]
    values = [pltpu.with_memory_space_constraint(x, VMEM if kind == "v" else pltpu.HBM) for kind, x in args]
    return pl.pallas_call(
        kernel,
        out_shape=shapes,
        in_specs=[spec(k) for k, _ in args],
        out_specs=[spec(k) for k, _ in outs],
        scratch_shapes=list(scratch),
        input_output_aliases=aliases or {},
        compiler_params=pltpu.CompilerParams(vmem_limit_bytes=24 << 20),
        cost_estimate=pl.CostEstimate(flops=int(us * 1e6), bytes_accessed=int(us * 3e6), transcendentals=0),
    )(*values)


def from_ahead(x, axis, k):
    n = lax.axis_size(axis)
    return lax.ppermute(x, axis, [(i, (i - k) % n) for i in range(n)])


def diagonal(x):
    n, k = lax.axis_size("space"), lax.axis_size("tm")
    pairs = [(i * k + j, (i + 1) % n * k + (j - 1) % k) for i in range(n) for j in range(k)]
    return lax.ppermute(x, ("space", "tm"), pairs)


def in_row(x, k):
    n = lax.axis_size("tm")
    return lax.ppermute(x, "tm", [(i, i // ROW * ROW + (i - k) % ROW) for i in range(n)])


def program(gauge_links):
    dma = pltpu.SemaphoreType.DMA
    whole = (4, 2, 3, 3, 4, 2, 4, 128)
    mat18 = ("v", (2, 3, 3, 8, 128))
    full = ("h", gauge_links.shape)

    def pack(n):
        return ("v", (n, 8, 128))

    u, st, low, high, corner = call(
        load_kernel, [("v", whole), pack(36), pack(36), pack(48), ("v", (24, 128))], [("h", gauge_links)], [dma((4, 2))]
    )
    u = ("v", u)
    high = ("v", from_ahead(high, "space", -1))
    corner = ("v", diagonal(corner))
    ht = ("v", from_ahead(st, "tm", 1))
    low = ("v", from_ahead(low, "space", 1))
    acc = [("v", (4, 8, 4, 8, 128)), ("v", (4, 8, 5, 8, 128))]
    slices = ("v", (2, 3, 3, 4, 2, 4, 128))
    c, r = call(steep_kernel, acc, [u], us=1.5)
    c, r, ft, ab, zt, nt, s = call(
        time_kernel,
        [*acc, pack(24), pack(16), slices, slices, mat18],
        [u, ht, low, high, corner, ("v", c), ("v", r)],
        [VMEM((16, 32, 128), F32), VMEM((2, 3, 3, 8, 128), F32), VMEM((2, 3, 3, 8, 128), F32)],
        {5: 0, 6: 1},
        us=1.4,
    )
    s1, s3, s2 = in_row(s, 1), in_row(s, 3), in_row(s, 2)
    ft = ("v", from_ahead(ft, "tm", -1))
    c, r = call(flat_kernel, acc, [u, ("v", c), ("v", r), ("v", s)], (), {1: 0, 2: 1}, us=2.0)
    head, tail, row = call(join_kernel, [mat18] * 3, [("v", s), ("v", s1), ("v", s2), ("v", s3)], us=0.1)
    row = from_ahead(row, "tm", ROW)
    stage = VMEM((3, 2, 3, 3, 4, 2, 4, 128), F32)
    new, force = call(
        space_kernel,
        [full, full],
        [u, low, high, ("v", ab), ft, ("v", c), ("v", r), ("v", zt), ("v", nt)],
        [stage, stage, VMEM((48, 32, 128), F32), dma((8, 2))],
        us=3.0,
    )
    (hol,) = call(
        holonomy_kernel,
        [("h", (2, 3, 3, 1, *gauge_links.shape[5:]))],
        [("v", head), ("v", row), ("v", tail)],
        [VMEM((2, 3, 3, 2, 4, 128), F32), dma((2,))],
    )
    return new, force, hol


def solution(mesh):
    in_specs = (P(None, None, None, None, "tm", "space", None),)
    out_specs = (
        P(None, None, None, None, "tm", "space", None),
        P(None, None, None, None, "tm", "space", None),
        P(None, None, None, "tm", "space", None),
    )
    return jax.shard_map(program, mesh=mesh, in_specs=in_specs, out_specs=out_specs, check_vma=False)
```

```python
import jax
import jax.numpy as jnp
from jax import lax
from jax.experimental import pallas as pl
from jax.experimental.pallas import tpu as pltpu
from jax.sharding import PartitionSpec as P


F32 = jnp.float32
VMEM = pltpu.VMEM
PAIRS = ((0, 1), (0, 2), (1, 2))
ROW = 4


def entry(terms):
    re = im = None
    for (ar, ai), ca, (br, bi), cb in terms:
        p = ar * br
        q = ai * bi
        re = p if re is None else re + p
        re = re + q if ca != cb else re - q
        u = ar * bi
        v = ai * br
        if im is None:
            im = (v - u) if cb and not ca else (u - v) if ca and not cb else (u + v)
        else:
            im = im - u if cb else im + u
            im = im - v if ca else im + v
    return re, im


def entry_im(terms):
    im = None
    for (ar, ai), ca, (br, bi), cb in terms:
        u = ar * bi
        v = ai * br
        if im is None:
            im = (v - u) if cb and not ca else (u - v) if ca and not cb else (u + v)
        else:
            im = im - u if cb else im + u
            im = im - v if ca else im + v
    return im


def terms(a, ha, b, hb, i, j):
    out = []
    for k in range(3):
        x = a[k][i] if ha else a[i][k]
        y = b[j][k] if hb else b[k][j]
        out.append((x, ha, y, hb))
    return out


def product(a, b, ha=False, hb=False):
    return [[entry(terms(a, ha, b, hb, i, j)) for j in range(3)] for i in range(3)]


def twice_ta(a, b):
    out = []
    for i, j in PAIRS:
        r1, i1 = entry(terms(a, False, b, False, i, j))
        r2, i2 = entry(terms(a, False, b, False, j, i))
        out += [r1 - r2, i1 + i2]
    d = [entry_im(terms(a, False, b, False, k, k)) for k in range(3)]
    tr = (d[0] + d[1] + d[2]) * (2.0 / 3.0)
    return out + [d[0] + d[0] - tr, d[1] + d[1] - tr]


def transport(u, c):
    r01, i01, r02, i02, r12, i12, d0, d1 = c
    d2 = -(d0 + d1)
    off = {(0, 1): (r01, i01), (0, 2): (r02, i02), (1, 2): (r12, i12)}
    diag = (d0, d1, d2)
    t = []
    for i in range(3):
        row = []
        for j in range(3):
            ur, ui = u[i][j]
            re = -(ui * diag[j])
            im = ur * diag[j]
            for k in range(3):
                if k == j:
                    continue
                ar, ai = u[i][k]
                if k < j:
                    cr, ci = off[k, j]
                    re = re + ar * cr - ai * ci
                    im = im + ar * ci + ai * cr
                else:
                    cr, ci = off[j, k]
                    re = re - ar * cr - ai * ci
                    im = im + ar * ci - ai * cr
            row.append((re, im))
        t.append(row)
    out = []
    for i, j in PAIRS:
        out += list(entry(terms(t, False, u, True, i, j)))
    for k in range(2):
        out.append(entry_im(terms(t, False, u, True, k, k)))
    return out


def taylor(f):
    r01, i01, r02, i02, r12, i12, h0, h1 = f
    h2 = -(h0 + h1)
    n01 = r01 * r01 + i01 * i01
    n02 = r02 * r02 + i02 * i02
    n12 = r12 * r12 + i12 * i12
    y0 = -(h0 * h0 + n01 + n02)
    y1 = -(h1 * h1 + n01 + n12)
    y2 = -(h2 * h2 + n02 + n12)
    s = 0.5 * (y0 + y1 + y2)
    y01 = (h2 * i01 - (r02 * r12 + i02 * i12), -(h2 * r01) - (i02 * r12 - r02 * i12))
    y02 = (h1 * i02 + (r01 * r12 - i01 * i12), -(h1 * r02) + (r01 * i12 + i01 * r12))
    y12 = (h0 * i12 - (r01 * r02 + i01 * i02), -(h0 * r12) - (r01 * i02 - i01 * r02))
    zr = r01 * r12 - i01 * i12
    zi = r01 * i12 + i01 * r12
    trip = zi * r02 - zr * i02
    e = -(h0 * h1 * h2 + (trip + trip) - h0 * n12 - h1 * n02 - h2 * n01)
    q0r = 1.0 - e * e * (1.0 / 720.0)
    q0i = e * (1.0 / 6.0 + s * (1.0 / 120.0))
    q1r = 1.0 + s * (1.0 / 6.0 + s * (1.0 / 120.0))
    q1i = e * (1.0 / 24.0 + s * (1.0 / 360.0))
    q2r = 0.5 + s * (1.0 / 24.0 + s * (1.0 / 720.0))
    q2i = e * (1.0 / 120.0)
    out = [[None] * 3 for _ in range(3)]
    offs = (((r01, i01), y01), ((r02, i02), y02), ((r12, i12), y12))
    for (i, j), ((xr, xi), (yr, yi)) in zip(PAIRS, offs):
        p1, p2, p3, p4 = q1r * xr, q1i * xi, q1r * xi, q1i * xr
        s1, s2, s3, s4 = q2r * yr, q2i * yi, q2r * yi, q2i * yr
        out[i][j] = ((p1 - p2) + (s1 - s2), (p3 + p4) + (s3 + s4))
        out[j][i] = ((s1 + s2) - (p1 + p2), (p3 - p4) + (s4 - s3))
    for k, (h, y) in enumerate(((h0, y0), (h1, y1), (h2, y2))):
        out[k][k] = (q0r - q1i * h + q2r * y, q0i + q1r * h + q2i * y)
    return out


def masks():
    lane = lax.broadcasted_iota(jnp.int32, (8, 128), 1)
    z = lax.broadcasted_iota(jnp.int32, (8, 128), 0) & 3
    return {"x": lane & 15, "y": lane >> 4, "z": z}


def shift_x(v, m, up):
    if up:
        return jnp.where(m["x"] == 15, pltpu.roll(v, 15, 1), pltpu.roll(v, 127, 1))
    return jnp.where(m["x"] == 0, pltpu.roll(v, 113, 1), pltpu.roll(v, 1, 1))


def shift_y(v, m, up):
    r = pltpu.roll(v, 112 if up else 16, 1)
    return jnp.where(m["y"] == (7 if up else 0), pltpu.roll(r, 4, 0), r)


def mat(fetch):
    return [[(fetch(0, i, j), fetch(1, i, j)) for j in range(3)] for i in range(3)]


def on_mat(m, f):
    return [[(f(a), f(b)) for a, b in row] for row in m]


def plane(u_mu, u_nu, mu_up, nu_up):
    d = product(u_mu, u_nu, ha=True)
    g = product(mu_up, nu_up, hb=True)
    return twice_ta(g, d), twice_ta(d, g)


def corner_loop(u_mu, u_nu, mu_up, nu_up, at_nu):
    d = product(u_mu, u_nu, ha=True)
    g = product(mu_up, nu_up, hb=True)
    return twice_ta(g, d) if at_nu else twice_ta(d, g)


def unpack_rows(ref, base):
    m = [[(ref[base * 12 + i * 3 + j], ref[base * 12 + 6 + i * 3 + j]) for j in range(3)] for i in range(2)]
    return m + [third_row(m)]


def third_row(m):
    third = []
    for k in range(3):
        a, b = (k + 1) % 3, (k + 2) % 3
        r1, i1 = entry([(m[0][a], False, m[1][b], False)])
        r2, i2 = entry([(m[0][b], False, m[1][a], False)])
        third.append((r1 - r2, i2 - i1))
    return third


def tiles(ref, shape):
    return ref.reshape(*shape, 8, 128)


FIRST = pl.ds(0, 8, stride=4)
LAST = pl.ds(3, 8, stride=4)


def load_kernel(u_hbm, u_ref, st_ref, lowt_ref, low_ref, high_ref, corner_ref, sem):
    whole = pltpu.make_async_copy(u_hbm, u_ref, sem)
    whole.start()
    whole.wait()
    u = tiles(u_ref, (4, 2, 3, 3, 4))
    rows = u_ref.reshape(4, 2, 3, 3, 32, 128)
    for d in range(4):
        for p in range(2):
            for i in range(2):
                for j in range(3):
                    k = p * 6 + i * 3 + j
                    high_ref[d * 12 + k] = rows[d, p, i, j, LAST, :]
                    if d < 3:
                        st_ref[d * 12 + k] = u[d, p, i, j, 0]
                    if d < 2:
                        low_ref[d * 12 + k] = rows[d, p, i, j, FIRST, :]
                    if d == 3:
                        lowt_ref[k] = rows[d, p, i, j, FIRST, :]
                    if d == 2:
                        corner_ref[pl.ds(2 * k, 2), :] = rows[d, p, i, j, pl.ds(3, 2, stride=4), :]


def accumulate(ref, mu, t, vals, sign=1):
    for k in range(8):
        if sign > 0:
            ref[mu, k, t] += vals[k]
        else:
            ref[mu, k, t] -= vals[k]


def inside(vals, m):
    return [jnp.where(m["z"] == 3, 0.0, v) for v in vals]


def next_z(v):
    return pltpu.roll(v, 7, 0)


def down_z(v, m):
    return jnp.where(m["z"] == 0, 0.0, pltpu.roll(v, 1, 0))


def links(u):
    return lambda d, t: mat(lambda p, i, j: u[d, p, i, j, t])


def side_z(c_ref, r_ref, mu, shift, m, t, u_mu, u_z):
    a, b = plane(u_mu, u_z, on_mat(u_mu, next_z), on_mat(u_z, lambda v: shift(v, m, True)))
    b = inside(b, m)
    accumulate(c_ref, 2, t, inside(a, m))
    accumulate(c_ref, mu, t, b, -1)
    accumulate(r_ref, mu, t, [down_z(v, m) for v in a])
    accumulate(r_ref, 2, t, [shift(v, m, False) for v in b], -1)


def zt_inside(c_ref, r_ref, m, t, u_z, u_t, z_up):
    a, b = plane(u_z, u_t, z_up, on_mat(u_t, next_z))
    a = inside(a, m)
    accumulate(c_ref, 3, t, a)
    accumulate(c_ref, 2, t, inside(b, m), -1)
    accumulate(r_ref, 2, t + 1, a)
    accumulate(r_ref, 3, t, [down_z(v, m) for v in b], -1)


def steep_kernel(u_ref, c_ref, r_ref):
    link = links(tiles(u_ref, (4, 2, 3, 3, 4)))
    m = masks()
    c_ref[...] = jnp.zeros_like(c_ref)
    r_ref[...] = jnp.zeros_like(r_ref)

    def body(t, carry):
        for mu, shift in ((0, shift_x), (1, shift_y)):
            side_time(c_ref, r_ref, mu, shift, m, t, link(mu, t), link(3, t), link(mu, t + 1))
        zt_inside(c_ref, r_ref, m, t, link(2, t), link(3, t), link(2, t + 1))
        return carry

    lax.fori_loop(0, 3, body, 0)


def flat_kernel(u_ref, low_ref, high_ref, ab_ref, c_in, r_in, after_ref, c_ref, r_ref, x_ref):
    link = links(tiles(u_ref, (4, 2, 3, 3, 4)))
    rows = u_ref.reshape(4, 2, 3, 3, 32, 128)
    m = masks()
    line = lax.broadcasted_iota(jnp.int32, (8, 128), 0)
    m["odd"] = (line & 1) == 1

    def body(t, carry):
        ux, uy, uz = link(0, t), link(1, t), link(2, t)
        a, b = plane(ux, uy, on_mat(ux, lambda v: shift_y(v, m, True)), on_mat(uy, lambda v: shift_x(v, m, True)))
        accumulate(c_ref, 1, t, a)
        accumulate(c_ref, 0, t, b, -1)
        accumulate(r_ref, 0, t, [shift_y(v, m, False) for v in a])
        accumulate(r_ref, 1, t, [shift_x(v, m, False) for v in b], -1)
        side_z(c_ref, r_ref, 0, shift_x, m, t, ux, uz)
        side_z(c_ref, r_ref, 1, shift_y, m, t, uy, uz)
        return carry

    lax.fori_loop(0, 4, body, 0)
    uz = packed(rows, 2, LAST)
    uz_low = unpack_rows(high_ref, 2)
    cz = [-ab_ref[8 + k] for k in range(8)]
    rz = [jnp.where(line >= 2, pltpu.roll(ab_ref[k], 2, 0), 0.0) for k in range(8)]
    for mu, shift in ((0, shift_x), (1, packed_shift_y)):
        a, b = plane(packed(rows, mu, LAST), uz, unpack_rows(low_ref, mu), on_mat(uz, lambda v: shift(v, m, True)))
        for k in range(8):
            expand(x_ref, mu * 8 + k, -b[k], 3)
        cz = [v + a[k] for k, v in enumerate(cz)]
        rz = [v - shift(b[k], m, False) for k, v in enumerate(rz)]
        a = corner_loop(unpack_rows(high_ref, mu), uz_low, packed(rows, mu, FIRST), on_mat(uz_low, lambda v: shift(v, m, True)), True)
        for k in range(8):
            expand(x_ref, 32 + mu * 8 + k, a[k], 0)
    for k in range(8):
        expand(x_ref, 16 + k, cz[k], 3)
        expand(x_ref, 24 + k, rz[k], 3)


def side_time(c_ref, r_ref, mu, shift, m, t, u_mu, u_t, mu_up):
    a, b = plane(u_mu, u_t, mu_up, on_mat(u_t, lambda v: shift(v, m, True)))
    accumulate(c_ref, 3, t, a)
    accumulate(c_ref, mu, t, b, -1)
    accumulate(r_ref, mu, t + 1, a)
    accumulate(r_ref, 3, t, [shift(v, m, False) for v in b], -1)


def expand(x_ref, n, tile, offset):
    x_ref[n] = jnp.zeros((32, 128), F32)
    x_ref[n, pl.ds(offset, 8, stride=4), :] = tile


def at(t):
    return pl.ds(t * 8 if isinstance(t, int) else pl.multiple_of(t * 8, 8), 8)


def packed_shift_y(v, m, up):
    r = pltpu.roll(v, 112 if up else 16, 1)
    other = jnp.where(m["odd"], pltpu.roll(r, 1, 0), pltpu.roll(r, 7, 0))
    return jnp.where(m["y"] == (7 if up else 0), other, r)


def packed(rows, d, part):
    return mat(lambda p, i, j: rows[d, p, i, j, part, :])


def finish(f, u, z_out, new_out):
    z = [-0.5 * v for v in f]
    zero = jnp.zeros_like(z[0])
    for n, (i, j) in enumerate(PAIRS):
        z_out(0, i, j, z[2 * n])
        z_out(1, i, j, z[2 * n + 1])
        z_out(0, j, i, -z[2 * n])
        z_out(1, j, i, z[2 * n + 1])
    for k, d in enumerate((z[6], z[7], -(z[6] + z[7]))):
        z_out(0, k, k, zero)
        z_out(1, k, k, d)
    new = product(taylor([0.125 * v for v in z]), u)
    for i in range(3):
        for j in range(3):
            for p in range(2):
                new_out(p, i, j, new[i][j][p])
    return new


def writer(ref, *head, t):
    def put(p, i, j, v):
        ref[(*head, p, i, j, t)] = v

    return put


def top_kernel(u_ref, ht_ref, c_in, r_in, c_ref, r_ref, uz4_ref):
    link = links(tiles(u_ref, (4, 2, 3, 3, 4)))
    m = masks()
    put18(uz4_ref, unpack_rows(ht_ref, 2))
    for mu, shift in ((0, shift_x), (1, shift_y)):
        side_time(c_ref, r_ref, mu, shift, m, 3, link(mu, 3), link(3, 3), unpack_rows(ht_ref, mu))
    zt_inside(c_ref, r_ref, m, 3, link(2, 3), link(3, 3), get18(uz4_ref))


def time_kernel(u_ref, uz4_ref, lowt_ref, high_ref, corner_ref, c_ref, r_ref, ft_ref, ab_ref, zt_ref, nt_ref, s_ref, x_ref, pk_ref):
    link = links(tiles(u_ref, (4, 2, 3, 3, 4)))
    rows = u_ref.reshape(4, 2, 3, 3, 32, 128)
    zt, nt = tiles(zt_ref, (2, 3, 3, 4)), tiles(nt_ref, (2, 3, 3, 4))
    for p in range(2):
        for i in range(3):
            for j in range(3):
                pk_ref[p, i, j, pl.ds(0, 6), :] = rows[2, p, i, j, pl.ds(11, 6, stride=4), :]
                pk_ref[p, i, j, pl.ds(6, 2), :] = uz4_ref[p, i, j, pl.ds(3, 2, stride=4), :]
    a, b = plane(packed(rows, 2, LAST), packed(rows, 3, LAST), get18(pk_ref), unpack_rows(lowt_ref, 0))
    for k in range(8):
        ab_ref[k] = a[k]
        ab_ref[8 + k] = b[k]
        expand(x_ref, k, a[k], 3)
    for k in range(12):
        pk_ref[k // 6, k // 3 % 2, k % 3, pl.ds(0, 6), :] = high_ref[24 + k, pl.ds(2, 6), :]
        pk_ref[k // 6, k // 3 % 2, k % 3, pl.ds(6, 2), :] = corner_ref[pl.ds(2 * k, 2), :]
    up = [[(pk_ref[0, i, j], pk_ref[1, i, j]) for j in range(3)] for i in range(2)]
    b = corner_loop(unpack_rows(high_ref, 2), unpack_rows(high_ref, 3), up + [third_row(up)], packed(rows, 3, FIRST), False)
    for k in range(8):
        expand(x_ref, 8 + k, b[k], 0)
    for mu in range(3):
        for k in range(8):
            v = r_ref[mu, k, 4]
            ft_ref[mu * 8 + k] = v + x_ref[k, at(3), :] if mu == 2 else v

    def body(t, carry):
        u = link(3, t)
        w = transport(u, [c_ref[3, k, t] + x_ref[k, at(t), :] for k in range(8)])
        f = [w[k] + (r_ref[3, k, t] - x_ref[8 + k, at(t), :]) for k in range(8)]
        finish(f, u, writer(zt, t=t), writer(nt, t=t))
        return carry

    lax.fori_loop(0, 4, body, 0)
    slab = mat(lambda p, i, j: nt[p, i, j, 0])
    for t in range(1, 4):
        slab = product(slab, mat(lambda p, i, j: nt[p, i, j, t]))
    put18(s_ref, slab)


def out_copies(src, dst, sem, d):
    return [pltpu.make_async_copy(src.at[h], dst.at[d, h], sem.at[h]) for h in range(2)]


def space_kernel(u_ref, x_ref, ft_ref, c_ref, r_ref, zt_ref, nt_ref, new_hbm, z_hbm, zs_ref, ns_ref, sem):
    link = links(tiles(u_ref, (4, 2, 3, 3, 4)))
    copies = out_copies(zt_ref, z_hbm, sem.at[6], 3) + out_copies(nt_ref, new_hbm, sem.at[7], 3)
    for c in copies:
        c.start()
    for mu, first in ((0, 32), (1, 40), (2, 24)):
        zs, ns = tiles(zs_ref.at[mu], (2, 3, 3, 4)), tiles(ns_ref.at[mu], (2, 3, 3, 4))

        def body(t, carry):
            u = link(mu, t)
            w = transport(u, [c_ref[mu, k, t] + x_ref[mu * 8 + k, at(t), :] for k in range(8)])
            f = [w[k] + (r_ref[mu, k, t] + x_ref[first + k, at(t), :]) for k in range(8)]
            below = jnp.where(t == 0, 1.0, 0.0)
            f = [v + below * ft_ref[mu * 8 + k] for k, v in enumerate(f)]
            finish(f, u, writer(zs, t=t), writer(ns, t=t))
            return carry

        lax.fori_loop(0, 4, body, 0)
        more = out_copies(zs_ref.at[mu], z_hbm, sem.at[2 * mu], mu) + out_copies(ns_ref.at[mu], new_hbm, sem.at[2 * mu + 1], mu)
        for c in more:
            c.start()
        copies += more
    for c in copies:
        c.wait()


def get18(ref):
    return mat(lambda p, i, j: ref[p, i, j])


def put18(ref, m):
    for i in range(3):
        for j in range(3):
            for p in range(2):
                ref[p, i, j] = m[i][j][p]


def chain(mats):
    out = mats[0]
    for x in mats[1:]:
        out = product(out, x)
    return out


def join_kernel(s0_ref, s1_ref, s2_ref, s3_ref, head_ref, tail_ref, row_ref):
    x = lax.rem(lax.axis_index("tm"), ROW)
    cyc = [s0_ref, s1_ref, s2_ref, s3_ref]
    for n in range(ROW):

        @pl.when(x == n)
        def _():
            head = chain([get18(r) for r in cyc[: ROW - n]])
            put18(head_ref, head)
            if n == 0:
                put18(row_ref, head)
                one, zero = jnp.ones((8, 128), F32), jnp.zeros((8, 128), F32)
                put18(tail_ref, [[(one if i == j else zero, zero) for j in range(3)] for i in range(3)])
            else:
                tail = chain([get18(r) for r in cyc[ROW - n :]])
                put18(tail_ref, tail)
                put18(row_ref, product(tail, head))


def holonomy_kernel(head_ref, row_ref, tail_ref, out_hbm, o_ref, sem):
    loop = product(product(get18(head_ref), get18(row_ref)), get18(tail_ref))
    put18(tiles(o_ref, (2, 3, 3)), loop)
    copies = []
    for h in range(2):
        copies.append(pltpu.make_async_copy(o_ref.at[h], out_hbm.at[h], sem.at[h]))
    for c in copies:
        c.start()
    for c in copies:
        c.wait()


def call(kernel, outs, args, scratch=(), aliases=None, us=1.0):
    def spec(kind):
        return pl.BlockSpec(memory_space=VMEM if kind == "v" else pltpu.HBM)

    shapes = [VMEM(s, F32) if kind == "v" else jax.ShapeDtypeStruct(s, F32) for kind, s in outs]
    values = [pltpu.with_memory_space_constraint(x, VMEM if kind == "v" else pltpu.HBM) for kind, x in args]
    return pl.pallas_call(
        kernel,
        out_shape=shapes,
        in_specs=[spec(k) for k, _ in args],
        out_specs=[spec(k) for k, _ in outs],
        scratch_shapes=list(scratch),
        input_output_aliases=aliases or {},
        compiler_params=pltpu.CompilerParams(vmem_limit_bytes=24 << 20),
        cost_estimate=pl.CostEstimate(flops=int(us * 1e6), bytes_accessed=int(us * 3e6), transcendentals=0),
    )(*values)


def from_ahead(x, axis, k):
    n = lax.axis_size(axis)
    return lax.ppermute(x, axis, [(i, (i - k) % n) for i in range(n)])


def diagonal(x):
    n, k = lax.axis_size("space"), lax.axis_size("tm")
    pairs = [(i * k + j, (i + 1) % n * k + (j - 1) % k) for i in range(n) for j in range(k)]
    return lax.ppermute(x, ("space", "tm"), pairs)


def in_row(x, k):
    n = lax.axis_size("tm")
    return lax.ppermute(x, "tm", [(i, i // ROW * ROW + (i - k) % ROW) for i in range(n)])


def plain(x, slices):
    return jnp.swapaxes(x, -3, -2).reshape(*x.shape[: -4 if slices > 1 else -3], slices, 4, 256)


def program(gauge_links):
    dma = pltpu.SemaphoreType.DMA
    whole = (4, 2, 3, 3, 4, 2, 4, 128)
    mat18 = ("v", (2, 3, 3, 8, 128))
    full = ("h", whole)
    gauge_links = jnp.swapaxes(gauge_links.reshape(4, 2, 3, 3, 4, 4, 2, 128), 5, 6)

    def pack(n):
        return ("v", (n, 8, 128))

    u, st, lowt, low, high, corner = call(
        load_kernel,
        [("v", whole), pack(36), pack(12), pack(24), pack(48), ("v", (24, 128))],
        [("h", gauge_links)],
        [dma(())],
    )
    u = ("v", u)
    high = ("v", from_ahead(high, "space", -1))
    corner = ("v", diagonal(corner))
    ht = ("v", from_ahead(st, "tm", 1))
    lowt = ("v", from_ahead(lowt, "space", 1))
    low = ("v", from_ahead(low, "space", 1))
    acc = [("v", (4, 8, 4, 8, 128)), ("v", (4, 8, 5, 8, 128))]
    slices = ("v", (2, 3, 3, 4, 2, 4, 128))
    c, r = call(steep_kernel, acc, [u], us=1.5)
    c, r, uz4 = call(top_kernel, [*acc, mat18], [u, ht, ("v", c), ("v", r)], (), {2: 0, 3: 1}, us=0.5)
    ft, ab, zt, nt, s = call(
        time_kernel,
        [pack(24), pack(16), slices, slices, mat18],
        [u, ("v", uz4), lowt, high, corner, ("v", c), ("v", r)],
        [VMEM((16, 32, 128), F32), VMEM((2, 3, 3, 8, 128), F32)],
        us=0.7,
    )
    s1, s3, s2 = in_row(s, 1), in_row(s, 3), in_row(s, 2)
    ft = ("v", from_ahead(ft, "tm", -1))
    edges = ("v", (48, 32, 128))
    c, r, x = call(flat_kernel, [*acc, edges], [u, low, high, ("v", ab), ("v", c), ("v", r), ("v", s)], (), {4: 0, 5: 1}, us=2.6)
    head, tail, row = call(join_kernel, [mat18] * 3, [("v", s), ("v", s1), ("v", s2), ("v", s3)], us=0.1)
    row = from_ahead(row, "tm", ROW)
    stage = VMEM((3, 2, 3, 3, 4, 2, 4, 128), F32)
    new, force = call(
        space_kernel,
        [full, full],
        [u, ("v", x), ft, ("v", c), ("v", r), ("v", zt), ("v", nt)],
        [stage, stage, dma((8, 2))],
        us=3.0,
    )
    (hol,) = call(
        holonomy_kernel,
        [("h", (2, 3, 3, 2, 4, 128))],
        [("v", head), ("v", row), ("v", tail)],
        [VMEM((2, 3, 3, 2, 4, 128), F32), dma((2,))],
    )
    return plain(new, 4), plain(force, 4), plain(hol, 1)


def solution(mesh):
    in_specs = (P(None, None, None, None, "tm", "space", None),)
    out_specs = (
        P(None, None, None, None, "tm", "space", None),
        P(None, None, None, None, "tm", "space", None),
        P(None, None, None, "tm", "space", None),
    )
    return jax.shard_map(program, mesh=mesh, in_specs=in_specs, out_specs=out_specs, check_vma=False)
```

```python
import jax
import jax.numpy as jnp
from jax import lax
from jax.experimental import pallas as pl
from jax.experimental.pallas import tpu as pltpu
from jax.sharding import PartitionSpec as P


F32 = jnp.float32
VMEM = pltpu.VMEM
PAIRS = ((0, 1), (0, 2), (1, 2))
ROW = 4


def entry(terms):
    re = im = None
    for (ar, ai), ca, (br, bi), cb in terms:
        p = ar * br
        q = ai * bi
        re = p if re is None else re + p
        re = re + q if ca != cb else re - q
        u = ar * bi
        v = ai * br
        if im is None:
            im = (v - u) if cb and not ca else (u - v) if ca and not cb else (u + v)
        else:
            im = im - u if cb else im + u
            im = im - v if ca else im + v
    return re, im


def entry_im(terms):
    im = None
    for (ar, ai), ca, (br, bi), cb in terms:
        u = ar * bi
        v = ai * br
        if im is None:
            im = (v - u) if cb and not ca else (u - v) if ca and not cb else (u + v)
        else:
            im = im - u if cb else im + u
            im = im - v if ca else im + v
    return im


def terms(a, ha, b, hb, i, j):
    out = []
    for k in range(3):
        x = a[k][i] if ha else a[i][k]
        y = b[j][k] if hb else b[k][j]
        out.append((x, ha, y, hb))
    return out


def product(a, b, ha=False, hb=False):
    return [[entry(terms(a, ha, b, hb, i, j)) for j in range(3)] for i in range(3)]


def twice_ta(a, b):
    out = []
    for i, j in PAIRS:
        r1, i1 = entry(terms(a, False, b, False, i, j))
        r2, i2 = entry(terms(a, False, b, False, j, i))
        out += [r1 - r2, i1 + i2]
    d = [entry_im(terms(a, False, b, False, k, k)) for k in range(3)]
    tr = (d[0] + d[1] + d[2]) * (2.0 / 3.0)
    return out + [d[0] + d[0] - tr, d[1] + d[1] - tr]


def transport(u, c):
    r01, i01, r02, i02, r12, i12, d0, d1 = c
    d2 = -(d0 + d1)
    off = {(0, 1): (r01, i01), (0, 2): (r02, i02), (1, 2): (r12, i12)}
    diag = (d0, d1, d2)
    t = []
    for i in range(3):
        row = []
        for j in range(3):
            ur, ui = u[i][j]
            re = -(ui * diag[j])
            im = ur * diag[j]
            for k in range(3):
                if k == j:
                    continue
                ar, ai = u[i][k]
                if k < j:
                    cr, ci = off[k, j]
                    re = re + ar * cr - ai * ci
                    im = im + ar * ci + ai * cr
                else:
                    cr, ci = off[j, k]
                    re = re - ar * cr - ai * ci
                    im = im + ar * ci - ai * cr
            row.append((re, im))
        t.append(row)
    out = []
    for i, j in PAIRS:
        out += list(entry(terms(t, False, u, True, i, j)))
    for k in range(2):
        out.append(entry_im(terms(t, False, u, True, k, k)))
    return out


def taylor(f):
    r01, i01, r02, i02, r12, i12, h0, h1 = f
    h2 = -(h0 + h1)
    n01 = r01 * r01 + i01 * i01
    n02 = r02 * r02 + i02 * i02
    n12 = r12 * r12 + i12 * i12
    y0 = -(h0 * h0 + n01 + n02)
    y1 = -(h1 * h1 + n01 + n12)
    y2 = -(h2 * h2 + n02 + n12)
    s = 0.5 * (y0 + y1 + y2)
    y01 = (h2 * i01 - (r02 * r12 + i02 * i12), -(h2 * r01) - (i02 * r12 - r02 * i12))
    y02 = (h1 * i02 + (r01 * r12 - i01 * i12), -(h1 * r02) + (r01 * i12 + i01 * r12))
    y12 = (h0 * i12 - (r01 * r02 + i01 * i02), -(h0 * r12) - (r01 * i02 - i01 * r02))
    zr = r01 * r12 - i01 * i12
    zi = r01 * i12 + i01 * r12
    trip = zi * r02 - zr * i02
    e = -(h0 * h1 * h2 + (trip + trip) - h0 * n12 - h1 * n02 - h2 * n01)
    q0r = 1.0 - e * e * (1.0 / 720.0)
    q0i = e * (1.0 / 6.0 + s * (1.0 / 120.0))
    q1r = 1.0 + s * (1.0 / 6.0 + s * (1.0 / 120.0))
    q1i = e * (1.0 / 24.0 + s * (1.0 / 360.0))
    q2r = 0.5 + s * (1.0 / 24.0 + s * (1.0 / 720.0))
    q2i = e * (1.0 / 120.0)
    out = [[None] * 3 for _ in range(3)]
    offs = (((r01, i01), y01), ((r02, i02), y02), ((r12, i12), y12))
    for (i, j), ((xr, xi), (yr, yi)) in zip(PAIRS, offs):
        p1, p2, p3, p4 = q1r * xr, q1i * xi, q1r * xi, q1i * xr
        s1, s2, s3, s4 = q2r * yr, q2i * yi, q2r * yi, q2i * yr
        out[i][j] = ((p1 - p2) + (s1 - s2), (p3 + p4) + (s3 + s4))
        out[j][i] = ((s1 + s2) - (p1 + p2), (p3 - p4) + (s4 - s3))
    for k, (h, y) in enumerate(((h0, y0), (h1, y1), (h2, y2))):
        out[k][k] = (q0r - q1i * h + q2r * y, q0i + q1r * h + q2i * y)
    return out


def masks():
    lane = lax.broadcasted_iota(jnp.int32, (8, 128), 1)
    z = lax.broadcasted_iota(jnp.int32, (8, 128), 0) & 3
    return {"x": lane & 15, "y": lane >> 4, "z": z}


def shift_x(v, m, up):
    if up:
        return jnp.where(m["x"] == 15, pltpu.roll(v, 15, 1), pltpu.roll(v, 127, 1))
    return jnp.where(m["x"] == 0, pltpu.roll(v, 113, 1), pltpu.roll(v, 1, 1))


def shift_y(v, m, up):
    r = pltpu.roll(v, 112 if up else 16, 1)
    return jnp.where(m["y"] == (7 if up else 0), pltpu.roll(r, 4, 0), r)


def mat(fetch):
    return [[(fetch(0, i, j), fetch(1, i, j)) for j in range(3)] for i in range(3)]


def on_mat(m, f):
    return [[(f(a), f(b)) for a, b in row] for row in m]


def special(a, b, ha=False, hb=False):
    m = [[entry(terms(a, ha, b, hb, i, j)) for j in range(3)] for i in range(2)]
    return m + [third_row(m)]


def plane(u_mu, u_nu, mu_up, nu_up):
    d = special(u_mu, u_nu, ha=True)
    g = special(mu_up, nu_up, hb=True)
    return twice_ta(g, d), twice_ta(d, g)


def corner_loop(u_mu, u_nu, mu_up, nu_up, at_nu):
    d = special(u_mu, u_nu, ha=True)
    g = special(mu_up, nu_up, hb=True)
    return twice_ta(g, d) if at_nu else twice_ta(d, g)


def unpack_rows(ref, base):
    m = [[(ref[base * 12 + i * 3 + j], ref[base * 12 + 6 + i * 3 + j]) for j in range(3)] for i in range(2)]
    return m + [third_row(m)]


def third_row(m):
    third = []
    for k in range(3):
        a, b = (k + 1) % 3, (k + 2) % 3
        r1, i1 = entry([(m[0][a], False, m[1][b], False)])
        r2, i2 = entry([(m[0][b], False, m[1][a], False)])
        third.append((r1 - r2, i2 - i1))
    return third


def tiles(ref, shape):
    return ref.reshape(*shape, 8, 128)


FIRST = pl.ds(0, 8, stride=4)
LAST = pl.ds(3, 8, stride=4)


def load_kernel(u_hbm, u_ref, st_ref, lowt_ref, low_ref, high_ref, corner_ref, sem):
    two = pl.ds(0, 2)
    copy = pltpu.make_async_copy(u_hbm.at[:, :, two], u_ref.at[:, :, two], sem)
    copy.start()
    copy.wait()
    u = tiles(u_ref, (4, 2, 3, 3, 4))
    rows = u_ref.reshape(4, 2, 3, 3, 32, 128)
    for d in range(4):
        for p in range(2):
            for i in range(2):
                for j in range(3):
                    k = p * 6 + i * 3 + j
                    high_ref[d * 12 + k] = rows[d, p, i, j, LAST, :]
                    if d < 3:
                        st_ref[d * 12 + k] = u[d, p, i, j, 0]
                    if d < 2:
                        low_ref[d * 12 + k] = rows[d, p, i, j, FIRST, :]
                    if d == 3:
                        lowt_ref[k] = rows[d, p, i, j, FIRST, :]
                    if d == 2:
                        corner_ref[pl.ds(2 * k, 2), :] = rows[d, p, i, j, pl.ds(3, 2, stride=4), :]


def accumulate(ref, mu, t, vals, sign=1):
    for k in range(8):
        if sign > 0:
            ref[mu, k, t] += vals[k]
        else:
            ref[mu, k, t] -= vals[k]


def inside(vals, m):
    return [jnp.where(m["z"] == 3, 0.0, v) for v in vals]


def next_z(v):
    return pltpu.roll(v, 7, 0)


def down_z(v, m):
    return jnp.where(m["z"] == 0, 0.0, pltpu.roll(v, 1, 0))


def links(u):
    return lambda d, t: mat(lambda p, i, j: u[d, p, i, j, t])


def zt_inside(c_ref, r_ref, m, t, u_z, u_t, z_up):
    a, b = plane(u_z, u_t, z_up, on_mat(u_t, next_z))
    a = inside(a, m)
    accumulate(c_ref, 3, t, a)
    accumulate(c_ref, 2, t, inside(b, m), -1)
    accumulate(r_ref, 2, t + 1, a)
    accumulate(r_ref, 3, t, [down_z(v, m) for v in b], -1)


def steep_kernel(u_in, u_ref, c_ref, r_ref):
    u = tiles(u_ref, (4, 2, 3, 3, 4))

    def complete(t, carry):
        for d in range(4):
            row = third_row([[(u[d, 0, i, j, t], u[d, 1, i, j, t]) for j in range(3)] for i in range(2)])
            for j in range(3):
                for p in range(2):
                    u[d, p, 2, j, t] = row[j][p]
        return carry

    lax.fori_loop(0, 4, complete, 0)
    link = links(u)
    m = masks()
    c_ref[...] = jnp.zeros_like(c_ref)
    r_ref[...] = jnp.zeros_like(r_ref)

    def body(t, carry):
        for mu, shift in ((0, shift_x), (1, shift_y)):
            side_time(c_ref, r_ref, mu, shift, m, t, link(mu, t), link(3, t), link(mu, t + 1))
        zt_inside(c_ref, r_ref, m, t, link(2, t), link(3, t), link(2, t + 1))
        return carry

    lax.fori_loop(0, 3, body, 0)


def flat_kernel(u_ref, low_ref, high_ref, ab_ref, c_in, r_in, after_ref, c_ref, r_ref, x_ref, above_ref):
    link = links(tiles(u_ref, (4, 2, 3, 3, 4)))
    rows = u_ref.reshape(4, 2, 3, 3, 32, 128)
    m = masks()
    line = lax.broadcasted_iota(jnp.int32, (8, 128), 0)
    m["odd"] = (line & 1) == 1
    for mu in range(2):
        halo = unpack_rows(low_ref, mu)
        for i in range(3):
            for j in range(3):
                for p in range(2):
                    above_ref[mu, p, i, j, LAST, :] = halo[i][j][p]

    def body(t, carry):
        us = [link(d, t) for d in range(3)]
        a, b = plane(us[0], us[1], on_mat(us[0], lambda v: shift_y(v, m, True)), on_mat(us[1], lambda v: shift_x(v, m, True)))
        accumulate(c_ref, 1, t, a)
        accumulate(c_ref, 0, t, b, -1)
        accumulate(r_ref, 0, t, [shift_y(v, m, False) for v in a])
        accumulate(r_ref, 1, t, [shift_x(v, m, False) for v in b], -1)
        for mu, shift in ((0, shift_x), (1, shift_y)):
            up = mat(lambda p, i, j: jnp.where(m["z"] == 3, above_ref[mu, p, i, j, at(t), :], next_z(us[mu][i][j][p])))
            a, b = plane(us[mu], us[2], up, on_mat(us[2], lambda v: shift(v, m, True)))
            accumulate(c_ref, 2, t, a)
            accumulate(c_ref, mu, t, b, -1)
            accumulate(r_ref, mu, t, [down_z(v, m) for v in a])
            accumulate(r_ref, 2, t, [shift(v, m, False) for v in b], -1)
        return carry

    lax.fori_loop(0, 4, body, 0)
    uz_low = unpack_rows(high_ref, 2)
    for mu, shift in ((0, shift_x), (1, packed_shift_y)):
        a = corner_loop(unpack_rows(high_ref, mu), uz_low, packed(rows, mu, FIRST), on_mat(uz_low, lambda v: shift(v, m, True)), True)
        for k in range(8):
            expand(x_ref, 16 + mu * 8 + k, a[k], 0)
    for k in range(8):
        expand(x_ref, k, -ab_ref[8 + k], 3)
        expand(x_ref, 8 + k, jnp.where(line >= 2, pltpu.roll(ab_ref[k], 2, 0), 0.0), 3)


def side_time(c_ref, r_ref, mu, shift, m, t, u_mu, u_t, mu_up):
    a, b = plane(u_mu, u_t, mu_up, on_mat(u_t, lambda v: shift(v, m, True)))
    accumulate(c_ref, 3, t, a)
    accumulate(c_ref, mu, t, b, -1)
    accumulate(r_ref, mu, t + 1, a)
    accumulate(r_ref, 3, t, [shift(v, m, False) for v in b], -1)


def expand(x_ref, n, tile, offset):
    x_ref[n] = jnp.zeros((32, 128), F32)
    x_ref[n, pl.ds(offset, 8, stride=4), :] = tile


def at(t):
    return pl.ds(t * 8 if isinstance(t, int) else pl.multiple_of(t * 8, 8), 8)


def packed_shift_y(v, m, up):
    r = pltpu.roll(v, 112 if up else 16, 1)
    other = jnp.where(m["odd"], pltpu.roll(r, 1, 0), pltpu.roll(r, 7, 0))
    return jnp.where(m["y"] == (7 if up else 0), other, r)


def packed(rows, d, part):
    return mat(lambda p, i, j: rows[d, p, i, j, part, :])


def finish(f, u, z_out, new_out):
    z = [-0.5 * v for v in f]
    zero = jnp.zeros_like(z[0])
    for n, (i, j) in enumerate(PAIRS):
        z_out(0, i, j, z[2 * n])
        z_out(1, i, j, z[2 * n + 1])
        z_out(0, j, i, -z[2 * n])
        z_out(1, j, i, z[2 * n + 1])
    for k, d in enumerate((z[6], z[7], -(z[6] + z[7]))):
        z_out(0, k, k, zero)
        z_out(1, k, k, d)
    new = product(taylor([0.125 * v for v in z]), u)
    for i in range(3):
        for j in range(3):
            for p in range(2):
                new_out(p, i, j, new[i][j][p])
    return new


def writer(ref, *head, t):
    def put(p, i, j, v):
        ref[(*head, p, i, j, t)] = v

    return put


def top_kernel(u_ref, ht_ref, c_in, r_in, c_ref, r_ref, uz4_ref):
    link = links(tiles(u_ref, (4, 2, 3, 3, 4)))
    m = masks()
    put18(uz4_ref, unpack_rows(ht_ref, 2))
    for mu, shift in ((0, shift_x), (1, shift_y)):
        side_time(c_ref, r_ref, mu, shift, m, 3, link(mu, 3), link(3, 3), unpack_rows(ht_ref, mu))
    zt_inside(c_ref, r_ref, m, 3, link(2, 3), link(3, 3), get18(uz4_ref))


def time_kernel(u_ref, uz4_ref, lowt_ref, high_ref, corner_ref, c_ref, r_ref, ft_ref, ab_ref, zt_ref, nt_ref, s_ref, x_ref, pk_ref):
    link = links(tiles(u_ref, (4, 2, 3, 3, 4)))
    rows = u_ref.reshape(4, 2, 3, 3, 32, 128)
    zt, nt = tiles(zt_ref, (2, 3, 3, 4)), tiles(nt_ref, (2, 3, 3, 4))
    for p in range(2):
        for i in range(3):
            for j in range(3):
                pk_ref[p, i, j, pl.ds(0, 6), :] = rows[2, p, i, j, pl.ds(11, 6, stride=4), :]
                pk_ref[p, i, j, pl.ds(6, 2), :] = uz4_ref[p, i, j, pl.ds(3, 2, stride=4), :]
    a, b = plane(packed(rows, 2, LAST), packed(rows, 3, LAST), get18(pk_ref), unpack_rows(lowt_ref, 0))
    for k in range(8):
        ab_ref[k] = a[k]
        ab_ref[8 + k] = b[k]
        expand(x_ref, k, a[k], 3)
    for k in range(12):
        pk_ref[k // 6, k // 3 % 2, k % 3, pl.ds(0, 6), :] = high_ref[24 + k, pl.ds(2, 6), :]
        pk_ref[k // 6, k // 3 % 2, k % 3, pl.ds(6, 2), :] = corner_ref[pl.ds(2 * k, 2), :]
    up = [[(pk_ref[0, i, j], pk_ref[1, i, j]) for j in range(3)] for i in range(2)]
    b = corner_loop(unpack_rows(high_ref, 2), unpack_rows(high_ref, 3), up + [third_row(up)], packed(rows, 3, FIRST), False)
    for k in range(8):
        expand(x_ref, 8 + k, b[k], 0)
    for mu in range(3):
        for k in range(8):
            v = r_ref[mu, k, 4]
            ft_ref[mu * 8 + k] = v + x_ref[k, at(3), :] if mu == 2 else v

    def body(t, carry):
        u = link(3, t)
        w = transport(u, [c_ref[3, k, t] + x_ref[k, at(t), :] for k in range(8)])
        f = [w[k] + (r_ref[3, k, t] - x_ref[8 + k, at(t), :]) for k in range(8)]
        finish(f, u, writer(zt, t=t), writer(nt, t=t))
        return carry

    lax.fori_loop(0, 4, body, 0)
    slab = mat(lambda p, i, j: nt[p, i, j, 0])
    for t in range(1, 4):
        slab = product(slab, mat(lambda p, i, j: nt[p, i, j, t]))
    put18(s_ref, slab)


def out_copies(src, dst, sem, d):
    return [pltpu.make_async_copy(src.at[h], dst.at[d, h], sem.at[h]) for h in range(2)]


def space_kernel(u_ref, x_ref, ft_ref, c_ref, r_ref, zt_ref, nt_ref, new_hbm, z_hbm, zs_ref, ns_ref, sem):
    link = links(tiles(u_ref, (4, 2, 3, 3, 4)))
    copies = out_copies(zt_ref, z_hbm, sem.at[6], 3) + out_copies(nt_ref, new_hbm, sem.at[7], 3)
    for c in copies:
        c.start()
    for mu, first in ((0, 16), (1, 24), (2, 8)):
        zs, ns = tiles(zs_ref.at[mu], (2, 3, 3, 4)), tiles(ns_ref.at[mu], (2, 3, 3, 4))

        def body(t, carry):
            u = link(mu, t)
            c = [c_ref[mu, k, t] for k in range(8)]
            if mu == 2:
                c = [v + x_ref[k, at(t), :] for k, v in enumerate(c)]
            w = transport(u, c)
            f = [w[k] + (r_ref[mu, k, t] + x_ref[first + k, at(t), :]) for k in range(8)]
            below = jnp.where(t == 0, 1.0, 0.0)
            f = [v + below * ft_ref[mu * 8 + k] for k, v in enumerate(f)]
            finish(f, u, writer(zs, t=t), writer(ns, t=t))
            return carry

        lax.fori_loop(0, 4, body, 0)
        more = out_copies(zs_ref.at[mu], z_hbm, sem.at[2 * mu], mu) + out_copies(ns_ref.at[mu], new_hbm, sem.at[2 * mu + 1], mu)
        for c in more:
            c.start()
        copies += more
    for c in copies:
        c.wait()


def get18(ref):
    return mat(lambda p, i, j: ref[p, i, j])


def put18(ref, m):
    for i in range(3):
        for j in range(3):
            for p in range(2):
                ref[p, i, j] = m[i][j][p]


def chain(mats):
    out = mats[0]
    for x in mats[1:]:
        out = product(out, x)
    return out


def join_kernel(s0_ref, s1_ref, s2_ref, s3_ref, head_ref, tail_ref, row_ref):
    x = lax.rem(lax.axis_index("tm"), ROW)
    cyc = [s0_ref, s1_ref, s2_ref, s3_ref]
    for n in range(ROW):

        @pl.when(x == n)
        def _():
            head = chain([get18(r) for r in cyc[: ROW - n]])
            put18(head_ref, head)
            if n == 0:
                put18(row_ref, head)
                one, zero = jnp.ones((8, 128), F32), jnp.zeros((8, 128), F32)
                put18(tail_ref, [[(one if i == j else zero, zero) for j in range(3)] for i in range(3)])
            else:
                tail = chain([get18(r) for r in cyc[ROW - n :]])
                put18(tail_ref, tail)
                put18(row_ref, product(tail, head))


def holonomy_kernel(head_ref, row_ref, tail_ref, out_hbm, o_ref, sem):
    loop = product(product(get18(head_ref), get18(row_ref)), get18(tail_ref))
    put18(tiles(o_ref, (2, 3, 3)), loop)
    copies = []
    for h in range(2):
        copies.append(pltpu.make_async_copy(o_ref.at[h], out_hbm.at[h], sem.at[h]))
    for c in copies:
        c.start()
    for c in copies:
        c.wait()


def call(kernel, outs, args, scratch=(), aliases=None, us=1.0):
    def spec(kind):
        return pl.BlockSpec(memory_space=VMEM if kind == "v" else pltpu.HBM)

    shapes = [VMEM(s, F32) if kind == "v" else jax.ShapeDtypeStruct(s, F32) for kind, s in outs]
    values = [pltpu.with_memory_space_constraint(x, VMEM if kind == "v" else pltpu.HBM) for kind, x in args]
    return pl.pallas_call(
        kernel,
        out_shape=shapes,
        in_specs=[spec(k) for k, _ in args],
        out_specs=[spec(k) for k, _ in outs],
        scratch_shapes=list(scratch),
        input_output_aliases=aliases or {},
        compiler_params=pltpu.CompilerParams(vmem_limit_bytes=24 << 20),
        cost_estimate=pl.CostEstimate(flops=int(us * 1e6), bytes_accessed=int(us * 3e6), transcendentals=0),
    )(*values)


def from_ahead(x, axis, k):
    n = lax.axis_size(axis)
    return lax.ppermute(x, axis, [(i, (i - k) % n) for i in range(n)])


def diagonal(x):
    n, k = lax.axis_size("space"), lax.axis_size("tm")
    pairs = [(i * k + j, (i + 1) % n * k + (j - 1) % k) for i in range(n) for j in range(k)]
    return lax.ppermute(x, ("space", "tm"), pairs)


def in_row(x, k):
    n = lax.axis_size("tm")
    return lax.ppermute(x, "tm", [(i, i // ROW * ROW + (i - k) % ROW) for i in range(n)])


def plain(x, slices):
    return jnp.swapaxes(x, -3, -2).reshape(*x.shape[: -4 if slices > 1 else -3], slices, 4, 256)


def program(gauge_links):
    dma = pltpu.SemaphoreType.DMA
    whole = (4, 2, 3, 3, 4, 2, 4, 128)
    mat18 = ("v", (2, 3, 3, 8, 128))
    full = ("h", whole)
    gauge_links = jnp.swapaxes(gauge_links.reshape(4, 2, 3, 3, 4, 4, 2, 128), 5, 6)

    def pack(n):
        return ("v", (n, 8, 128))

    u, st, lowt, low, high, corner = call(
        load_kernel,
        [("v", whole), pack(36), pack(12), pack(24), pack(48), ("v", (24, 128))],
        [("h", gauge_links)],
        [dma(())],
    )
    high = ("v", from_ahead(high, "space", -1))
    corner = ("v", diagonal(corner))
    ht = ("v", from_ahead(st, "tm", 1))
    lowt = ("v", from_ahead(lowt, "space", 1))
    low = ("v", from_ahead(low, "space", 1))
    acc = [("v", (4, 8, 4, 8, 128)), ("v", (4, 8, 5, 8, 128))]
    slices = ("v", (2, 3, 3, 4, 2, 4, 128))
    u, c, r = call(steep_kernel, [("v", whole), *acc], [("v", u)], (), {0: 0}, us=1.3)
    u = ("v", u)
    c, r, uz4 = call(top_kernel, [*acc, mat18], [u, ht, ("v", c), ("v", r)], (), {2: 0, 3: 1}, us=0.5)
    ft, ab, zt, nt, s = call(
        time_kernel,
        [pack(24), pack(16), slices, slices, mat18],
        [u, ("v", uz4), lowt, high, corner, ("v", c), ("v", r)],
        [VMEM((16, 32, 128), F32), VMEM((2, 3, 3, 8, 128), F32)],
        us=0.7,
    )
    s1, s3, s2 = in_row(s, 1), in_row(s, 3), in_row(s, 2)
    ft = ("v", from_ahead(ft, "tm", -1))
    edges = ("v", (32, 32, 128))
    c, r, x = call(
        flat_kernel,
        [*acc, edges],
        [u, low, high, ("v", ab), ("v", c), ("v", r), ("v", s)],
        [VMEM((2, 2, 3, 3, 32, 128), F32)],
        {4: 0, 5: 1},
        us=2.2,
    )
    head, tail, row = call(join_kernel, [mat18] * 3, [("v", s), ("v", s1), ("v", s2), ("v", s3)], us=0.1)
    row = from_ahead(row, "tm", ROW)
    stage = VMEM((3, 2, 3, 3, 4, 2, 4, 128), F32)
    new, force = call(
        space_kernel,
        [full, full],
        [u, ("v", x), ft, ("v", c), ("v", r), ("v", zt), ("v", nt)],
        [stage, stage, dma((8, 2))],
        us=3.0,
    )
    (hol,) = call(
        holonomy_kernel,
        [("h", (2, 3, 3, 2, 4, 128))],
        [("v", head), ("v", row), ("v", tail)],
        [VMEM((2, 3, 3, 2, 4, 128), F32), dma((2,))],
    )
    return plain(new, 4), plain(force, 4), plain(hol, 1)


def solution(mesh):
    in_specs = (P(None, None, None, None, "tm", "space", None),)
    out_specs = (
        P(None, None, None, None, "tm", "space", None),
        P(None, None, None, None, "tm", "space", None),
        P(None, None, None, "tm", "space", None),
    )
    return jax.shard_map(program, mesh=mesh, in_specs=in_specs, out_specs=out_specs, check_vma=False)
```

```python
import jax
import jax.numpy as jnp
from jax import lax
from jax.experimental import pallas as pl
from jax.experimental.pallas import tpu as pltpu
from jax.sharding import PartitionSpec as P


F32 = jnp.float32
VMEM = pltpu.VMEM
PAIRS = ((0, 1), (0, 2), (1, 2))
ROW = 4


def entry(terms):
    re = im = None
    for (ar, ai), ca, (br, bi), cb in terms:
        p = ar * br
        q = ai * bi
        re = p if re is None else re + p
        re = re + q if ca != cb else re - q
        u = ar * bi
        v = ai * br
        if im is None:
            im = (v - u) if cb and not ca else (u - v) if ca and not cb else (u + v)
        else:
            im = im - u if cb else im + u
            im = im - v if ca else im + v
    return re, im


def entry_im(terms):
    im = None
    for (ar, ai), ca, (br, bi), cb in terms:
        u = ar * bi
        v = ai * br
        if im is None:
            im = (v - u) if cb and not ca else (u - v) if ca and not cb else (u + v)
        else:
            im = im - u if cb else im + u
            im = im - v if ca else im + v
    return im


def terms(a, ha, b, hb, i, j):
    out = []
    for k in range(3):
        x = a[k][i] if ha else a[i][k]
        y = b[j][k] if hb else b[k][j]
        out.append((x, ha, y, hb))
    return out


def product(a, b, ha=False, hb=False):
    return [[entry(terms(a, ha, b, hb, i, j)) for j in range(3)] for i in range(3)]


def twice_ta(a, b):
    out = []
    for i, j in PAIRS:
        r1, i1 = entry(terms(a, False, b, False, i, j))
        r2, i2 = entry(terms(a, False, b, False, j, i))
        out += [r1 - r2, i1 + i2]
    d = [entry_im(terms(a, False, b, False, k, k)) for k in range(3)]
    tr = (d[0] + d[1] + d[2]) * (2.0 / 3.0)
    return out + [d[0] + d[0] - tr, d[1] + d[1] - tr]


def transport(u, c):
    r01, i01, r02, i02, r12, i12, d0, d1 = c
    d2 = -(d0 + d1)
    off = {(0, 1): (r01, i01), (0, 2): (r02, i02), (1, 2): (r12, i12)}
    diag = (d0, d1, d2)
    t = []
    for i in range(3):
        row = []
        for j in range(3):
            ur, ui = u[i][j]
            re = -(ui * diag[j])
            im = ur * diag[j]
            for k in range(3):
                if k == j:
                    continue
                ar, ai = u[i][k]
                if k < j:
                    cr, ci = off[k, j]
                    re = re + ar * cr - ai * ci
                    im = im + ar * ci + ai * cr
                else:
                    cr, ci = off[j, k]
                    re = re - ar * cr - ai * ci
                    im = im + ar * ci - ai * cr
            row.append((re, im))
        t.append(row)
    out = []
    for i, j in PAIRS:
        out += list(entry(terms(t, False, u, True, i, j)))
    for k in range(2):
        out.append(entry_im(terms(t, False, u, True, k, k)))
    return out


def taylor(f):
    r01, i01, r02, i02, r12, i12, h0, h1 = f
    h2 = -(h0 + h1)
    n01 = r01 * r01 + i01 * i01
    n02 = r02 * r02 + i02 * i02
    n12 = r12 * r12 + i12 * i12
    y0 = -(h0 * h0 + n01 + n02)
    y1 = -(h1 * h1 + n01 + n12)
    y2 = -(h2 * h2 + n02 + n12)
    s = 0.5 * (y0 + y1 + y2)
    y01 = (h2 * i01 - (r02 * r12 + i02 * i12), -(h2 * r01) - (i02 * r12 - r02 * i12))
    y02 = (h1 * i02 + (r01 * r12 - i01 * i12), -(h1 * r02) + (r01 * i12 + i01 * r12))
    y12 = (h0 * i12 - (r01 * r02 + i01 * i02), -(h0 * r12) - (r01 * i02 - i01 * r02))
    zr = r01 * r12 - i01 * i12
    zi = r01 * i12 + i01 * r12
    trip = zi * r02 - zr * i02
    e = -(h0 * h1 * h2 + (trip + trip) - h0 * n12 - h1 * n02 - h2 * n01)
    q0r = 1.0 - e * e * (1.0 / 720.0)
    q0i = e * (1.0 / 6.0 + s * (1.0 / 120.0))
    q1r = 1.0 + s * (1.0 / 6.0 + s * (1.0 / 120.0))
    q1i = e * (1.0 / 24.0 + s * (1.0 / 360.0))
    q2r = 0.5 + s * (1.0 / 24.0 + s * (1.0 / 720.0))
    q2i = e * (1.0 / 120.0)
    out = [[None] * 3 for _ in range(3)]
    offs = (((r01, i01), y01), ((r02, i02), y02), ((r12, i12), y12))
    for (i, j), ((xr, xi), (yr, yi)) in zip(PAIRS, offs):
        p1, p2, p3, p4 = q1r * xr, q1i * xi, q1r * xi, q1i * xr
        s1, s2, s3, s4 = q2r * yr, q2i * yi, q2r * yi, q2i * yr
        out[i][j] = ((p1 - p2) + (s1 - s2), (p3 + p4) + (s3 + s4))
        out[j][i] = ((s1 + s2) - (p1 + p2), (p3 - p4) + (s4 - s3))
    for k, (h, y) in enumerate(((h0, y0), (h1, y1), (h2, y2))):
        out[k][k] = (q0r - q1i * h + q2r * y, q0i + q1r * h + q2i * y)
    return out


def masks():
    lane = lax.broadcasted_iota(jnp.int32, (8, 128), 1)
    z = lax.broadcasted_iota(jnp.int32, (8, 128), 0) & 3
    return {"x": lane & 15, "y": lane >> 4, "z": z}


def shift_x(v, m, up):
    if up:
        return jnp.where(m["x"] == 15, pltpu.roll(v, 15, 1), pltpu.roll(v, 127, 1))
    return jnp.where(m["x"] == 0, pltpu.roll(v, 113, 1), pltpu.roll(v, 1, 1))


def shift_y(v, m, up):
    r = pltpu.roll(v, 112 if up else 16, 1)
    return jnp.where(m["y"] == (7 if up else 0), pltpu.roll(r, 4, 0), r)


def mat(fetch):
    return [[(fetch(0, i, j), fetch(1, i, j)) for j in range(3)] for i in range(3)]


def on_mat(m, f):
    return [[(f(a), f(b)) for a, b in row] for row in m]


def special(a, b, ha=False, hb=False):
    m = [[entry(terms(a, ha, b, hb, i, j)) for j in range(3)] for i in range(2)]
    return m + [third_row(m)]


def plane(u_mu, u_nu, mu_up, nu_up):
    d = special(u_mu, u_nu, ha=True)
    g = special(mu_up, nu_up, hb=True)
    return twice_ta(g, d), twice_ta(d, g)


def corner_loop(u_mu, u_nu, mu_up, nu_up, at_nu):
    d = special(u_mu, u_nu, ha=True)
    g = special(mu_up, nu_up, hb=True)
    return twice_ta(g, d) if at_nu else twice_ta(d, g)


def unpack_rows(ref, base):
    m = [[(ref[base * 12 + i * 3 + j], ref[base * 12 + 6 + i * 3 + j]) for j in range(3)] for i in range(2)]
    return m + [third_row(m)]


def third_row(m):
    third = []
    for k in range(3):
        a, b = (k + 1) % 3, (k + 2) % 3
        r1, i1 = entry([(m[0][a], False, m[1][b], False)])
        r2, i2 = entry([(m[0][b], False, m[1][a], False)])
        third.append((r1 - r2, i2 - i1))
    return third


def tiles(ref, shape):
    return ref.reshape(*shape, 8, 128)


FIRST = pl.ds(0, 8, stride=4)
LAST = pl.ds(3, 8, stride=4)


def load_kernel(u_hbm, u_ref, st_ref, lowt_ref, low_ref, high_ref, corner_ref, sem):
    two = pl.ds(0, 2)
    copy = pltpu.make_async_copy(u_hbm.at[:, :, two], u_ref.at[:, :, two], sem)
    copy.start()
    copy.wait()
    u = tiles(u_ref, (4, 2, 3, 3, 4))
    rows = u_ref.reshape(4, 2, 3, 3, 32, 128)
    for d in range(4):
        for p in range(2):
            for i in range(2):
                for j in range(3):
                    k = p * 6 + i * 3 + j
                    high_ref[d * 12 + k] = rows[d, p, i, j, LAST, :]
                    if d < 3:
                        st_ref[d * 12 + k] = u[d, p, i, j, 0]
                    if d < 2:
                        low_ref[d * 12 + k] = rows[d, p, i, j, FIRST, :]
                    if d == 3:
                        lowt_ref[k] = rows[d, p, i, j, FIRST, :]
                    if d == 2:
                        corner_ref[pl.ds(2 * k, 2), :] = rows[d, p, i, j, pl.ds(3, 2, stride=4), :]


def accumulate(ref, mu, t, vals, sign=1):
    for k in range(8):
        if sign > 0:
            ref[mu, k, t] += vals[k]
        else:
            ref[mu, k, t] -= vals[k]


def inside(vals, m):
    return [jnp.where(m["z"] == 3, 0.0, v) for v in vals]


def next_z(v):
    return pltpu.roll(v, 7, 0)


def down_z(v, m):
    return jnp.where(m["z"] == 0, 0.0, pltpu.roll(v, 1, 0))


def links(u):
    return lambda d, t: mat(lambda p, i, j: u[d, p, i, j, t])


TURNS = (shift_x, shift_y, None)


def upward(mu, v, m):
    return TURNS[mu](v, m, True) if mu < 2 else next_z(v)


def time_loops(u_t, loops, c_ref, r_ref, m, t):
    own = back = None
    for mu, (a, b) in enumerate(loops):
        down = [TURNS[mu](v, m, False) for v in b] if mu < 2 else [down_z(v, m) for v in b]
        if mu == 2:
            a, b = inside(a, m), inside(b, m)
        accumulate(c_ref, mu, t, b, -1)
        accumulate(r_ref, mu, t + 1, a)
        own = a if own is None else [v + w for v, w in zip(own, a)]
        back = down if back is None else [v + w for v, w in zip(back, down)]
    return [v - w for v, w in zip(transport(u_t, own), back)]


def steep_kernel(u_in, u_ref, c_ref, r_ref, f_ref, d_ref, up_ref):
    u = tiles(u_ref, (4, 2, 3, 3, 4))
    rows = u_ref.reshape(4, 2, 3, 3, 32, 128)

    def complete(t, carry):
        for d in range(4):
            row = third_row([[(u[d, 0, i, j, t], u[d, 1, i, j, t]) for j in range(3)] for i in range(2)])
            for j in range(3):
                for p in range(2):
                    u[d, p, 2, j, t] = row[j][p]
        return carry

    lax.fori_loop(0, 4, complete, 0)
    link = links(u)
    m = masks()
    c_ref[...] = jnp.zeros_like(c_ref)
    r_ref[...] = jnp.zeros_like(r_ref)

    def body(t, carry):
        ut = link(3, t)
        loops = (plane(link(mu, t), ut, link(mu, t + 1), on_mat(ut, lambda v: upward(mu, v, m))) for mu in range(3))
        f = time_loops(ut, loops, c_ref, r_ref, m, t)
        for k in range(8):
            f_ref[k, t] = f[k]
        return carry

    lax.fori_loop(0, 3, body, 0)
    ut = link(3, 3)
    for mu in range(3):
        put18(d_ref.at[mu], special(link(mu, 3), ut, ha=True))
        put18(up_ref.at[mu], on_mat(ut, lambda v: upward(mu, v, m)))
    put18(d_ref.at[3], special(packed(rows, 2, LAST), packed(rows, 3, LAST), ha=True))


def flat_kernel(u_ref, low_ref, high_ref, ab_ref, c_in, r_in, after_ref, c_ref, r_ref, x_ref, above_ref):
    link = links(tiles(u_ref, (4, 2, 3, 3, 4)))
    rows = u_ref.reshape(4, 2, 3, 3, 32, 128)
    m = masks()
    line = lax.broadcasted_iota(jnp.int32, (8, 128), 0)
    m["odd"] = (line & 1) == 1
    for mu in range(2):
        halo = unpack_rows(low_ref, mu)
        for i in range(3):
            for j in range(3):
                for p in range(2):
                    above_ref[mu, p, i, j, LAST, :] = halo[i][j][p]

    def body(t, carry):
        us = [link(d, t) for d in range(3)]
        a, b = plane(us[0], us[1], on_mat(us[0], lambda v: shift_y(v, m, True)), on_mat(us[1], lambda v: shift_x(v, m, True)))
        accumulate(c_ref, 1, t, a)
        accumulate(c_ref, 0, t, b, -1)
        accumulate(r_ref, 0, t, [shift_y(v, m, False) for v in a])
        accumulate(r_ref, 1, t, [shift_x(v, m, False) for v in b], -1)
        for mu, shift in ((0, shift_x), (1, shift_y)):
            up = mat(lambda p, i, j: jnp.where(m["z"] == 3, above_ref[mu, p, i, j, at(t), :], next_z(us[mu][i][j][p])))
            a, b = plane(us[mu], us[2], up, on_mat(us[2], lambda v: shift(v, m, True)))
            accumulate(c_ref, 2, t, a)
            accumulate(c_ref, mu, t, b, -1)
            accumulate(r_ref, mu, t, [down_z(v, m) for v in a])
            accumulate(r_ref, 2, t, [shift(v, m, False) for v in b], -1)
        return carry

    lax.fori_loop(0, 4, body, 0)
    uz_low = unpack_rows(high_ref, 2)
    for mu, shift in ((0, shift_x), (1, packed_shift_y)):
        a = corner_loop(unpack_rows(high_ref, mu), uz_low, packed(rows, mu, FIRST), on_mat(uz_low, lambda v: shift(v, m, True)), True)
        for k in range(8):
            expand(x_ref, 16 + mu * 8 + k, a[k], 0)
    for k in range(8):
        expand(x_ref, k, -ab_ref[8 + k], 3)
        expand(x_ref, 8 + k, jnp.where(line >= 2, pltpu.roll(ab_ref[k], 2, 0), 0.0), 3)


def expand(x_ref, n, tile, offset):
    x_ref[n] = jnp.zeros((32, 128), F32)
    x_ref[n, pl.ds(offset, 8, stride=4), :] = tile


def at(t):
    return pl.ds(t * 8 if isinstance(t, int) else pl.multiple_of(t * 8, 8), 8)


def packed_shift_y(v, m, up):
    r = pltpu.roll(v, 112 if up else 16, 1)
    other = jnp.where(m["odd"], pltpu.roll(r, 1, 0), pltpu.roll(r, 7, 0))
    return jnp.where(m["y"] == (7 if up else 0), other, r)


def packed(rows, d, part):
    return mat(lambda p, i, j: rows[d, p, i, j, part, :])


def finish(f, u, z_out, new_out):
    z = [-0.5 * v for v in f]
    zero = jnp.zeros_like(z[0])
    for n, (i, j) in enumerate(PAIRS):
        z_out(0, i, j, z[2 * n])
        z_out(1, i, j, z[2 * n + 1])
        z_out(0, j, i, -z[2 * n])
        z_out(1, j, i, z[2 * n + 1])
    for k, d in enumerate((z[6], z[7], -(z[6] + z[7]))):
        z_out(0, k, k, zero)
        z_out(1, k, k, d)
    new = product(taylor([0.125 * v for v in z]), u)
    for i in range(3):
        for j in range(3):
            for p in range(2):
                new_out(p, i, j, new[i][j][p])
    return new


def writer(ref, *head, t):
    def put(p, i, j, v):
        ref[(*head, p, i, j, t)] = v

    return put


def both_loops(d, g):
    return twice_ta(g, d), twice_ta(d, g)


def top_kernel(u_ref, ht_ref, d_ref, up_ref, c_in, r_in, f_in, c_ref, r_ref, f_ref, uz4_ref):
    ut = links(tiles(u_ref, (4, 2, 3, 3, 4)))(3, 3)
    above = [unpack_rows(ht_ref, mu) for mu in range(3)]
    put18(uz4_ref, above[2])
    loops = (both_loops(get18(d_ref.at[mu]), special(above[mu], get18(up_ref.at[mu]), hb=True)) for mu in range(3))
    f = time_loops(ut, loops, c_ref, r_ref, masks(), 3)
    for k in range(8):
        f_ref[k, 3] = f[k]


def time_kernel(u_ref, uz4_ref, lowt_ref, high_ref, corner_ref, d_ref, f_ref, r_ref, ft_ref, ab_ref, zt_ref, nt_ref, s_ref, x_ref, pk_ref, end_ref):
    link = links(tiles(u_ref, (4, 2, 3, 3, 4)))
    rows = u_ref.reshape(4, 2, 3, 3, 32, 128)
    zt, nt = tiles(zt_ref, (2, 3, 3, 4)), tiles(nt_ref, (2, 3, 3, 4))
    for p in range(2):
        for i in range(3):
            for j in range(3):
                pk_ref[p, i, j, pl.ds(0, 6), :] = rows[2, p, i, j, pl.ds(11, 6, stride=4), :]
                pk_ref[p, i, j, pl.ds(6, 2), :] = uz4_ref[p, i, j, pl.ds(3, 2, stride=4), :]
    a, b = both_loops(get18(d_ref.at[3]), special(get18(pk_ref), unpack_rows(lowt_ref, 0), hb=True))
    w = transport(packed(rows, 3, LAST), a)
    for k in range(8):
        ab_ref[k] = a[k]
        ab_ref[8 + k] = b[k]
        expand(x_ref, k, w[k], 3)
        end_ref[k] = jnp.zeros((8, 128), F32)
        end_ref[k, pl.ds(3, 2, stride=4), :] = ab_ref[k, pl.ds(6, 2), :]
    for k in range(12):
        pk_ref[k // 6, k // 3 % 2, k % 3, pl.ds(0, 6), :] = high_ref[24 + k, pl.ds(2, 6), :]
        pk_ref[k // 6, k // 3 % 2, k % 3, pl.ds(6, 2), :] = corner_ref[pl.ds(2 * k, 2), :]
    up = [[(pk_ref[0, i, j], pk_ref[1, i, j]) for j in range(3)] for i in range(2)]
    b = corner_loop(unpack_rows(high_ref, 2), unpack_rows(high_ref, 3), up + [third_row(up)], packed(rows, 3, FIRST), False)
    for k in range(8):
        x_ref[k, FIRST, :] = -b[k]
    for mu in range(3):
        for k in range(8):
            v = r_ref[mu, k, 4]
            ft_ref[mu * 8 + k] = v + end_ref[k] if mu == 2 else v

    def body(t, carry):
        u = link(3, t)
        finish([f_ref[k, t] + x_ref[k, at(t), :] for k in range(8)], u, writer(zt, t=t), writer(nt, t=t))
        return carry

    lax.fori_loop(0, 4, body, 0)
    slab = mat(lambda p, i, j: nt[p, i, j, 0])
    for t in range(1, 4):
        slab = product(slab, mat(lambda p, i, j: nt[p, i, j, t]))
    put18(s_ref, slab)


def out_copies(src, dst, sem, d, first, count):
    return [pltpu.make_async_copy(src.at[p], dst.at[d, p, :, :, pl.ds(first, count)], sem.at[p]) for p in range(2)]


def finish_space(first, count, u_ref, x_ref, c_ref, r_ref, extra, new_hbm, z_hbm, zs_ref, ns_ref, sem):
    link = links(tiles(u_ref, (4, 2, 3, 3, 4)))
    copies = []
    for mu, part in ((0, 16), (1, 24), (2, 8)):
        zs, ns = tiles(zs_ref.at[mu], (2, 3, 3, count)), tiles(ns_ref.at[mu], (2, 3, 3, count))

        def body(n, carry):
            t = first + n
            u = link(mu, t)
            c = [c_ref[mu, k, t] for k in range(8)]
            if mu == 2:
                c = [v + x_ref[k, at(t), :] for k, v in enumerate(c)]
            w = transport(u, c)
            f = [w[k] + (r_ref[mu, k, t] + x_ref[part + k, at(t), :]) for k in range(8)]
            if extra is not None:
                f = [v + extra[mu * 8 + k] for k, v in enumerate(f)]
            finish(f, u, writer(zs, t=n), writer(ns, t=n))
            return carry

        if count > 1:
            lax.fori_loop(0, count, body, 0)
        else:
            body(0, 0)
        more = out_copies(zs_ref.at[mu], z_hbm, sem.at[2 * mu], mu, first, count)
        more += out_copies(ns_ref.at[mu], new_hbm, sem.at[2 * mu + 1], mu, first, count)
        for c in more:
            c.start()
        copies += more
    return copies


def space_kernel(u_ref, x_ref, c_ref, r_ref, zt_ref, nt_ref, new_hbm, z_hbm, zs_ref, ns_ref, sem):
    copies = out_copies(zt_ref, z_hbm, sem.at[6], 3, 0, 4) + out_copies(nt_ref, new_hbm, sem.at[7], 3, 0, 4)
    for c in copies:
        c.start()
    copies += finish_space(1, 3, u_ref, x_ref, c_ref, r_ref, None, new_hbm, z_hbm, zs_ref, ns_ref, sem)
    for c in copies:
        c.wait()


def first_kernel(u_ref, x_ref, c_ref, r_ref, ft_ref, new_in, z_in, new_hbm, z_hbm, zs_ref, ns_ref, sem):
    copies = finish_space(0, 1, u_ref, x_ref, c_ref, r_ref, ft_ref, new_hbm, z_hbm, zs_ref, ns_ref, sem)
    for c in copies:
        c.wait()


def get18(ref):
    return mat(lambda p, i, j: ref[p, i, j])


def put18(ref, m):
    for i in range(3):
        for j in range(3):
            for p in range(2):
                ref[p, i, j] = m[i][j][p]


def chain(mats):
    out = mats[0]
    for x in mats[1:]:
        out = product(out, x)
    return out


def join_kernel(s0_ref, s1_ref, s2_ref, s3_ref, head_ref, tail_ref, row_ref):
    x = lax.rem(lax.axis_index("tm"), ROW)
    cyc = [s0_ref, s1_ref, s2_ref, s3_ref]
    for n in range(ROW):

        @pl.when(x == n)
        def _():
            head = chain([get18(r) for r in cyc[: ROW - n]])
            put18(head_ref, head)
            if n == 0:
                put18(row_ref, head)
                one, zero = jnp.ones((8, 128), F32), jnp.zeros((8, 128), F32)
                put18(tail_ref, [[(one if i == j else zero, zero) for j in range(3)] for i in range(3)])
            else:
                tail = chain([get18(r) for r in cyc[ROW - n :]])
                put18(tail_ref, tail)
                put18(row_ref, product(tail, head))


def holonomy_kernel(head_ref, row_ref, tail_ref, out_hbm, o_ref, sem):
    loop = product(product(get18(head_ref), get18(row_ref)), get18(tail_ref))
    put18(tiles(o_ref, (2, 3, 3)), loop)
    copies = []
    for h in range(2):
        copies.append(pltpu.make_async_copy(o_ref.at[h], out_hbm.at[h], sem.at[h]))
    for c in copies:
        c.start()
    for c in copies:
        c.wait()


def call(kernel, outs, args, scratch=(), aliases=None, us=1.0):
    def spec(kind):
        return pl.BlockSpec(memory_space=VMEM if kind == "v" else pltpu.HBM)

    shapes = [VMEM(s, F32) if kind == "v" else jax.ShapeDtypeStruct(s, F32) for kind, s in outs]
    values = [pltpu.with_memory_space_constraint(x, VMEM if kind == "v" else pltpu.HBM) for kind, x in args]
    return pl.pallas_call(
        kernel,
        out_shape=shapes,
        in_specs=[spec(k) for k, _ in args],
        out_specs=[spec(k) for k, _ in outs],
        scratch_shapes=list(scratch),
        input_output_aliases=aliases or {},
        compiler_params=pltpu.CompilerParams(vmem_limit_bytes=24 << 20),
        cost_estimate=pl.CostEstimate(flops=int(us * 1e6), bytes_accessed=int(us * 3e6), transcendentals=0),
    )(*values)


def from_ahead(x, axis, k):
    n = lax.axis_size(axis)
    return lax.ppermute(x, axis, [(i, (i - k) % n) for i in range(n)])


def diagonal(x):
    n, k = lax.axis_size("space"), lax.axis_size("tm")
    pairs = [(i * k + j, (i + 1) % n * k + (j - 1) % k) for i in range(n) for j in range(k)]
    return lax.ppermute(x, ("space", "tm"), pairs)


def in_row(x, k):
    n = lax.axis_size("tm")
    return lax.ppermute(x, "tm", [(i, i // ROW * ROW + (i - k) % ROW) for i in range(n)])


def plain(x, slices):
    return jnp.swapaxes(x, -3, -2).reshape(*x.shape[: -4 if slices > 1 else -3], slices, 4, 256)


def program(gauge_links):
    dma = pltpu.SemaphoreType.DMA
    whole = (4, 2, 3, 3, 4, 2, 4, 128)
    mat18 = ("v", (2, 3, 3, 8, 128))
    full = ("h", whole)
    gauge_links = jnp.swapaxes(gauge_links.reshape(4, 2, 3, 3, 4, 4, 2, 128), 5, 6)

    def pack(n):
        return ("v", (n, 8, 128))

    u, st, lowt, low, high, corner = call(
        load_kernel,
        [("v", whole), pack(36), pack(12), pack(24), pack(48), ("v", (24, 128))],
        [("h", gauge_links)],
        [dma(())],
    )
    high = ("v", from_ahead(high, "space", -1))
    corner = ("v", diagonal(corner))
    ht = ("v", from_ahead(st, "tm", 1))
    lowt = ("v", from_ahead(lowt, "space", 1))
    low = ("v", from_ahead(low, "space", 1))
    acc = [("v", (4, 8, 4, 8, 128)), ("v", (4, 8, 5, 8, 128))]
    slices = ("v", (2, 3, 3, 4, 2, 4, 128))
    sums = ("v", (8, 4, 8, 128))
    u, c, r, f, d, up = call(
        steep_kernel,
        [("v", whole), *acc, sums, ("v", (4, 2, 3, 3, 8, 128)), ("v", (3, 2, 3, 3, 8, 128))],
        [("v", u)],
        (),
        {0: 0},
        us=1.5,
    )
    u = ("v", u)
    c, r, f, uz4 = call(
        top_kernel, [*acc, sums, mat18], [u, ht, ("v", d), ("v", up), ("v", c), ("v", r), ("v", f)], (), {4: 0, 5: 1, 6: 2}, us=0.4
    )
    ft, ab, zt, nt, s = call(
        time_kernel,
        [pack(24), pack(16), slices, slices, mat18],
        [u, ("v", uz4), lowt, high, corner, ("v", d), ("v", f), ("v", r)],
        [VMEM((8, 32, 128), F32), VMEM((2, 3, 3, 8, 128), F32), VMEM((8, 8, 128), F32)],
        us=0.6,
    )
    s1, s3, s2 = in_row(s, 1), in_row(s, 3), in_row(s, 2)
    ft = ("v", from_ahead(ft, "tm", -1))
    edges = ("v", (32, 32, 128))
    c, r, x = call(
        flat_kernel,
        [*acc, edges],
        [u, low, high, ("v", ab), ("v", c), ("v", r), ("v", s)],
        [VMEM((2, 2, 3, 3, 32, 128), F32)],
        {4: 0, 5: 1},
        us=2.2,
    )
    head, tail, row = call(join_kernel, [mat18] * 3, [("v", s), ("v", s1), ("v", s2), ("v", s3)], us=0.1)
    row = from_ahead(row, "tm", ROW)

    def stage(count):
        return [VMEM((3, 2, 3, 3, count, 2, 4, 128), F32)] * 2 + [dma((8, 2))]

    shared = [u, ("v", x), ("v", c), ("v", r)]
    new, force = call(space_kernel, [full, full], [*shared, ("v", zt), ("v", nt)], stage(3), us=1.6)
    new, force = call(first_kernel, [full, full], [*shared, ft, ("h", new), ("h", force)], stage(1), {5: 0, 6: 1}, us=1.0)
    (hol,) = call(
        holonomy_kernel,
        [("h", (2, 3, 3, 2, 4, 128))],
        [("v", head), ("v", row), ("v", tail)],
        [VMEM((2, 3, 3, 2, 4, 128), F32), dma((2,))],
    )
    return plain(new, 4), plain(force, 4), plain(hol, 1)


def solution(mesh):
    in_specs = (P(None, None, None, None, "tm", "space", None),)
    out_specs = (
        P(None, None, None, None, "tm", "space", None),
        P(None, None, None, None, "tm", "space", None),
        P(None, None, None, "tm", "space", None),
    )
    return jax.shard_map(program, mesh=mesh, in_specs=in_specs, out_specs=out_specs, check_vma=False)
```

```python
import jax
import jax.numpy as jnp
from jax import lax
from jax.experimental import pallas as pl
from jax.experimental.pallas import tpu as pltpu
from jax.sharding import PartitionSpec as P


F32 = jnp.float32
VMEM = pltpu.VMEM
PAIRS = ((0, 1), (0, 2), (1, 2))
ROW = 4


def entry(terms):
    re = im = None
    for (ar, ai), ca, (br, bi), cb in terms:
        p = ar * br
        q = ai * bi
        re = p if re is None else re + p
        re = re + q if ca != cb else re - q
        u = ar * bi
        v = ai * br
        if im is None:
            im = (v - u) if cb and not ca else (u - v) if ca and not cb else (u + v)
        else:
            im = im - u if cb else im + u
            im = im - v if ca else im + v
    return re, im


def entry_im(terms):
    im = None
    for (ar, ai), ca, (br, bi), cb in terms:
        u = ar * bi
        v = ai * br
        if im is None:
            im = (v - u) if cb and not ca else (u - v) if ca and not cb else (u + v)
        else:
            im = im - u if cb else im + u
            im = im - v if ca else im + v
    return im


def terms(a, ha, b, hb, i, j):
    out = []
    for k in range(3):
        x = a[k][i] if ha else a[i][k]
        y = b[j][k] if hb else b[k][j]
        out.append((x, ha, y, hb))
    return out


def product(a, b, ha=False, hb=False):
    return [[entry(terms(a, ha, b, hb, i, j)) for j in range(3)] for i in range(3)]


def twice_ta(a, b):
    out = []
    for i, j in PAIRS:
        r1, i1 = entry(terms(a, False, b, False, i, j))
        r2, i2 = entry(terms(a, False, b, False, j, i))
        out += [r1 - r2, i1 + i2]
    d = [entry_im(terms(a, False, b, False, k, k)) for k in range(3)]
    tr = (d[0] + d[1] + d[2]) * (2.0 / 3.0)
    return out + [d[0] + d[0] - tr, d[1] + d[1] - tr]


def transport(u, c):
    r01, i01, r02, i02, r12, i12, d0, d1 = c
    d2 = -(d0 + d1)
    off = {(0, 1): (r01, i01), (0, 2): (r02, i02), (1, 2): (r12, i12)}
    diag = (d0, d1, d2)
    t = []
    for i in range(3):
        row = []
        for j in range(3):
            ur, ui = u[i][j]
            re = -(ui * diag[j])
            im = ur * diag[j]
            for k in range(3):
                if k == j:
                    continue
                ar, ai = u[i][k]
                if k < j:
                    cr, ci = off[k, j]
                    re = re + ar * cr - ai * ci
                    im = im + ar * ci + ai * cr
                else:
                    cr, ci = off[j, k]
                    re = re - ar * cr - ai * ci
                    im = im + ar * ci - ai * cr
            row.append((re, im))
        t.append(row)
    out = []
    for i, j in PAIRS:
        out += list(entry(terms(t, False, u, True, i, j)))
    for k in range(2):
        out.append(entry_im(terms(t, False, u, True, k, k)))
    return out


def taylor(f):
    r01, i01, r02, i02, r12, i12, h0, h1 = f
    h2 = -(h0 + h1)
    n01 = r01 * r01 + i01 * i01
    n02 = r02 * r02 + i02 * i02
    n12 = r12 * r12 + i12 * i12
    y0 = -(h0 * h0 + n01 + n02)
    y1 = -(h1 * h1 + n01 + n12)
    y2 = -(h2 * h2 + n02 + n12)
    s = 0.5 * (y0 + y1 + y2)
    y01 = (h2 * i01 - (r02 * r12 + i02 * i12), -(h2 * r01) - (i02 * r12 - r02 * i12))
    y02 = (h1 * i02 + (r01 * r12 - i01 * i12), -(h1 * r02) + (r01 * i12 + i01 * r12))
    y12 = (h0 * i12 - (r01 * r02 + i01 * i02), -(h0 * r12) - (r01 * i02 - i01 * r02))
    zr = r01 * r12 - i01 * i12
    zi = r01 * i12 + i01 * r12
    trip = zi * r02 - zr * i02
    e = -(h0 * h1 * h2 + (trip + trip) - h0 * n12 - h1 * n02 - h2 * n01)
    q0r = 1.0 - e * e * (1.0 / 720.0)
    q0i = e * (1.0 / 6.0 + s * (1.0 / 120.0))
    q1r = 1.0 + s * (1.0 / 6.0 + s * (1.0 / 120.0))
    q1i = e * (1.0 / 24.0 + s * (1.0 / 360.0))
    q2r = 0.5 + s * (1.0 / 24.0 + s * (1.0 / 720.0))
    q2i = e * (1.0 / 120.0)
    out = [[None] * 3 for _ in range(3)]
    offs = (((r01, i01), y01), ((r02, i02), y02), ((r12, i12), y12))
    for (i, j), ((xr, xi), (yr, yi)) in zip(PAIRS, offs):
        p1, p2, p3, p4 = q1r * xr, q1i * xi, q1r * xi, q1i * xr
        s1, s2, s3, s4 = q2r * yr, q2i * yi, q2r * yi, q2i * yr
        out[i][j] = ((p1 - p2) + (s1 - s2), (p3 + p4) + (s3 + s4))
        out[j][i] = ((s1 + s2) - (p1 + p2), (p3 - p4) + (s4 - s3))
    for k, (h, y) in enumerate(((h0, y0), (h1, y1), (h2, y2))):
        out[k][k] = (q0r - q1i * h + q2r * y, q0i + q1r * h + q2i * y)
    return out


def masks():
    lane = lax.broadcasted_iota(jnp.int32, (8, 128), 1)
    z = lax.broadcasted_iota(jnp.int32, (8, 128), 0) & 3
    return {"x": lane & 15, "y": lane >> 4, "z": z}


def shift_x(v, m, up):
    if up:
        return jnp.where(m["x"] == 15, pltpu.roll(v, 15, 1), pltpu.roll(v, 127, 1))
    return jnp.where(m["x"] == 0, pltpu.roll(v, 113, 1), pltpu.roll(v, 1, 1))


def shift_y(v, m, up):
    r = pltpu.roll(v, 112 if up else 16, 1)
    return jnp.where(m["y"] == (7 if up else 0), pltpu.roll(r, 4, 0), r)


def mat(fetch):
    return [[(fetch(0, i, j), fetch(1, i, j)) for j in range(3)] for i in range(3)]


def on_mat(m, f):
    return [[(f(a), f(b)) for a, b in row] for row in m]


def special(a, b, ha=False, hb=False):
    m = [[entry(terms(a, ha, b, hb, i, j)) for j in range(3)] for i in range(2)]
    return m + [third_row(m)]


def plane(u_mu, u_nu, mu_up, nu_up):
    d = special(u_mu, u_nu, ha=True)
    g = special(mu_up, nu_up, hb=True)
    return twice_ta(g, d), twice_ta(d, g)


def corner_loop(u_mu, u_nu, mu_up, nu_up, at_nu):
    d = special(u_mu, u_nu, ha=True)
    g = special(mu_up, nu_up, hb=True)
    return twice_ta(g, d) if at_nu else twice_ta(d, g)


def unpack_rows(ref, base):
    m = [[(ref[base * 12 + i * 3 + j], ref[base * 12 + 6 + i * 3 + j]) for j in range(3)] for i in range(2)]
    return m + [third_row(m)]


def third_row(m):
    third = []
    for k in range(3):
        a, b = (k + 1) % 3, (k + 2) % 3
        r1, i1 = entry([(m[0][a], False, m[1][b], False)])
        r2, i2 = entry([(m[0][b], False, m[1][a], False)])
        third.append((r1 - r2, i2 - i1))
    return third


def tiles(ref, shape):
    return ref.reshape(*shape, 8, 128)


FIRST = pl.ds(0, 8, stride=4)
LAST = pl.ds(3, 8, stride=4)


def load_kernel(u_hbm, u_ref, st_ref, lowt_ref, low_ref, high_ref, corner_ref, sem):
    two = pl.ds(0, 2)
    copies = [pltpu.make_async_copy(u_hbm.at[d, :, two], u_ref.at[d, :, two], sem.at[d]) for d in range(4)]
    for copy in copies:
        copy.start()
    u = tiles(u_ref, (4, 2, 3, 3, 4))
    rows = u_ref.reshape(4, 2, 3, 3, 32, 128)
    for d in range(4):
        copies[d].wait()
        for p in range(2):
            for i in range(2):
                for j in range(3):
                    k = p * 6 + i * 3 + j
                    high_ref[d * 12 + k] = rows[d, p, i, j, LAST, :]
                    if d < 3:
                        st_ref[d * 12 + k] = u[d, p, i, j, 0]
                    if d < 2:
                        low_ref[d * 12 + k] = rows[d, p, i, j, FIRST, :]
                    if d == 3:
                        lowt_ref[k] = rows[d, p, i, j, FIRST, :]
                    if d == 2:
                        corner_ref[pl.ds(2 * k, 2), :] = rows[d, p, i, j, pl.ds(3, 2, stride=4), :]


def accumulate(ref, mu, t, vals, sign=1):
    for k in range(8):
        if sign > 0:
            ref[mu, k, t] += vals[k]
        else:
            ref[mu, k, t] -= vals[k]


def inside(vals, m):
    return [jnp.where(m["z"] == 3, 0.0, v) for v in vals]


def next_z(v):
    return pltpu.roll(v, 7, 0)


def down_z(v, m):
    return jnp.where(m["z"] == 0, 0.0, pltpu.roll(v, 1, 0))


def links(u):
    return lambda d, t: mat(lambda p, i, j: u[d, p, i, j, t])


TURNS = (shift_x, shift_y, None)


def upward(mu, v, m):
    return TURNS[mu](v, m, True) if mu < 2 else next_z(v)


def time_loops(u_t, loops, c_ref, r_ref, m, t):
    own = back = None
    for mu, (a, b) in enumerate(loops):
        down = [TURNS[mu](v, m, False) for v in b] if mu < 2 else [down_z(v, m) for v in b]
        if mu == 2:
            a, b = inside(a, m), inside(b, m)
        accumulate(c_ref, mu, t, b, -1)
        accumulate(r_ref, mu, t + 1, a)
        own = a if own is None else [v + w for v, w in zip(own, a)]
        back = down if back is None else [v + w for v, w in zip(back, down)]
    return [v - w for v, w in zip(transport(u_t, own), back)]


def steep_kernel(u_in, u_ref, c_ref, r_ref, f_ref, d_ref, up_ref):
    u = tiles(u_ref, (4, 2, 3, 3, 4))
    rows = u_ref.reshape(4, 2, 3, 3, 32, 128)

    def complete(t, carry):
        for d in range(4):
            row = third_row([[(u[d, 0, i, j, t], u[d, 1, i, j, t]) for j in range(3)] for i in range(2)])
            for j in range(3):
                for p in range(2):
                    u[d, p, 2, j, t] = row[j][p]
        return carry

    lax.fori_loop(0, 4, complete, 0)
    link = links(u)
    m = masks()
    c_ref[...] = jnp.zeros_like(c_ref)
    r_ref[...] = jnp.zeros_like(r_ref)

    def body(t, carry):
        ut = link(3, t)
        loops = (plane(link(mu, t), ut, link(mu, t + 1), on_mat(ut, lambda v: upward(mu, v, m))) for mu in range(3))
        f = time_loops(ut, loops, c_ref, r_ref, m, t)
        for k in range(8):
            f_ref[k, t] = f[k]
        return carry

    lax.fori_loop(0, 3, body, 0)
    ut = link(3, 3)
    for mu in range(3):
        put18(d_ref.at[mu], special(link(mu, 3), ut, ha=True))
        put18(up_ref.at[mu], on_mat(ut, lambda v: upward(mu, v, m)))
    put18(d_ref.at[3], special(packed(rows, 2, LAST), packed(rows, 3, LAST), ha=True))


def flat_kernel(u_ref, low_ref, high_ref, ab_ref, c_in, r_in, after_ref, c_ref, r_ref, x_ref, above_ref):
    link = links(tiles(u_ref, (4, 2, 3, 3, 4)))
    rows = u_ref.reshape(4, 2, 3, 3, 32, 128)
    m = masks()
    line = lax.broadcasted_iota(jnp.int32, (8, 128), 0)
    m["odd"] = (line & 1) == 1
    for mu in range(2):
        halo = unpack_rows(low_ref, mu)
        for i in range(3):
            for j in range(3):
                for p in range(2):
                    above_ref[mu, p, i, j, LAST, :] = halo[i][j][p]

    def body(t, carry):
        us = [link(d, t) for d in range(3)]
        a, b = plane(us[0], us[1], on_mat(us[0], lambda v: shift_y(v, m, True)), on_mat(us[1], lambda v: shift_x(v, m, True)))
        accumulate(c_ref, 1, t, a)
        accumulate(c_ref, 0, t, b, -1)
        accumulate(r_ref, 0, t, [shift_y(v, m, False) for v in a])
        accumulate(r_ref, 1, t, [shift_x(v, m, False) for v in b], -1)
        for mu, shift in ((0, shift_x), (1, shift_y)):
            up = mat(lambda p, i, j: jnp.where(m["z"] == 3, above_ref[mu, p, i, j, at(t), :], next_z(us[mu][i][j][p])))
            a, b = plane(us[mu], us[2], up, on_mat(us[2], lambda v: shift(v, m, True)))
            accumulate(c_ref, 2, t, a)
            accumulate(c_ref, mu, t, b, -1)
            accumulate(r_ref, mu, t, [down_z(v, m) for v in a])
            accumulate(r_ref, 2, t, [shift(v, m, False) for v in b], -1)
        return carry

    lax.fori_loop(0, 4, body, 0)
    uz_low = unpack_rows(high_ref, 2)
    for mu, shift in ((0, shift_x), (1, packed_shift_y)):
        a = corner_loop(unpack_rows(high_ref, mu), uz_low, packed(rows, mu, FIRST), on_mat(uz_low, lambda v: shift(v, m, True)), True)
        for k in range(8):
            expand(x_ref, 16 + mu * 8 + k, a[k], 0)
    for k in range(8):
        expand(x_ref, k, -ab_ref[8 + k], 3)
        expand(x_ref, 8 + k, jnp.where(line >= 2, pltpu.roll(ab_ref[k], 2, 0), 0.0), 3)


def expand(x_ref, n, tile, offset):
    x_ref[n] = jnp.zeros((32, 128), F32)
    x_ref[n, pl.ds(offset, 8, stride=4), :] = tile


def at(t):
    return pl.ds(t * 8 if isinstance(t, int) else pl.multiple_of(t * 8, 8), 8)


def packed_shift_y(v, m, up):
    r = pltpu.roll(v, 112 if up else 16, 1)
    other = jnp.where(m["odd"], pltpu.roll(r, 1, 0), pltpu.roll(r, 7, 0))
    return jnp.where(m["y"] == (7 if up else 0), other, r)


def packed(rows, d, part):
    return mat(lambda p, i, j: rows[d, p, i, j, part, :])


def finish(f, u, z_out, new_out):
    z = [-0.5 * v for v in f]
    zero = jnp.zeros_like(z[0])
    for n, (i, j) in enumerate(PAIRS):
        z_out(0, i, j, z[2 * n])
        z_out(1, i, j, z[2 * n + 1])
        z_out(0, j, i, -z[2 * n])
        z_out(1, j, i, z[2 * n + 1])
    for k, d in enumerate((z[6], z[7], -(z[6] + z[7]))):
        z_out(0, k, k, zero)
        z_out(1, k, k, d)
    new = product(taylor([0.125 * v for v in z]), u)
    for i in range(3):
        for j in range(3):
            for p in range(2):
                new_out(p, i, j, new[i][j][p])
    return new


def writer(ref, *head, t):
    def put(p, i, j, v):
        ref[(*head, p, i, j, t)] = v

    return put


def both_loops(d, g):
    return twice_ta(g, d), twice_ta(d, g)


def top_kernel(u_ref, ht_ref, d_ref, up_ref, c_in, r_in, f_in, c_ref, r_ref, f_ref, uz4_ref):
    ut = links(tiles(u_ref, (4, 2, 3, 3, 4)))(3, 3)
    above = [unpack_rows(ht_ref, mu) for mu in range(3)]
    put18(uz4_ref, above[2])
    loops = (both_loops(get18(d_ref.at[mu]), special(above[mu], get18(up_ref.at[mu]), hb=True)) for mu in range(3))
    f = time_loops(ut, loops, c_ref, r_ref, masks(), 3)
    for k in range(8):
        f_ref[k, 3] = f[k]


def time_kernel(u_ref, uz4_ref, lowt_ref, high_ref, corner_ref, d_ref, f_ref, r_ref, ft_ref, ab_ref, zt_ref, nt_ref, s_ref, x_ref, pk_ref, end_ref):
    link = links(tiles(u_ref, (4, 2, 3, 3, 4)))
    rows = u_ref.reshape(4, 2, 3, 3, 32, 128)
    zt, nt = tiles(zt_ref, (2, 3, 3, 4)), tiles(nt_ref, (2, 3, 3, 4))
    for p in range(2):
        for i in range(3):
            for j in range(3):
                pk_ref[p, i, j, pl.ds(0, 6), :] = rows[2, p, i, j, pl.ds(11, 6, stride=4), :]
                pk_ref[p, i, j, pl.ds(6, 2), :] = uz4_ref[p, i, j, pl.ds(3, 2, stride=4), :]
    a, b = both_loops(get18(d_ref.at[3]), special(get18(pk_ref), unpack_rows(lowt_ref, 0), hb=True))
    w = transport(packed(rows, 3, LAST), a)
    for k in range(8):
        ab_ref[k] = a[k]
        ab_ref[8 + k] = b[k]
        expand(x_ref, k, w[k], 3)
        end_ref[k] = jnp.zeros((8, 128), F32)
        end_ref[k, pl.ds(3, 2, stride=4), :] = ab_ref[k, pl.ds(6, 2), :]
    for k in range(12):
        pk_ref[k // 6, k // 3 % 2, k % 3, pl.ds(0, 6), :] = high_ref[24 + k, pl.ds(2, 6), :]
        pk_ref[k // 6, k // 3 % 2, k % 3, pl.ds(6, 2), :] = corner_ref[pl.ds(2 * k, 2), :]
    up = [[(pk_ref[0, i, j], pk_ref[1, i, j]) for j in range(3)] for i in range(2)]
    b = corner_loop(unpack_rows(high_ref, 2), unpack_rows(high_ref, 3), up + [third_row(up)], packed(rows, 3, FIRST), False)
    for k in range(8):
        x_ref[k, FIRST, :] = -b[k]
    for mu in range(3):
        for k in range(8):
            v = r_ref[mu, k, 4]
            ft_ref[mu * 8 + k] = v + end_ref[k] if mu == 2 else v

    def body(t, carry):
        u = link(3, t)
        finish([f_ref[k, t] + x_ref[k, at(t), :] for k in range(8)], u, writer(zt, t=t), writer(nt, t=t))
        return carry

    lax.fori_loop(0, 4, body, 0)
    slab = mat(lambda p, i, j: nt[p, i, j, 0])
    for t in range(1, 4):
        slab = product(slab, mat(lambda p, i, j: nt[p, i, j, t]))
    put18(s_ref, slab)


def out_copies(src, dst, sem, d, first, count):
    return [pltpu.make_async_copy(src.at[p], dst.at[d, p, :, :, pl.ds(first, count)], sem.at[p]) for p in range(2)]


def finish_space(first, count, u_ref, x_ref, c_ref, r_ref, extra, new_hbm, z_hbm, zs_ref, ns_ref, sem):
    link = links(tiles(u_ref, (4, 2, 3, 3, 4)))
    copies = []
    for mu, part in ((0, 16), (1, 24), (2, 8)):
        zs, ns = tiles(zs_ref.at[mu], (2, 3, 3, count)), tiles(ns_ref.at[mu], (2, 3, 3, count))

        def body(n, carry):
            t = first + n
            u = link(mu, t)
            c = [c_ref[mu, k, t] for k in range(8)]
            if mu == 2:
                c = [v + x_ref[k, at(t), :] for k, v in enumerate(c)]
            w = transport(u, c)
            f = [w[k] + (r_ref[mu, k, t] + x_ref[part + k, at(t), :]) for k in range(8)]
            if extra is not None:
                f = [v + extra[mu * 8 + k] for k, v in enumerate(f)]
            finish(f, u, writer(zs, t=n), writer(ns, t=n))
            return carry

        if count > 1:
            lax.fori_loop(0, count, body, 0)
        else:
            body(0, 0)
        more = out_copies(zs_ref.at[mu], z_hbm, sem.at[2 * mu], mu, first, count)
        more += out_copies(ns_ref.at[mu], new_hbm, sem.at[2 * mu + 1], mu, first, count)
        for c in more:
            c.start()
        copies += more
    return copies


def space_kernel(u_ref, x_ref, c_ref, r_ref, zt_ref, nt_ref, new_hbm, z_hbm, zs_ref, ns_ref, sem):
    copies = out_copies(zt_ref, z_hbm, sem.at[6], 3, 0, 4) + out_copies(nt_ref, new_hbm, sem.at[7], 3, 0, 4)
    for c in copies:
        c.start()
    copies += finish_space(1, 3, u_ref, x_ref, c_ref, r_ref, None, new_hbm, z_hbm, zs_ref, ns_ref, sem)
    for c in copies:
        c.wait()


def first_kernel(u_ref, x_ref, c_ref, r_ref, ft_ref, new_in, z_in, new_hbm, z_hbm, zs_ref, ns_ref, sem):
    copies = finish_space(0, 1, u_ref, x_ref, c_ref, r_ref, ft_ref, new_hbm, z_hbm, zs_ref, ns_ref, sem)
    for c in copies:
        c.wait()


def get18(ref):
    return mat(lambda p, i, j: ref[p, i, j])


def put18(ref, m):
    for i in range(3):
        for j in range(3):
            for p in range(2):
                ref[p, i, j] = m[i][j][p]


def chain(mats):
    out = mats[0]
    for x in mats[1:]:
        out = product(out, x)
    return out


def join_kernel(s0_ref, s1_ref, s2_ref, s3_ref, head_ref, tail_ref, row_ref):
    x = lax.rem(lax.axis_index("tm"), ROW)
    cyc = [s0_ref, s1_ref, s2_ref, s3_ref]
    for n in range(ROW):

        @pl.when(x == n)
        def _():
            head = chain([get18(r) for r in cyc[: ROW - n]])
            put18(head_ref, head)
            if n == 0:
                put18(row_ref, head)
                one, zero = jnp.ones((8, 128), F32), jnp.zeros((8, 128), F32)
                put18(tail_ref, [[(one if i == j else zero, zero) for j in range(3)] for i in range(3)])
            else:
                tail = chain([get18(r) for r in cyc[ROW - n :]])
                put18(tail_ref, tail)
                put18(row_ref, product(tail, head))


def holonomy_kernel(head_ref, row_ref, tail_ref, out_hbm, o_ref, sem):
    loop = product(product(get18(head_ref), get18(row_ref)), get18(tail_ref))
    put18(tiles(o_ref, (2, 3, 3)), loop)
    copies = []
    for h in range(2):
        copies.append(pltpu.make_async_copy(o_ref.at[h], out_hbm.at[h], sem.at[h]))
    for c in copies:
        c.start()
    for c in copies:
        c.wait()


def call(kernel, outs, args, scratch=(), aliases=None, us=1.0):
    def spec(kind):
        return pl.BlockSpec(memory_space=VMEM if kind == "v" else pltpu.HBM)

    shapes = [VMEM(s, F32) if kind == "v" else jax.ShapeDtypeStruct(s, F32) for kind, s in outs]
    values = [pltpu.with_memory_space_constraint(x, VMEM if kind == "v" else pltpu.HBM) for kind, x in args]
    return pl.pallas_call(
        kernel,
        out_shape=shapes,
        in_specs=[spec(k) for k, _ in args],
        out_specs=[spec(k) for k, _ in outs],
        scratch_shapes=list(scratch),
        input_output_aliases=aliases or {},
        compiler_params=pltpu.CompilerParams(vmem_limit_bytes=24 << 20),
        cost_estimate=pl.CostEstimate(flops=int(us * 1e6), bytes_accessed=int(us * 3e6), transcendentals=0),
    )(*values)


def from_ahead(x, axis, k):
    n = lax.axis_size(axis)
    return lax.ppermute(x, axis, [(i, (i - k) % n) for i in range(n)])


def diagonal(x):
    n, k = lax.axis_size("space"), lax.axis_size("tm")
    pairs = [(i * k + j, (i + 1) % n * k + (j - 1) % k) for i in range(n) for j in range(k)]
    return lax.ppermute(x, ("space", "tm"), pairs)


def in_row(x, k):
    n = lax.axis_size("tm")
    return lax.ppermute(x, "tm", [(i, i // ROW * ROW + (i - k) % ROW) for i in range(n)])


def plain(x, slices):
    return jnp.swapaxes(x, -3, -2).reshape(*x.shape[: -4 if slices > 1 else -3], slices, 4, 256)


def program(gauge_links):
    dma = pltpu.SemaphoreType.DMA
    whole = (4, 2, 3, 3, 4, 2, 4, 128)
    mat18 = ("v", (2, 3, 3, 8, 128))
    full = ("h", whole)
    gauge_links = jnp.swapaxes(gauge_links.reshape(4, 2, 3, 3, 4, 4, 2, 128), 5, 6)

    def pack(n):
        return ("v", (n, 8, 128))

    u, st, lowt, low, high, corner = call(
        load_kernel,
        [("v", whole), pack(36), pack(12), pack(24), pack(48), ("v", (24, 128))],
        [("h", gauge_links)],
        [dma((4,))],
    )
    high = ("v", from_ahead(high, "space", -1))
    corner = ("v", diagonal(corner))
    ht = ("v", from_ahead(st, "tm", 1))
    lowt = ("v", from_ahead(lowt, "space", 1))
    low = ("v", from_ahead(low, "space", 1))
    acc = [("v", (4, 8, 4, 8, 128)), ("v", (4, 8, 5, 8, 128))]
    slices = ("v", (2, 3, 3, 4, 2, 4, 128))
    sums = ("v", (8, 4, 8, 128))
    u, c, r, f, d, up = call(
        steep_kernel,
        [("v", whole), *acc, sums, ("v", (4, 2, 3, 3, 8, 128)), ("v", (3, 2, 3, 3, 8, 128))],
        [("v", u)],
        (),
        {0: 0},
        us=1.5,
    )
    u = ("v", u)
    c, r, f, uz4 = call(
        top_kernel, [*acc, sums, mat18], [u, ht, ("v", d), ("v", up), ("v", c), ("v", r), ("v", f)], (), {4: 0, 5: 1, 6: 2}, us=0.4
    )
    ft, ab, zt, nt, s = call(
        time_kernel,
        [pack(24), pack(16), slices, slices, mat18],
        [u, ("v", uz4), lowt, high, corner, ("v", d), ("v", f), ("v", r)],
        [VMEM((8, 32, 128), F32), VMEM((2, 3, 3, 8, 128), F32), VMEM((8, 8, 128), F32)],
        us=0.6,
    )
    s1, s3, s2 = in_row(s, 1), in_row(s, 3), in_row(s, 2)
    ft = ("v", from_ahead(ft, "tm", -1))
    edges = ("v", (32, 32, 128))
    c, r, x = call(
        flat_kernel,
        [*acc, edges],
        [u, low, high, ("v", ab), ("v", c), ("v", r), ("v", s)],
        [VMEM((2, 2, 3, 3, 32, 128), F32)],
        {4: 0, 5: 1},
        us=2.2,
    )
    head, tail, row = call(join_kernel, [mat18] * 3, [("v", s), ("v", s1), ("v", s2), ("v", s3)], us=0.1)
    row = from_ahead(row, "tm", ROW)

    def stage(count):
        return [VMEM((3, 2, 3, 3, count, 2, 4, 128), F32)] * 2 + [dma((8, 2))]

    shared = [u, ("v", x), ("v", c), ("v", r)]
    new, force = call(space_kernel, [full, full], [*shared, ("v", zt), ("v", nt)], stage(3), us=1.6)
    new, force = call(first_kernel, [full, full], [*shared, ft, ("h", new), ("h", force)], stage(1), {5: 0, 6: 1}, us=1.0)
    (hol,) = call(
        holonomy_kernel,
        [("h", (2, 3, 3, 2, 4, 128))],
        [("v", head), ("v", row), ("v", tail)],
        [VMEM((2, 3, 3, 2, 4, 128), F32), dma((2,))],
    )
    return plain(new, 4), plain(force, 4), plain(hol, 1)


def solution(mesh):
    in_specs = (P(None, None, None, None, "tm", "space", None),)
    out_specs = (
        P(None, None, None, None, "tm", "space", None),
        P(None, None, None, None, "tm", "space", None),
        P(None, None, None, "tm", "space", None),
    )
    return jax.shard_map(program, mesh=mesh, in_specs=in_specs, out_specs=out_specs, check_vma=False)
```
